32 devices in a mesh: shard: 4 (over x, core), context: 2 (over y), tensor: 4 (over z).
Axes of the slice: x: 2, y: 2, z: 4, core: 2. Of those that a mesh axis runs over, the one named last changes fastest.
Arguments:
- tokens: bfloat16 [8, 768, 960], P('shard', ('context', 'tensor')), may hold values from -6 to 6
- attn_gain: float32 [960], P('shard'), may hold values from 0.25 to 1.75
- w_query: bfloat16 [960, 960], P('shard'), may hold values from -0.1875 to 0.1875
- key_weight: bfloat16 [960, 320], P('shard'), may hold values from -0.1875 to 0.1875
- value_weight: bfloat16 [960, 320], P('shard'), may hold values from -0.1875 to 0.1875
- w_output: bfloat16 [960, 960], P(None, 'shard'), may hold values from -1 to 1
- mlp_gain: float32 [960], P('shard'), may hold values from 0.25 to 1.75
- w_gate: bfloat16 [960, 2560], P('shard', 'tensor'), may hold values from -0.1875 to 0.1875
- w_up: bfloat16 [960, 2560], P('shard', 'tensor'), may hold values from -0.1875 to 0.1875
- w_down: bfloat16 [2560, 960], P('tensor', 'shard'), may hold values from -0.25 to 0.25
- cotangent: bfloat16 [8, 768, 960], P('shard', ('context', 'tensor')), may hold values from -6 to 6
Outputs:
- block_out: bfloat16 [8, 768, 960], P('shard', ('context', 'tensor'))
- tokens_grad: bfloat16 [8, 768, 960], P('shard', ('context', 'tensor'))
- attn_gain_grad: float32 [960], P('shard')
- w_query_grad: float32 [960, 960], P('shard')
- w_key_grad: float32 [960, 320], P('shard')
- w_value_grad: float32 [960, 320], P('shard')
- w_output_grad: float32 [960, 960], P(None, 'shard')
- mlp_gain_grad: float32 [960], P('shard')
- w_gate_grad: float32 [960, 2560], P('shard', 'tensor')
- w_up_grad: float32 [960, 2560], P('shard', 'tensor')
- w_down_grad: float32 [2560, 960], P('tensor', 'shard')
The draws below stay inside these ranges and needn't reach their ends.
All inputs are finite; a program needn't handle non-finite values.
Results may differ from the reference program's by a relative error of at most 0.022.
Values may be sent and summed in bfloat16 or wider, within the bound.
No kernel may reach another device: no remote copies, remote signals or barrier semaphores. Data moves between devices by JAX's collectives and lax.ppermute only.
A program may use at most 128 MiB of HBM per device.

```python
import jax
import jax.numpy as jnp
from jax import lax

MODEL_WIDTH = 960
QUERY_HEADS = 15
KEY_VALUE_HEADS = 5
HEAD_SIZE = 64
FF = 2560
SEQUENCE_LENGTH = 768
SEQS = 8


def with_spikes(array, stream_key, source, target, parts, factor):
    def block_of(axis_at):
        return (jnp.arange(array.shape[axis_at]) // (array.shape[axis_at] // parts)).reshape((-1,) + (1,) * (array.ndim - 1 - axis_at))

    one_side = jax.random.permutation(stream_key, parts)[block_of(target)]
    second = (block_of(target) + parts // 2) % parts
    return jnp.where((block_of(source) == one_side) | (block_of(source) == second), factor * array, array)


def shard_levels(own_key, shape, split, low, top_value):
    level, own = 1.0, jax.random.fold_in(own_key, 6)
    for position, parts in split:
        draws = jnp.exp(jax.random.uniform(jax.random.fold_in(own, position), (parts,), jnp.float32, low / len(split), top_value / len(split)))
        level = level * jnp.repeat(draws, shape[position] // parts).reshape([-1 if axis == position else 1 for axis in range(len(shape))])
    return level


def scatter_about(stream_key, shape, deviation, most, shards=(), held_as=jnp.bfloat16):
    entries = jax.random.normal(stream_key, shape, jnp.float32) * deviation
    if len(shards) > 0:
        entries = shard_levels(stream_key, shape, shards, -0.22, 0.18) * entries
    return jnp.clip(entries, min=-most, max=most).astype(held_as)


def heavy_noise(own_key, shape, width, limit, cuts, heavy, kind=jnp.bfloat16):
    drawn = width * jax.random.normal(own_key, shape, jnp.float32)
    if cuts:
        drawn = drawn * shard_levels(own_key, shape, cuts, -0.22, 0.18)
    return jnp.clip(with_spikes(drawn, jax.random.fold_in(own_key, 3), *heavy), -limit, limit).astype(kind)


def setup_inputs(seed: int = 0) -> dict:
    splits = jax.random.split(jax.random.key(seed), 12)
    tokens = scatter_about(splits[0], (SEQS, SEQUENCE_LENGTH, MODEL_WIDTH), 1.0, 6.0, ((0, 4), (1, 8)))
    attn_gain = jnp.clip(1.0 + 0.15 * jax.random.normal(splits[1], (MODEL_WIDTH,), jnp.float32), 0.25, 1.75)
    w_query = scatter_about(splits[2], (MODEL_WIDTH, QUERY_HEADS * HEAD_SIZE), MODEL_WIDTH ** -0.5, 0.1875, ((0, 4),))
    key_weight = scatter_about(splits[3], (MODEL_WIDTH, KEY_VALUE_HEADS * HEAD_SIZE), MODEL_WIDTH ** -0.5, 0.1875, ((0, 4),))
    value_weight = scatter_about(splits[4], (MODEL_WIDTH, KEY_VALUE_HEADS * HEAD_SIZE), MODEL_WIDTH ** -0.5, 0.1875, ((0, 4),))
    w_output = scatter_about(splits[5], (QUERY_HEADS * HEAD_SIZE, MODEL_WIDTH), (max(QUERY_HEADS * HEAD_SIZE // 32, 1)) ** -0.5, 1.0, ((1, 4),))
    mlp_gain = jnp.clip(1.0 + 0.15 * jax.random.normal(splits[6], (MODEL_WIDTH,), jnp.float32), 0.25, 1.75)
    w_gate = scatter_about(splits[7], (MODEL_WIDTH, FF), MODEL_WIDTH ** -0.5, 0.1875, ((0, 4), (1, 4)))
    w_up = scatter_about(splits[8], (MODEL_WIDTH, FF), MODEL_WIDTH ** -0.5, 0.1875, ((0, 4), (1, 4)))
    w_down = scatter_about(splits[9], (FF, MODEL_WIDTH), (FF // 4) ** -0.5, 0.25, ((0, 4), (1, 4)))
    cotangent = heavy_noise(splits[10], (SEQS, SEQUENCE_LENGTH, MODEL_WIDTH), 1.0, 6.0, ((0, 4), (1, 8)), (0, 2, 4, 2.0))
    return {"tokens": tokens, "attn_gain": attn_gain, "w_query": w_query, "key_weight": key_weight, "value_weight": value_weight, "w_output": w_output, "mlp_gain": mlp_gain, "w_gate": w_gate, "w_up": w_up, "w_down": w_down, "cotangent": cotangent}


EPS = 1e-05

def rope_tables(positions, head_dim):
    half = head_dim // 2
    freq = 10000.0 ** (-jnp.arange(half).astype(jnp.float32) * 2.0 / head_dim)
    angle = positions.astype(jnp.float32)[:, None] * freq[None, :]
    return (jnp.cos(angle), jnp.sin(angle))

def apply_rotation(value_tensor, cosine_lookup, sine_lookup, sign):
    half = value_tensor.shape[-1] // 2
    leading = value_tensor[..., :half]
    trailing = value_tensor[..., half:]
    cos_col = cosine_lookup[:, None, :]
    sin_col = sine_lookup[:, None, :] * sign
    return jnp.concatenate([leading * cos_col - trailing * sin_col, trailing * cos_col + leading * sin_col], -1)

def rms_scale(value_tensor):
    return lax.rsqrt(lax.optimization_barrier(jnp.mean(value_tensor * value_tensor, axis=-1, keepdims=True)) + EPS)

def norm_back(grad_norm, value_tensor, scale_rows, gain):
    normed = value_tensor * scale_rows
    scaled = grad_norm * gain
    grad_in = scale_rows * (scaled - normed * lax.optimization_barrier(jnp.mean(scaled * normed, axis=-1, keepdims=True)))
    return (grad_in, lax.optimization_barrier(jnp.sum(grad_norm * normed, axis=0)))

def dot_single_float(left, right):
    return jnp.dot(left, right, preferred_element_type=jnp.float32)

def attend(query_rotated, key_rot, value_low, positions):
    query_length = query_rotated.shape[0]
    group_count = QUERY_HEADS // KEY_VALUE_HEADS
    grouped_heads = query_rotated.reshape(query_length, KEY_VALUE_HEADS, group_count, HEAD_SIZE).astype(jnp.float32)
    scores = jnp.einsum('qkgd,tkd->kgqt', grouped_heads, key_rot.astype(jnp.float32)) * HEAD_SIZE ** (-0.5)
    allowed = positions[None, :] <= positions[:, None]
    scores = jnp.where(allowed, scores, -1e+30)
    peak = lax.optimization_barrier(jnp.max(scores, axis=-1, keepdims=True))
    expd = jnp.exp(scores - peak)
    total = lax.optimization_barrier(jnp.sum(expd, axis=-1, keepdims=True))
    probs = (expd / total).astype(jnp.bfloat16)
    mixed = jnp.einsum('kgqt,tkd->qkgd', probs.astype(jnp.float32), value_low.astype(jnp.float32))
    return (mixed.reshape(query_length, QUERY_HEADS * HEAD_SIZE).astype(jnp.bfloat16), peak[..., 0] + jnp.log(total[..., 0]))

def attend_back(query_rotated, key_rot, value_low, mixture_reduced, mixture_gradient, log_total, positions):
    query_length = query_rotated.shape[0]
    group_count = QUERY_HEADS // KEY_VALUE_HEADS
    grouped_heads = query_rotated.reshape(query_length, KEY_VALUE_HEADS, group_count, HEAD_SIZE).astype(jnp.float32)
    scores = jnp.einsum('qkgd,tkd->kgqt', grouped_heads, key_rot.astype(jnp.float32)) * HEAD_SIZE ** (-0.5)
    allowed = positions[None, :] <= positions[:, None]
    scores = jnp.where(allowed, scores, -1e+30)
    probs = jnp.exp(scores - log_total[..., None])
    probs_low = probs.astype(jnp.bfloat16)
    gradient_grouped = mixture_gradient.reshape(query_length, KEY_VALUE_HEADS, group_count, HEAD_SIZE).astype(jnp.float32)
    mixture_grouped = mixture_reduced.reshape(query_length, KEY_VALUE_HEADS, group_count, HEAD_SIZE).astype(jnp.float32)
    grad_probs = jnp.einsum('qkgd,tkd->kgqt', gradient_grouped, value_low.astype(jnp.float32))
    delta = jnp.transpose(lax.optimization_barrier(jnp.sum(gradient_grouped * mixture_grouped, axis=-1)), (1, 2, 0))[..., None]
    grad_scores = (probs * (grad_probs - delta) * HEAD_SIZE ** (-0.5)).astype(jnp.bfloat16).astype(jnp.float32)
    grad_query = jnp.einsum('kgqt,tkd->qkgd', grad_scores, key_rot.astype(jnp.float32)).reshape(query_length, QUERY_HEADS, HEAD_SIZE)
    key_gradient = jnp.einsum('kgqt,qkgd->tkd', grad_scores, grouped_heads)
    value_gradient = jnp.einsum('kgqt,qkgd->tkd', probs_low.astype(jnp.float32), gradient_grouped)
    return (grad_query, key_gradient, value_gradient)

def reference(tokens, attn_gain, w_query, key_weight, value_weight, w_output, mlp_gain, w_gate, w_up, w_down, cotangent):
    positions = jnp.arange(SEQUENCE_LENGTH).astype(jnp.int32)
    cosine_lookup, sine_lookup = rope_tables(positions, HEAD_SIZE)

    def one_sequence(carry, item):
        seq_tokens, seq_cot = item
        tokens_f = seq_tokens.astype(jnp.float32)
        scale_a = rms_scale(tokens_f)
        attention_normed = (tokens_f * scale_a * attn_gain).astype(jnp.bfloat16)
        query = dot_single_float(attention_normed, w_query).reshape(SEQUENCE_LENGTH, QUERY_HEADS, HEAD_SIZE)
        key = dot_single_float(attention_normed, key_weight).reshape(SEQUENCE_LENGTH, KEY_VALUE_HEADS, HEAD_SIZE)
        value_rows = dot_single_float(attention_normed, value_weight).reshape(SEQUENCE_LENGTH, KEY_VALUE_HEADS, HEAD_SIZE)
        query_rotated = apply_rotation(query, cosine_lookup, sine_lookup, 1.0).astype(jnp.bfloat16)
        key_rot = apply_rotation(key, cosine_lookup, sine_lookup, 1.0).astype(jnp.bfloat16)
        value_low = value_rows.astype(jnp.bfloat16)
        mixture_reduced, log_total = attend(query_rotated, key_rot, value_low, positions)
        hidden = tokens_f + dot_single_float(mixture_reduced, w_output)
        scale_m = rms_scale(hidden)
        normed_m = (hidden * scale_m * mlp_gain).astype(jnp.bfloat16)
        gate = dot_single_float(normed_m, w_gate)
        up_vals = dot_single_float(normed_m, w_up)
        sigma = jax.nn.sigmoid(gate)
        act = (gate * sigma * up_vals).astype(jnp.bfloat16)
        out_low = (hidden + dot_single_float(act, w_down)).astype(jnp.bfloat16)
        cot_f = seq_cot.astype(jnp.float32)
        grad_act = dot_single_float(seq_cot, w_down.T)
        g_down = dot_single_float(act.T, seq_cot)
        grad_up = (grad_act * gate * sigma).astype(jnp.bfloat16)
        grad_gate = (grad_act * up_vals * sigma * (1.0 + gate * (1.0 - sigma))).astype(jnp.bfloat16)
        grad_nm = dot_single_float(grad_gate, w_gate.T) + dot_single_float(grad_up, w_up.T)
        g_gate = dot_single_float(normed_m.T, grad_gate)
        g_up = dot_single_float(normed_m.T, grad_up)
        grad_hn, g_mgain = norm_back(grad_nm, hidden, scale_m, mlp_gain)
        grad_hidden = cot_f + grad_hn
        grad_hidden_low = grad_hidden.astype(jnp.bfloat16)
        g_out = dot_single_float(mixture_reduced.T, grad_hidden_low)
        mixture_gradient = dot_single_float(grad_hidden_low, w_output.T).astype(jnp.bfloat16)
        grad_query, key_gradient, value_gradient = attend_back(query_rotated, key_rot, value_low, mixture_reduced, mixture_gradient, log_total, positions)
        grad_query = apply_rotation(grad_query, cosine_lookup, sine_lookup, -1.0).reshape(SEQUENCE_LENGTH, QUERY_HEADS * HEAD_SIZE).astype(jnp.bfloat16)
        key_gradient = apply_rotation(key_gradient, cosine_lookup, sine_lookup, -1.0).reshape(SEQUENCE_LENGTH, KEY_VALUE_HEADS * HEAD_SIZE).astype(jnp.bfloat16)
        value_gradient = value_gradient.reshape(SEQUENCE_LENGTH, KEY_VALUE_HEADS * HEAD_SIZE).astype(jnp.bfloat16)
        grad_na = dot_single_float(grad_query, w_query.T) + dot_single_float(key_gradient, key_weight.T) + dot_single_float(value_gradient, value_weight.T)
        g_query = dot_single_float(attention_normed.T, grad_query)
        g_key = dot_single_float(attention_normed.T, key_gradient)
        g_value = dot_single_float(attention_normed.T, value_gradient)
        grad_tn, g_again = norm_back(grad_na, tokens_f, scale_a, attn_gain)
        grad_tokens = (grad_hidden + grad_tn).astype(jnp.bfloat16)
        terms = (g_again, g_query, g_key, g_value, g_out, g_mgain, g_gate, g_up, g_down)
        new_carry = tuple((total + term for total, term in zip(carry, terms)))
        return (new_carry, (out_low, grad_tokens))
    shapes = (attn_gain, w_query, key_weight, value_weight, w_output, mlp_gain, w_gate, w_up, w_down)
    init = tuple((jnp.zeros(item.shape, jnp.float32) for item in shapes))
    sums, (block_out, tokens_grad) = lax.scan(one_sequence, init, (tokens, cotangent))
    return (block_out, tokens_grad, sums[0], sums[1], sums[2], sums[3], sums[4], sums[5], sums[6], sums[7], sums[8])
```

```python
import functools

import jax
import jax.numpy as jnp
import numpy as np
from jax import lax
from jax.experimental import pallas as pl
from jax.experimental.pallas import tpu as pltpu
from jax.sharding import PartitionSpec as P

QUERY_HEADS = 15
KEY_VALUE_HEADS = 5
HEAD_SIZE = 64
GROUP = QUERY_HEADS // KEY_VALUE_HEADS
EPS = 1e-05
KERNEL_VMEM = 40 * 1024 * 1024


def dot(left, right):
    return jnp.dot(left, right, preferred_element_type=jnp.float32)


def dot_rows(left, right):
    return lax.dot_general(
        left, right, (((1,), (1,)), ((), ())), preferred_element_type=jnp.float32
    )


def dot_cols(left, right):
    return lax.dot_general(
        left, right, (((0,), (0,)), ((), ())), preferred_element_type=jnp.float32
    )


def rms_scale(rows):
    return lax.rsqrt(jnp.mean(rows * rows, axis=-1, keepdims=True) + EPS)


def norm_back(grad_norm, rows, scale_rows, gain):
    normed = rows * scale_rows
    scaled = grad_norm * gain
    return scale_rows * (scaled - normed * jnp.mean(scaled * normed, axis=-1, keepdims=True))


def after(value, *others):
    return lax.optimization_barrier((value, *others))[0]


def bits_of(count):
    return count.bit_length() - 1


def flip_blocks(rows, shards, index):
    width = rows.shape[-1] // shards
    bits = bits_of(shards)
    for place in range(bits):
        step = width << place
        pieces = [rows[..., i * step : (i + 1) * step] for i in range(rows.shape[-1] // step)]
        swapped = jnp.concatenate([pieces[i ^ 1] for i in range(len(pieces))], -1)
        rows = jnp.where((index >> (bits - 1 - place)) & 1 == 1, swapped, rows)
    return rows


def reverse_blocks(rows, shards):
    width = rows.shape[-1] // shards
    bits = bits_of(shards)
    order = [int(format(i, f"0{bits}b")[::-1], 2) for i in range(shards)]
    return jnp.concatenate([rows[..., i * width : (i + 1) * width] for i in order], -1)


def to_relative(rows, shards, index):
    return flip_blocks(reverse_blocks(rows, shards), shards, index)


def from_relative(rows, shards, index):
    return reverse_blocks(flip_blocks(rows, shards, index), shards)


def swap(value, axis, bit):
    size = lax.axis_size(axis)
    return lax.ppermute(value, axis, [(i, i ^ bit) for i in range(size)])


def gather_rows(rows):
    for place in reversed(range(bits_of(lax.axis_size("shard")))):
        rows = jnp.concatenate([rows, swap(rows, "shard", 1 << place)], 0)
    return rows


def scatter_rows(rows):
    for place in range(bits_of(lax.axis_size("shard"))):
        half = rows.shape[0] // 2
        rows = rows[:half] + swap(rows[half:], "shard", 1 << place)
    return rows


def ring(value):
    size = lax.axis_size("tensor")
    return lax.ppermute(value, "tensor", [(i, (i + 1) % size) for i in range(size)])


def ring_gather(rows):
    pieces = [rows]
    for _ in range(lax.axis_size("tensor") - 1):
        pieces.append(ring(pieces[-1]))
    return pieces


def ring_scatter(pieces):
    total = pieces[1]
    for piece in pieces[2:] + pieces[:1]:
        total = piece + ring(total)
    return total


SEND_FIRST = [(0, 0), (1, 2), (2, 1), (3, 3)]
SEND_SECOND = [(0, 2), (1, 0), (2, 3), (3, 1)]


def one_sequence(block, odd):
    first = jnp.where(odd, block[1], block[0])
    second = jnp.where(odd, block[0], block[1])
    return jnp.concatenate(
        [
            lax.ppermute(first, "tensor", SEND_FIRST),
            lax.ppermute(second, "tensor", SEND_SECOND),
        ],
        0,
    )


def both_sequences(rows, odd):
    half = rows.shape[0] // 2
    first = lax.ppermute(rows[:half], "tensor", [(b, a) for a, b in SEND_FIRST])
    second = lax.ppermute(rows[half:], "tensor", [(b, a) for a, b in SEND_SECOND])
    return jnp.stack([jnp.where(odd, second, first), jnp.where(odd, first, second)])


def sum_group(rows):
    axes = ("context", "tensor")
    group = lax.axis_size(axes)
    count = rows.shape[0]
    chunk = -(-count // group)
    if chunk > 16:
        chunk = -(-chunk // 16) * 16
    padded = jnp.pad(rows, ((0, chunk * group - count), (0, 0)))
    parts = lax.all_to_all(padded, axes, split_axis=0, concat_axis=0, tiled=True)
    parts = parts.reshape(group, chunk, rows.shape[1]).astype(jnp.float32)
    total = jnp.sum(parts, axis=0).astype(jnp.bfloat16)
    spread = jnp.broadcast_to(total[None], (group,) + total.shape).reshape(padded.shape)
    return lax.all_to_all(spread, axes, split_axis=0, concat_axis=0, tiled=True)[:count]


def rope_tables(length):
    half = HEAD_SIZE // 2
    freq = np.float32(10000.0) ** (-np.arange(half).astype(np.float32) * 2.0 / HEAD_SIZE)
    angle = np.arange(length).astype(np.float32)[:, None] * freq.astype(np.float32)[None, :]
    cosine, sine = np.cos(angle), np.sin(angle)
    return np.concatenate([cosine, cosine, -sine, sine], 1).astype(np.float32)


def turn(head, table):
    half = HEAD_SIZE // 2
    swapped = jnp.concatenate([head[:, half:], head[:, :half]], 1)
    return head * table[:, :HEAD_SIZE] + swapped * table[:, HEAD_SIZE:]


def turn_back(head, table):
    half = HEAD_SIZE // 2
    swapped = jnp.concatenate([head[:, half:], head[:, :half]], 1)
    return head * table[:, :HEAD_SIZE] - swapped * table[:, HEAD_SIZE:]


def head_cols(index):
    return slice(index * HEAD_SIZE, (index + 1) * HEAD_SIZE)


def attend_kernel(q_ref, k_ref, v_ref, qt_ref, kt_ref, qp_ref, kp_ref, mix_ref, log_ref, qr_ref, kr_ref):
    allowed = kp_ref[...] <= qp_ref[...]
    allowed = jnp.concatenate([allowed.astype(jnp.int32)] * GROUP, 0) > 0
    rows = q_ref.shape[0]
    for g in range(KEY_VALUE_HEADS):
        key = turn(k_ref[:, head_cols(g)], kt_ref[...]).astype(jnp.bfloat16)
        kr_ref[:, head_cols(g)] = key
        value = v_ref[:, head_cols(g)]
        heads = []
        for i in range(GROUP):
            cols = head_cols(g * GROUP + i)
            head = turn(q_ref[:, cols], qt_ref[...]).astype(jnp.bfloat16)
            qr_ref[:, cols] = head
            heads.append(head)
        query = jnp.concatenate(heads, 0)
        scores = dot_rows(query, key) * HEAD_SIZE ** (-0.5)
        scores = jnp.where(allowed, scores, -1e30)
        peak = jnp.max(scores, axis=-1, keepdims=True)
        expd = jnp.exp(scores - peak)
        total = jnp.sum(expd, axis=-1, keepdims=True)
        probs = (expd / total).astype(jnp.bfloat16)
        mixed = dot(probs, value).astype(jnp.bfloat16)
        for i in range(GROUP):
            mix_ref[:, head_cols(g * GROUP + i)] = mixed[i * rows : (i + 1) * rows]
        log_ref[:, g : g + 1] = peak + jnp.log(total)


def attend(query, key, value, query_table, key_table, query_pos, key_pos):
    rows, keys = query.shape[0], key.shape[0]
    return pl.pallas_call(
        attend_kernel,
        out_shape=(
            jax.ShapeDtypeStruct(query.shape, jnp.bfloat16),
            jax.ShapeDtypeStruct((GROUP * rows, 8), jnp.float32),
            jax.ShapeDtypeStruct(query.shape, jnp.bfloat16),
            jax.ShapeDtypeStruct(key.shape, jnp.bfloat16),
        ),
        compiler_params=pltpu.CompilerParams(vmem_limit_bytes=KERNEL_VMEM),
        cost_estimate=pl.CostEstimate(
            flops=4 * rows * keys * QUERY_HEADS * HEAD_SIZE,
            transcendentals=rows * keys * QUERY_HEADS,
            bytes_accessed=4_000_000,
        ),
        name="attend",
    )(query, key, value, query_table, key_table, query_pos, key_pos)


def attend_back_kernel(
    q_ref, k_ref, v_ref, mix_ref, gm_ref, log_ref, qt_ref, kt_ref, qp_ref, kp_ref, gq_ref, gkv_ref
):
    allowed = kp_ref[...] <= qp_ref[...]
    allowed = jnp.concatenate([allowed.astype(jnp.int32)] * GROUP, 0) > 0
    rows = q_ref.shape[0]
    for g in range(KEY_VALUE_HEADS):
        key, value = k_ref[:, head_cols(g)], v_ref[:, head_cols(g)]
        each = [head_cols(g * GROUP + i) for i in range(GROUP)]
        query = jnp.concatenate([q_ref[:, cols] for cols in each], 0)
        mixed = jnp.concatenate([mix_ref[:, cols] for cols in each], 0)
        grad_mix = jnp.concatenate([gm_ref[:, cols] for cols in each], 0)
        scores = dot_rows(query, key) * HEAD_SIZE ** (-0.5)
        scores = jnp.where(allowed, scores, -1e30)
        probs = jnp.exp(scores - log_ref[:, g : g + 1])
        grad_probs = dot_rows(grad_mix, value)
        delta = jnp.sum(
            grad_mix.astype(jnp.float32) * mixed.astype(jnp.float32), axis=-1, keepdims=True
        )
        grad_scores = (probs * (grad_probs - delta) * HEAD_SIZE ** (-0.5)).astype(jnp.bfloat16)
        grad_query = dot(grad_scores, key)
        grad_key = dot_cols(grad_scores, query)
        grad_value = dot_cols(probs.astype(jnp.bfloat16), grad_mix)
        for i in range(GROUP):
            head = turn_back(grad_query[i * rows : (i + 1) * rows], qt_ref[...])
            gq_ref[:, each[i]] = head.astype(jnp.bfloat16)
        gkv_ref[:, head_cols(g)] = turn_back(grad_key, kt_ref[...]).astype(jnp.bfloat16)
        gkv_ref[:, head_cols(KEY_VALUE_HEADS + g)] = grad_value.astype(jnp.bfloat16)


def attend_back(query, key, value, mix, grad_mix, log_total, query_table, key_table, query_pos, key_pos):
    rows, keys = query.shape[0], key.shape[0]
    return pl.pallas_call(
        attend_back_kernel,
        out_shape=(
            jax.ShapeDtypeStruct(query.shape, jnp.bfloat16),
            jax.ShapeDtypeStruct((keys, 2 * key.shape[1]), jnp.bfloat16),
        ),
        compiler_params=pltpu.CompilerParams(vmem_limit_bytes=KERNEL_VMEM),
        cost_estimate=pl.CostEstimate(
            flops=10 * rows * keys * QUERY_HEADS * HEAD_SIZE,
            transcendentals=rows * keys * QUERY_HEADS,
            bytes_accessed=6_000_000,
        ),
        name="attend_back",
    )(query, key, value, mix, grad_mix, log_total, query_table, key_table, query_pos, key_pos)


def body(
    tokens,
    attn_gain,
    w_query,
    key_weight,
    value_weight,
    w_output,
    mlp_gain,
    w_gate,
    w_up,
    w_down,
    cotangent,
):
    _, length, width = tokens.shape
    shards, shard = lax.axis_size("shard"), lax.axis_index("shard")
    context, place = lax.axis_index("context"), lax.axis_index("tensor")
    places = lax.axis_size("tensor")
    rows = 2 * length
    odd = place % 2 == 1
    q_cols, kv_cols, hidden_cols = w_query.shape[1], key_weight.shape[1], w_gate.shape[1]

    sequence, half = place // 2, place % 2

    def blocks_of(which, part):
        first = which * places + 2 * part
        return [first + sequence, first + 1 - sequence]

    starts = [
        block * length
        for which in (context, 1 - context)
        for part in (half, 1 - half)
        for block in blocks_of(which, part)
    ]
    table = jnp.asarray(rope_tables(length * places * lax.axis_size("context")))
    key_table = jnp.concatenate([lax.dynamic_slice_in_dim(table, at, length, 0) for at in starts], 0)
    key_pos = jnp.concatenate([at + jnp.arange(length, dtype=jnp.int32) for at in starts])
    query_table, query_pos = key_table[:rows], key_pos[:rows, None]
    key_pos = key_pos[None, :]

    own = one_sequence(to_relative(tokens, shards, shard), odd)
    beside = swap(own, "tensor", 1)
    across = swap(own, "context", 1)
    across_beside = swap(after(beside, across), "context", 1)
    all_tokens = jnp.concatenate([own, beside, across, across_beside], 0)

    attn_local = jnp.concatenate([w_query, key_weight, value_weight], 1)
    mlp_local = jnp.concatenate([w_gate, w_up, w_down.T], 1)
    gains = gather_rows(jnp.concatenate([attn_gain[:, None], mlp_gain[:, None]], 1))
    gain_a, gain_m = gains[:, 0], gains[:, 1]
    attn_weight = gather_rows(attn_local)
    out_weight = gather_rows(after(w_output.T, attn_weight))
    mlp_weight = gather_rows(after(mlp_local, out_weight))
    w_q, w_kv = attn_weight[:, :q_cols], attn_weight[:, q_cols:]
    w_in, w_dn = mlp_weight[:, : 2 * hidden_cols], mlp_weight[:, 2 * hidden_cols :]

    own_cot = one_sequence(after(to_relative(cotangent, shards, shard), across_beside), odd)
    cot_group = jnp.concatenate(ring_gather(own_cot), 0)

    all_float = all_tokens.astype(jnp.float32)
    all_scale = rms_scale(all_float)
    all_normed = (all_float * all_scale * gain_a).astype(jnp.bfloat16)
    tokens_f, scale_a, normed_a = all_float[:rows], all_scale[:rows], all_normed[:rows]
    query = dot(normed_a, w_q)
    key_value = dot(all_normed, w_kv)
    key, value = key_value[:, :kv_cols], key_value[:, kv_cols:].astype(jnp.bfloat16)
    mix, log_total, query_rot, key_rot = attend(
        query, key, value, query_table, key_table, query_pos, key_pos
    )
    hidden = tokens_f + dot_rows(mix, out_weight)
    scale_m = rms_scale(hidden)
    normed_m = (hidden * scale_m * gain_m).astype(jnp.bfloat16)

    group = jnp.concatenate(ring_gather(normed_m), 0)
    grad_act = dot(cot_group, w_dn)
    inner = dot(group, w_in)
    gate, up_vals = inner[:, :hidden_cols], inner[:, hidden_cols:]
    sigma = jax.nn.sigmoid(gate)
    act = (gate * sigma * up_vals).astype(jnp.bfloat16)
    grad_up = (grad_act * gate * sigma).astype(jnp.bfloat16)
    grad_gate = (grad_act * up_vals * sigma * (1.0 + gate * (1.0 - sigma))).astype(jnp.bfloat16)
    grad_in = jnp.concatenate([grad_gate, grad_up], 1)
    back = dot_rows(grad_in, w_in).astype(jnp.bfloat16)
    grad_nm = ring_scatter([back[i * rows : (i + 1) * rows] for i in range(places)])
    grad_hidden = own_cot.astype(jnp.float32) + norm_back(
        grad_nm.astype(jnp.float32), hidden, scale_m, gain_m
    )
    grad_hidden_low = grad_hidden.astype(jnp.bfloat16)
    grad_mix = dot(grad_hidden_low, out_weight).astype(jnp.bfloat16)

    grad_query, grad_kv = attend_back(
        query_rot, key_rot, value, mix, grad_mix, log_total, query_table, key_table, query_pos, key_pos
    )
    pair = grad_kv[: 2 * rows] + swap(grad_kv[2 * rows :], "context", 1)
    own_kv = pair[:rows] + swap(pair[rows:], "tensor", 1)
    grad_na = dot_rows(grad_query, w_q) + dot_rows(own_kv, w_kv)
    grad_tokens = grad_hidden + norm_back(grad_na, tokens_f, scale_a, gain_a)
    grad_tokens = from_relative(grad_tokens.astype(jnp.bfloat16), shards, shard)
    tokens_grad = both_sequences(grad_tokens, odd)

    forward = dot_rows(act, w_dn).astype(jnp.bfloat16)
    forward = after(forward, grad_nm)
    mlp_out = ring_scatter([forward[i * rows : (i + 1) * rows] for i in range(places)])
    block = (hidden + mlp_out.astype(jnp.float32)).astype(jnp.bfloat16)
    block_out = both_sequences(from_relative(block, shards, shard), odd)

    mlp_term = jnp.concatenate(
        [dot_cols(group, grad_in).astype(jnp.bfloat16), dot_cols(cot_group, act).astype(jnp.bfloat16)], 1
    )
    mlp_term = scatter_rows(mlp_term)
    mlp_total = mlp_term.astype(jnp.float32) + swap(mlp_term, "context", 1).astype(jnp.float32)
    gate_total = mlp_total[:, :hidden_cols]
    up_total = mlp_total[:, hidden_cols : 2 * hidden_cols]
    down_total = mlp_total[:, 2 * hidden_cols :].T
    gain_m_total = jnp.sum(
        w_gate.astype(jnp.float32) * gate_total + w_up.astype(jnp.float32) * up_total, axis=1
    )
    for place_bit in range(bits_of(places)):
        gain_m_total = gain_m_total + swap(gain_m_total, "tensor", 1 << place_bit)
    gain_m_total = gain_m_total / mlp_gain

    out_term = scatter_rows(dot_cols(grad_hidden_low, mix).astype(jnp.bfloat16))
    out_total = sum_group(out_term).astype(jnp.float32).T
    attn_term = jnp.concatenate(
        [
            dot_cols(normed_a, grad_query).astype(jnp.bfloat16),
            dot_cols(all_normed, grad_kv).astype(jnp.bfloat16),
        ],
        1,
    )
    attn_total = sum_group(scatter_rows(attn_term)).astype(jnp.float32)
    gain_a_total = jnp.sum(attn_local.astype(jnp.float32) * attn_total, axis=1) / attn_gain
    return (
        block_out,
        tokens_grad,
        gain_a_total,
        attn_total[:, :q_cols],
        attn_total[:, q_cols : q_cols + kv_cols],
        attn_total[:, q_cols + kv_cols :],
        out_total,
        gain_m_total,
        gate_total,
        up_total,
        down_total,
    )


def solution(mesh):
    specs = (
        P("shard", ("context", "tensor"), None),
        P("shard"),
        P("shard", None),
        P("shard", None),
        P("shard", None),
        P(None, "shard"),
        P("shard"),
        P("shard", "tensor"),
        P("shard", "tensor"),
        P("tensor", "shard"),
    )
    return jax.shard_map(
        body,
        mesh=mesh,
        in_specs=specs + specs[:1],
        out_specs=specs[:1] + specs,
        check_vma=False,
    )
```

```python
import jax
import jax.numpy as jnp
import numpy as np
from jax import lax
from jax.experimental import pallas as pl
from jax.experimental.pallas import tpu as pltpu
from jax.sharding import PartitionSpec as P

QUERY_HEADS = 15
KEY_VALUE_HEADS = 5
HEAD_SIZE = 64
GROUP = QUERY_HEADS // KEY_VALUE_HEADS
SCALE = HEAD_SIZE ** (-0.5)
EPS = 1e-05
KERNEL_VMEM = 40 * 1024 * 1024


def dot(left, right):
    return jnp.dot(left, right, preferred_element_type=jnp.float32)


def dot_rows(left, right):
    return lax.dot_general(
        left, right, (((1,), (1,)), ((), ())), preferred_element_type=jnp.float32
    )


def dot_cols(left, right):
    return lax.dot_general(
        left, right, (((0,), (0,)), ((), ())), preferred_element_type=jnp.float32
    )


def rms_scale(rows):
    return lax.rsqrt(jnp.mean(rows * rows, axis=-1, keepdims=True) + EPS)


def norm_back(grad_norm, rows, scale_rows, gain):
    normed = rows * scale_rows
    scaled = grad_norm * gain
    return scale_rows * (scaled - normed * jnp.mean(scaled * normed, axis=-1, keepdims=True))


def after(value, *others):
    return lax.optimization_barrier((value, *others))[0]


def bits_of(count):
    return count.bit_length() - 1


def flip_blocks(rows, shards, index):
    width = rows.shape[-1] // shards
    bits = bits_of(shards)
    for place in range(bits):
        step = width << place
        pieces = [rows[..., i * step : (i + 1) * step] for i in range(rows.shape[-1] // step)]
        swapped = jnp.concatenate([pieces[i ^ 1] for i in range(len(pieces))], -1)
        rows = jnp.where((index >> (bits - 1 - place)) & 1 == 1, swapped, rows)
    return rows


def reverse_blocks(rows, shards):
    width = rows.shape[-1] // shards
    bits = bits_of(shards)
    order = [int(format(i, f"0{bits}b")[::-1], 2) for i in range(shards)]
    return jnp.concatenate([rows[..., i * width : (i + 1) * width] for i in order], -1)


def to_relative(rows, shards, index):
    return flip_blocks(reverse_blocks(rows, shards), shards, index)


def from_relative(rows, shards, index):
    return reverse_blocks(flip_blocks(rows, shards, index), shards)


def swap(value, axis, bit):
    size = lax.axis_size(axis)
    return lax.ppermute(value, axis, [(i, i ^ bit) for i in range(size)])


def gather_pieces(rows, gate=None):
    pieces = [rows]
    for place in reversed(range(bits_of(lax.axis_size("shard")))):
        if len(pieces) > 2:
            pieces = [jnp.concatenate(pieces, 0)]
        sent = pieces if gate is None else [after(piece, *gate) for piece in pieces]
        gate = None
        pieces = pieces + [swap(piece, "shard", 1 << place) for piece in sent]
    return pieces


def gather_rows(rows):
    return jnp.concatenate(gather_pieces(rows), 0)


def scatter_rows(rows, first, last):
    for place in range(first, last):
        half = rows.shape[0] // 2
        rows = rows[:half] + swap(rows[half:], "shard", 1 << place)
    return rows


def shift(value, count):
    size = lax.axis_size("tensor")
    return lax.ppermute(value, "tensor", [(i, (i + count) % size) for i in range(size)])


def one_sequence(block, upper):
    mine = jnp.where(upper, block[1], block[0])
    other = jnp.where(upper, block[0], block[1])
    return jnp.concatenate([mine, swap(other, "tensor", 2)], 0)


def both_sequences(mine, other, upper):
    return jnp.stack([jnp.where(upper, other, mine), jnp.where(upper, mine, other)])


def group_sum_parts(rows):
    axes = ("context", "tensor")
    group = lax.axis_size(axes)
    count = rows.shape[0]
    chunk = -(-count // group)
    if chunk > 16:
        chunk = -(-chunk // 16) * 16
    padded = jnp.pad(rows, ((0, chunk * group - count), (0, 0)))
    parts = lax.all_to_all(padded, axes, split_axis=0, concat_axis=0, tiled=True)
    parts = parts.reshape(group, chunk, rows.shape[1]).astype(jnp.float32)
    return jnp.sum(parts, axis=0).astype(jnp.bfloat16)


def group_collect(part, count):
    axes = ("context", "tensor")
    group = lax.axis_size(axes)
    spread = jnp.broadcast_to(part[None], (group,) + part.shape)
    spread = spread.reshape(group * part.shape[0], part.shape[1])
    return lax.all_to_all(spread, axes, split_axis=0, concat_axis=0, tiled=True)[:count]


def rope_tables(length):
    half = HEAD_SIZE // 2
    freq = np.float32(10000.0) ** (-np.arange(half).astype(np.float32) * 2.0 / HEAD_SIZE)
    angle = np.arange(length).astype(np.float32)[:, None] * freq.astype(np.float32)[None, :]
    cosine, sine = np.cos(angle), np.sin(angle)
    return np.concatenate([cosine, cosine, -sine, sine], 1).astype(np.float32)


def turn(head, table):
    half = HEAD_SIZE // 2
    swapped = jnp.concatenate([head[:, half:], head[:, :half]], 1)
    return head * table[:, :HEAD_SIZE] + swapped * table[:, HEAD_SIZE:]


def turn_back(head, table):
    half = HEAD_SIZE // 2
    swapped = jnp.concatenate([head[:, half:], head[:, :half]], 1)
    return head * table[:, :HEAD_SIZE] - swapped * table[:, HEAD_SIZE:]


def head_cols(index):
    return slice(index * HEAD_SIZE, (index + 1) * HEAD_SIZE)


def attend_kernel(q_ref, k_ref, v_ref, qt_ref, kt_ref, qp_ref, kp_ref, mix_ref, log_ref, qr_ref, kr_ref):
    hidden = jnp.where(kp_ref[...] <= qp_ref[...], 0.0, -1e30)
    hidden = jnp.concatenate([hidden] * GROUP, 0)
    rows = q_ref.shape[0]
    for g in range(KEY_VALUE_HEADS):
        key = turn(k_ref[:, head_cols(g)], kt_ref[...]).astype(jnp.bfloat16)
        kr_ref[:, head_cols(g)] = key
        value = v_ref[:, head_cols(g)]
        heads = []
        for i in range(GROUP):
            cols = head_cols(g * GROUP + i)
            head = turn(q_ref[:, cols], qt_ref[...]).astype(jnp.bfloat16) * SCALE
            qr_ref[:, cols] = head
            heads.append(head)
        query = jnp.concatenate(heads, 0)
        scores = dot_rows(query, key) + hidden
        peak = jnp.max(scores, axis=-1, keepdims=True)
        expd = jnp.exp(scores - peak)
        total = jnp.sum(expd, axis=-1, keepdims=True)
        mixed = (dot(expd.astype(jnp.bfloat16), value) / total).astype(jnp.bfloat16)
        for i in range(GROUP):
            mix_ref[:, head_cols(g * GROUP + i)] = mixed[i * rows : (i + 1) * rows]
        log_ref[:, g : g + 1] = peak + jnp.log(total)


def attend(query, key, value, query_table, key_table, query_pos, key_pos):
    rows, keys = query.shape[0], key.shape[0]
    return pl.pallas_call(
        attend_kernel,
        out_shape=(
            jax.ShapeDtypeStruct(query.shape, jnp.bfloat16),
            jax.ShapeDtypeStruct((GROUP * rows, 8), jnp.float32),
            jax.ShapeDtypeStruct(query.shape, jnp.bfloat16),
            jax.ShapeDtypeStruct(key.shape, jnp.bfloat16),
        ),
        compiler_params=pltpu.CompilerParams(vmem_limit_bytes=KERNEL_VMEM),
        cost_estimate=pl.CostEstimate(
            flops=4 * rows * keys * QUERY_HEADS * HEAD_SIZE,
            transcendentals=rows * keys * QUERY_HEADS,
            bytes_accessed=4_000_000,
        ),
        name="attend",
    )(query, key, value, query_table, key_table, query_pos, key_pos)


def attend_back_kernel(
    q_ref, k_ref, v_ref, mix_ref, gm_ref, log_ref, qt_ref, kt_ref, qp_ref, kp_ref, gq_ref, gkv_ref
):
    hidden = jnp.where(kp_ref[...] <= qp_ref[...], 0.0, -1e30)
    hidden = jnp.concatenate([hidden] * GROUP, 0)
    rows = q_ref.shape[0]
    for g in range(KEY_VALUE_HEADS):
        key, value = k_ref[:, head_cols(g)], v_ref[:, head_cols(g)]
        each = [head_cols(g * GROUP + i) for i in range(GROUP)]
        query = jnp.concatenate([q_ref[:, cols] for cols in each], 0)
        mixed = jnp.concatenate([mix_ref[:, cols] for cols in each], 0)
        grad_mix = jnp.concatenate([gm_ref[:, cols] for cols in each], 0)
        scores = dot_rows(query, key) + hidden
        probs = jnp.exp(scores - log_ref[:, g : g + 1])
        grad_probs = dot_rows(grad_mix, value)
        delta = jnp.sum(
            grad_mix.astype(jnp.float32) * mixed.astype(jnp.float32), axis=-1, keepdims=True
        )
        grad_scores = (probs * (grad_probs - delta)).astype(jnp.bfloat16)
        grad_query = dot(grad_scores, key) * SCALE
        grad_key = dot_cols(grad_scores, query)
        grad_value = dot_cols(probs.astype(jnp.bfloat16), grad_mix)
        for i in range(GROUP):
            head = turn_back(grad_query[i * rows : (i + 1) * rows], qt_ref[...])
            gq_ref[:, each[i]] = head.astype(jnp.bfloat16)
        gkv_ref[:, head_cols(g)] = turn_back(grad_key, kt_ref[...]).astype(jnp.bfloat16)
        gkv_ref[:, head_cols(KEY_VALUE_HEADS + g)] = grad_value.astype(jnp.bfloat16)


def attend_back(query, key, value, mix, grad_mix, log_total, query_table, key_table, query_pos, key_pos):
    rows, keys = query.shape[0], key.shape[0]
    return pl.pallas_call(
        attend_back_kernel,
        out_shape=(
            jax.ShapeDtypeStruct(query.shape, jnp.bfloat16),
            jax.ShapeDtypeStruct((keys, 2 * key.shape[1]), jnp.bfloat16),
        ),
        compiler_params=pltpu.CompilerParams(vmem_limit_bytes=KERNEL_VMEM),
        cost_estimate=pl.CostEstimate(
            flops=10 * rows * keys * QUERY_HEADS * HEAD_SIZE,
            transcendentals=rows * keys * QUERY_HEADS,
            bytes_accessed=6_000_000,
        ),
        name="attend_back",
    )(query, key, value, mix, grad_mix, log_total, query_table, key_table, query_pos, key_pos)


def body(
    tokens,
    attn_gain,
    w_query,
    key_weight,
    value_weight,
    w_output,
    mlp_gain,
    w_gate,
    w_up,
    w_down,
    cotangent,
):
    _, length, width = tokens.shape
    shards, shard = lax.axis_size("shard"), lax.axis_index("shard")
    context, place = lax.axis_index("context"), lax.axis_index("tensor")
    places = lax.axis_size("tensor")
    rows = 2 * length
    upper = place // 2 == 1
    q_cols, kv_cols, hidden_cols = w_query.shape[1], key_weight.shape[1], w_gate.shape[1]

    starts = [
        (which * places + (place ^ step)) * length
        for which in (context, 1 - context)
        for step in (0, 2, 1, 3)
    ]
    table = jnp.asarray(rope_tables(length * places * lax.axis_size("context")))
    key_table = jnp.concatenate([lax.dynamic_slice_in_dim(table, at, length, 0) for at in starts], 0)
    key_pos = jnp.concatenate([at + jnp.arange(length, dtype=jnp.int32) for at in starts])
    query_table, query_pos = key_table[:rows], key_pos[:rows, None]
    key_pos = key_pos[None, :]

    own = one_sequence(to_relative(tokens, shards, shard), upper)
    beside = swap(own, "tensor", 1)
    across = swap(own, "context", 1)
    across_beside = swap(after(beside, across), "context", 1)
    all_tokens = jnp.concatenate([own, beside, across, across_beside], 0)

    attn_local = jnp.concatenate([w_query, key_weight, value_weight], 1)
    mlp_local = jnp.concatenate([w_gate, w_up, w_down.T], 1)
    attn_pieces = gather_pieces(attn_local)
    gains = gather_rows(jnp.concatenate([attn_gain[:, None], mlp_gain[:, None]], 1))
    gain_a, gain_m = gains[:, 0], gains[:, 1]
    out_pieces = gather_pieces(w_output.T, attn_pieces[1:2])
    mlp_pieces = gather_pieces(mlp_local, out_pieces[1:2])
    attn_weight = jnp.concatenate(attn_pieces, 0)
    out_weight = jnp.concatenate(out_pieces, 0)
    mlp_weight = jnp.concatenate(mlp_pieces, 0)
    w_q, w_kv = attn_weight[:, :q_cols], attn_weight[:, q_cols:]
    w_in, w_dn = mlp_weight[:, : 2 * hidden_cols], mlp_weight[:, 2 * hidden_cols :]

    cots = [after(to_relative(cotangent, shards, shard), beside)]
    cots.append(shift(cots[0], 1))
    cots = [after(cots[0], cots[1]), cots[1], shift(cots[1], 1)]
    cots.append(shift(cots[0], -1))
    all_tokens = after(all_tokens, cots[1])

    all_float = all_tokens.astype(jnp.float32)
    all_scale = rms_scale(all_float)
    all_normed = (all_float * all_scale * gain_a).astype(jnp.bfloat16)
    tokens_f, scale_a, normed_a = all_float[:rows], all_scale[:rows], all_normed[:rows]
    query = dot(normed_a, w_q)
    key_value = dot(all_normed, w_kv)
    key, value = key_value[:, :kv_cols], key_value[:, kv_cols:].astype(jnp.bfloat16)
    mix, log_total, query_rot, key_rot = attend(
        query, key, value, query_table, key_table, query_pos, key_pos
    )
    hidden = tokens_f + dot_rows(mix, out_weight)
    scale_m = rms_scale(hidden)
    normed_m = (hidden * scale_m * gain_m).astype(jnp.bfloat16)

    normed_m, cots[2], cots[3] = lax.optimization_barrier((normed_m, cots[2], cots[3]))

    def cot_of(k):
        above = ((place - k) % places) // 2 == 1
        pair = (cots[k], cots[(k + 2) % places])
        return jnp.concatenate([jnp.where(above, one[1], one[0]) for one in pair], 0)

    cots = [cot_of(k) for k in range(places)]
    own_cot = cots[0]
    barrier = lax.optimization_barrier

    group, acts, grads_in, backs = [normed_m], [], [], []
    arriving = shift(normed_m, 1)
    for k, cot in enumerate(cots):
        if k > 0:
            group.append(arriving)
            if k + 1 < places:
                arriving = shift(after(arriving, backs[-1]), 1)
        rows_in = group[k]
        grad_act = dot(cot, w_dn)
        inner = dot(rows_in, w_in)
        gate, up_vals = inner[:, :hidden_cols], inner[:, hidden_cols:]
        sigma = jax.nn.sigmoid(gate)
        acts.append((gate * sigma * up_vals).astype(jnp.bfloat16))
        grad_up = (grad_act * gate * sigma).astype(jnp.bfloat16)
        grad_gate = (grad_act * up_vals * sigma * (1.0 + gate * (1.0 - sigma))).astype(jnp.bfloat16)
        grads_in.append(jnp.concatenate([grad_gate, grad_up], 1))
        backs.append(dot_rows(grads_in[-1], w_in).astype(jnp.bfloat16))
    grad_nm = backs[1]
    for k in [*range(2, places), 0]:
        grad_nm = backs[k] + shift(grad_nm, 1)
    grad_hidden = own_cot.astype(jnp.float32) + norm_back(
        grad_nm.astype(jnp.float32), hidden, scale_m, gain_m
    )
    grad_hidden_low = grad_hidden.astype(jnp.bfloat16)
    grad_mix = dot(grad_hidden_low, out_weight).astype(jnp.bfloat16)

    bits = bits_of(shards)
    group, grad_in = jnp.concatenate(group, 0), jnp.concatenate(grads_in, 0)
    act, cot_group = jnp.concatenate(acts, 0), jnp.concatenate(cots, 0)
    mlp_term = jnp.concatenate(
        [dot_cols(group, grad_in).astype(jnp.bfloat16), dot_cols(cot_group, act).astype(jnp.bfloat16)], 1
    )
    mlp_term = scatter_rows(mlp_term, 0, bits)
    out_term = scatter_rows(dot_cols(grad_hidden_low, mix).astype(jnp.bfloat16), 0, 1)
    forward = [dot_rows(act, w_dn).astype(jnp.bfloat16) for act in acts]
    total = shift(after(forward[1], grad_mix), 1)

    grad_query, grad_kv = attend_back(
        query_rot, key_rot, value, mix, grad_mix, log_total, query_table, key_table, query_pos, key_pos
    )
    grad_query, grad_kv, mlp_term, out_term, total = barrier(
        (grad_query, grad_kv, mlp_term, out_term, total)
    )
    attn_term = jnp.concatenate(
        [
            dot_cols(normed_a, grad_query).astype(jnp.bfloat16),
            dot_cols(all_normed, grad_kv).astype(jnp.bfloat16),
        ],
        1,
    )
    attn_term = scatter_rows(attn_term, 0, bits)
    out_term = scatter_rows(out_term, 1, bits)
    pair = grad_kv[: 2 * rows] + swap(grad_kv[2 * rows :], "context", 1)
    total = shift(forward[2] + total, 1)
    mlp_across = swap(mlp_term, "context", 1)
    attn_term, out_term, pair, total, mlp_across = barrier(
        (attn_term, out_term, pair, total, mlp_across)
    )

    attn_part, out_part = group_sum_parts(attn_term), group_sum_parts(out_term)
    own_kv = pair[:rows] + swap(pair[rows:], "tensor", 1)
    grad_na = dot_rows(grad_query, w_q) + dot_rows(own_kv, w_kv)
    grad_tokens = grad_hidden + norm_back(grad_na, tokens_f, scale_a, gain_a)
    grad_tokens = from_relative(grad_tokens.astype(jnp.bfloat16), shards, shard)
    total = shift(forward[3] + total, 1)
    block = hidden + forward[0].astype(jnp.float32) + total.astype(jnp.float32)
    block = from_relative(block.astype(jnp.bfloat16), shards, shard)
    attn_part, out_part, grad_tokens, block = barrier((attn_part, out_part, grad_tokens, block))

    back_rows = swap(jnp.concatenate([block[length:], grad_tokens[length:]], 0), "tensor", 2)
    block_out = both_sequences(block[:length], back_rows[:length], upper)
    tokens_grad = both_sequences(grad_tokens[:length], back_rows[length:], upper)
    out_total = group_collect(out_part, out_term.shape[0]).astype(jnp.float32).T
    attn_total = group_collect(attn_part, attn_term.shape[0]).astype(jnp.float32)
    gain_a_total = jnp.sum(attn_local.astype(jnp.float32) * attn_total, axis=1) / attn_gain

    mlp_total = mlp_term.astype(jnp.float32) + mlp_across.astype(jnp.float32)
    gate_total = mlp_total[:, :hidden_cols]
    up_total = mlp_total[:, hidden_cols : 2 * hidden_cols]
    down_total = mlp_total[:, 2 * hidden_cols :].T
    gain_m_total = jnp.sum(
        w_gate.astype(jnp.float32) * gate_total + w_up.astype(jnp.float32) * up_total, axis=1
    )
    for place_bit in range(bits_of(places)):
        gain_m_total = gain_m_total + swap(gain_m_total, "tensor", 1 << place_bit)
    gain_m_total = gain_m_total / mlp_gain
    return (
        block_out,
        tokens_grad,
        gain_a_total,
        attn_total[:, :q_cols],
        attn_total[:, q_cols : q_cols + kv_cols],
        attn_total[:, q_cols + kv_cols :],
        out_total,
        gain_m_total,
        gate_total,
        up_total,
        down_total,
    )


def solution(mesh):
    specs = (
        P("shard", ("context", "tensor"), None),
        P("shard"),
        P("shard", None),
        P("shard", None),
        P("shard", None),
        P(None, "shard"),
        P("shard"),
        P("shard", "tensor"),
        P("shard", "tensor"),
        P("tensor", "shard"),
    )
    return jax.shard_map(
        body,
        mesh=mesh,
        in_specs=specs + specs[:1],
        out_specs=specs[:1] + specs,
        check_vma=False,
    )
```

```python
import jax
import jax.numpy as jnp
import numpy as np
from jax import lax
from jax.experimental import pallas as pl
from jax.experimental.pallas import tpu as pltpu
from jax.sharding import PartitionSpec as P

QUERY_HEADS = 15
KEY_VALUE_HEADS = 5
HEAD_SIZE = 64
GROUP = QUERY_HEADS // KEY_VALUE_HEADS
SCALE = HEAD_SIZE ** (-0.5)
EPS = 1e-05
KERNEL_VMEM = 40 * 1024 * 1024


def dot(left, right):
    return jnp.dot(left, right, preferred_element_type=jnp.float32)


def dot_rows(left, right):
    return lax.dot_general(
        left, right, (((1,), (1,)), ((), ())), preferred_element_type=jnp.float32
    )


def dot_cols(left, right):
    return lax.dot_general(
        left, right, (((0,), (0,)), ((), ())), preferred_element_type=jnp.float32
    )


def rms_scale(rows):
    return lax.rsqrt(jnp.mean(rows * rows, axis=-1, keepdims=True) + EPS)


def norm_back(grad_norm, rows, scale_rows, gain):
    normed = rows * scale_rows
    scaled = grad_norm * gain
    return scale_rows * (scaled - normed * jnp.mean(scaled * normed, axis=-1, keepdims=True))


def after(value, *others):
    return lax.optimization_barrier((value, *others))[0]


def bits_of(count):
    return count.bit_length() - 1


def flip_blocks(rows, shards, index):
    width = rows.shape[-1] // shards
    bits = bits_of(shards)
    for place in range(bits):
        step = width << place
        pieces = [rows[..., i * step : (i + 1) * step] for i in range(rows.shape[-1] // step)]
        swapped = jnp.concatenate([pieces[i ^ 1] for i in range(len(pieces))], -1)
        rows = jnp.where((index >> (bits - 1 - place)) & 1 == 1, swapped, rows)
    return rows


def reverse_blocks(rows, shards):
    width = rows.shape[-1] // shards
    bits = bits_of(shards)
    order = [int(format(i, f"0{bits}b")[::-1], 2) for i in range(shards)]
    return jnp.concatenate([rows[..., i * width : (i + 1) * width] for i in order], -1)


def to_relative(rows, shards, index):
    return flip_blocks(reverse_blocks(rows, shards), shards, index)


def from_relative(rows, shards, index):
    return reverse_blocks(flip_blocks(rows, shards, index), shards)


def swap(value, axis, bit):
    size = lax.axis_size(axis)
    return lax.ppermute(value, axis, [(i, i ^ bit) for i in range(size)])


def gather_pieces(rows, gate=None, later=None):
    pieces = [rows]
    for place in reversed(range(bits_of(lax.axis_size("shard")))):
        if len(pieces) > 2:
            pieces = [jnp.concatenate(pieces, 0)]
        sent = pieces
        if gate is not None:
            sent = [after(piece, *gate) for piece in pieces]
            gate = None
        elif later is not None:
            sent = pieces[:1] + [after(piece, later) for piece in pieces[1:]]
        pieces = pieces + [swap(piece, "shard", 1 << place) for piece in sent]
    return pieces


def gather_rows(rows):
    return jnp.concatenate(gather_pieces(rows), 0)


def scatter_rows(rows, first, last):
    for place in range(first, last):
        half = rows.shape[0] // 2
        rows = rows[:half] + swap(rows[half:], "shard", 1 << place)
    return rows


def shift(value, count):
    size = lax.axis_size("tensor")
    return lax.ppermute(value, "tensor", [(i, (i + count) % size) for i in range(size)])


def both_sequences(mine, other, upper):
    return jnp.stack([jnp.where(upper, other, mine), jnp.where(upper, mine, other)])


def group_sum_parts(rows):
    axes = ("context", "tensor")
    group = lax.axis_size(axes)
    count = rows.shape[0]
    chunk = -(-count // group)
    if chunk > 16:
        chunk = -(-chunk // 16) * 16
    padded = jnp.pad(rows, ((0, chunk * group - count), (0, 0)))
    parts = lax.all_to_all(padded, axes, split_axis=0, concat_axis=0, tiled=True)
    parts = parts.reshape(group, chunk, rows.shape[1]).astype(jnp.float32)
    return jnp.sum(parts, axis=0).astype(jnp.bfloat16)


def group_collect(part, count):
    axes = ("context", "tensor")
    group = lax.axis_size(axes)
    spread = jnp.broadcast_to(part[None], (group,) + part.shape)
    spread = spread.reshape(group * part.shape[0], part.shape[1])
    return lax.all_to_all(spread, axes, split_axis=0, concat_axis=0, tiled=True)[:count]


def rope_tables(length):
    half = HEAD_SIZE // 2
    freq = np.float32(10000.0) ** (-np.arange(half).astype(np.float32) * 2.0 / HEAD_SIZE)
    angle = np.arange(length).astype(np.float32)[:, None] * freq.astype(np.float32)[None, :]
    cosine, sine = np.cos(angle), np.sin(angle)
    return np.concatenate([cosine, cosine, -sine, sine], 1).astype(np.float32)


def turn(head, table):
    half = HEAD_SIZE // 2
    swapped = jnp.concatenate([head[:, half:], head[:, :half]], 1)
    return head * table[:, :HEAD_SIZE] + swapped * table[:, HEAD_SIZE:]


def turn_back(head, table):
    half = HEAD_SIZE // 2
    swapped = jnp.concatenate([head[:, half:], head[:, :half]], 1)
    return head * table[:, :HEAD_SIZE] - swapped * table[:, HEAD_SIZE:]


def head_cols(index):
    return slice(index * HEAD_SIZE, (index + 1) * HEAD_SIZE)


def attend_kernel(q_ref, k_ref, v_ref, qt_ref, kt_ref, qp_ref, kp_ref, mix_ref, log_ref, qr_ref, kr_ref):
    hidden = jnp.where(kp_ref[...] <= qp_ref[...], 0.0, -1e30)
    hidden = jnp.concatenate([hidden] * GROUP, 0)
    rows = q_ref.shape[0]
    for g in range(KEY_VALUE_HEADS):
        key = turn(k_ref[:, head_cols(g)], kt_ref[...]).astype(jnp.bfloat16)
        kr_ref[:, head_cols(g)] = key
        value = v_ref[:, head_cols(g)]
        heads = []
        for i in range(GROUP):
            cols = head_cols(g * GROUP + i)
            head = turn(q_ref[:, cols], qt_ref[...]).astype(jnp.bfloat16) * SCALE
            qr_ref[:, cols] = head
            heads.append(head)
        query = jnp.concatenate(heads, 0)
        scores = dot_rows(query, key) + hidden
        peak = jnp.max(scores, axis=-1, keepdims=True)
        expd = jnp.exp(scores - peak)
        total = jnp.sum(expd, axis=-1, keepdims=True)
        mixed = (dot(expd.astype(jnp.bfloat16), value) / total).astype(jnp.bfloat16)
        for i in range(GROUP):
            mix_ref[:, head_cols(g * GROUP + i)] = mixed[i * rows : (i + 1) * rows]
        log_ref[:, g : g + 1] = peak + jnp.log(total)


def attend(query, key, value, query_table, key_table, query_pos, key_pos):
    rows, keys = query.shape[0], key.shape[0]
    return pl.pallas_call(
        attend_kernel,
        out_shape=(
            jax.ShapeDtypeStruct(query.shape, jnp.bfloat16),
            jax.ShapeDtypeStruct((GROUP * rows, 8), jnp.float32),
            jax.ShapeDtypeStruct(query.shape, jnp.bfloat16),
            jax.ShapeDtypeStruct(key.shape, jnp.bfloat16),
        ),
        compiler_params=pltpu.CompilerParams(vmem_limit_bytes=KERNEL_VMEM),
        cost_estimate=pl.CostEstimate(
            flops=4 * rows * keys * QUERY_HEADS * HEAD_SIZE,
            transcendentals=rows * keys * QUERY_HEADS,
            bytes_accessed=4_000_000,
        ),
        name="attend",
    )(query, key, value, query_table, key_table, query_pos, key_pos)


def attend_back_kernel(
    q_ref, k_ref, v_ref, mix_ref, gm_ref, log_ref, qt_ref, kt_ref, qp_ref, kp_ref, gq_ref, gkv_ref
):
    hidden = jnp.where(kp_ref[...] <= qp_ref[...], 0.0, -1e30)
    hidden = jnp.concatenate([hidden] * GROUP, 0)
    rows = q_ref.shape[0]
    for g in range(KEY_VALUE_HEADS):
        key, value = k_ref[:, head_cols(g)], v_ref[:, head_cols(g)]
        each = [head_cols(g * GROUP + i) for i in range(GROUP)]
        query = jnp.concatenate([q_ref[:, cols] for cols in each], 0)
        mixed = jnp.concatenate([mix_ref[:, cols] for cols in each], 0)
        grad_mix = jnp.concatenate([gm_ref[:, cols] for cols in each], 0)
        scores = dot_rows(query, key) + hidden
        probs = jnp.exp(scores - log_ref[:, g : g + 1])
        grad_probs = dot_rows(grad_mix, value)
        delta = jnp.sum(
            grad_mix.astype(jnp.float32) * mixed.astype(jnp.float32), axis=-1, keepdims=True
        )
        grad_scores = (probs * (grad_probs - delta)).astype(jnp.bfloat16)
        grad_query = dot(grad_scores, key) * SCALE
        grad_key = dot_cols(grad_scores, query)
        grad_value = dot_cols(probs.astype(jnp.bfloat16), grad_mix)
        for i in range(GROUP):
            head = turn_back(grad_query[i * rows : (i + 1) * rows], qt_ref[...])
            gq_ref[:, each[i]] = head.astype(jnp.bfloat16)
        gkv_ref[:, head_cols(g)] = turn_back(grad_key, kt_ref[...]).astype(jnp.bfloat16)
        gkv_ref[:, head_cols(KEY_VALUE_HEADS + g)] = grad_value.astype(jnp.bfloat16)


def attend_back(query, key, value, mix, grad_mix, log_total, query_table, key_table, query_pos, key_pos):
    rows, keys = query.shape[0], key.shape[0]
    return pl.pallas_call(
        attend_back_kernel,
        out_shape=(
            jax.ShapeDtypeStruct(query.shape, jnp.bfloat16),
            jax.ShapeDtypeStruct((keys, 2 * key.shape[1]), jnp.bfloat16),
        ),
        compiler_params=pltpu.CompilerParams(vmem_limit_bytes=KERNEL_VMEM),
        cost_estimate=pl.CostEstimate(
            flops=10 * rows * keys * QUERY_HEADS * HEAD_SIZE,
            transcendentals=rows * keys * QUERY_HEADS,
            bytes_accessed=6_000_000,
        ),
        name="attend_back",
    )(query, key, value, mix, grad_mix, log_total, query_table, key_table, query_pos, key_pos)


def body(
    tokens,
    attn_gain,
    w_query,
    key_weight,
    value_weight,
    w_output,
    mlp_gain,
    w_gate,
    w_up,
    w_down,
    cotangent,
):
    _, length, width = tokens.shape
    shards, shard = lax.axis_size("shard"), lax.axis_index("shard")
    context, place = lax.axis_index("context"), lax.axis_index("tensor")
    places = lax.axis_size("tensor")
    rows = 2 * length
    upper = place // 2 == 1
    kv_cols, hidden_cols = key_weight.shape[1], w_gate.shape[1]

    starts = [
        (which * places + (place ^ step)) * length
        for which in (context, 1 - context)
        for step in (0, 2, 1, 3)
    ]
    table = jnp.asarray(rope_tables(length * places * lax.axis_size("context")))
    key_table = jnp.concatenate([lax.dynamic_slice_in_dim(table, at, length, 0) for at in starts], 0)
    key_pos = jnp.concatenate([at + jnp.arange(length, dtype=jnp.int32) for at in starts])
    query_table, query_pos = key_table[:rows], key_pos[:rows, None]
    key_pos = key_pos[None, :]

    mine = jnp.where(upper, tokens[1], tokens[0])
    moved = swap(jnp.where(upper, tokens[0], tokens[1]), "tensor", 2)
    own = jnp.concatenate([to_relative(mine, shards, shard), to_relative(moved, shards, shard)], 0)
    beside = swap(own, "tensor", 1)
    across = swap(own, "context", 1)

    across_beside = swap(after(beside, across), "context", 1)
    all_tokens = jnp.concatenate([own, beside, across, across_beside], 0)

    attn_local = jnp.concatenate([key_weight, value_weight, w_query], 1)
    out_local = w_output.T
    gap = -attn_local.shape[1] % 128
    first_pieces = gather_pieces(
        jnp.concatenate([attn_local, jnp.zeros_like(attn_local[:, :gap]), out_local], 1)
    )
    gains = gather_rows(after(jnp.concatenate([attn_gain[:, None], mlp_gain[:, None]], 1), moved))
    gain_a, gain_m = gains[:, 0], gains[:, 1]
    ends = (2 * kv_cols, attn_local.shape[1], attn_local.shape[1] + gap)
    w_kv = jnp.concatenate([piece[:, : ends[0]] for piece in first_pieces], 0)
    w_q = jnp.concatenate([piece[:, ends[0] : ends[1]] for piece in first_pieces], 0)
    out_weight = jnp.concatenate([piece[:, ends[2] :] for piece in first_pieces], 0)
    mlp_local = jnp.concatenate([w_gate, w_up, w_down.T], 1)

    cots = [after(to_relative(cotangent, shards, shard), beside)]
    cots.append(shift(cots[0], 1))
    cots = [after(cots[0], cots[1]), cots[1], shift(cots[1], 1)]
    cots.append(shift(cots[0], -1))
    all_tokens = after(all_tokens, cots[1])

    all_float = all_tokens.astype(jnp.float32)
    all_scale = rms_scale(all_float)
    all_normed = (all_float * all_scale * gain_a).astype(jnp.bfloat16)
    tokens_f, scale_a, normed_a = all_float[:rows], all_scale[:rows], all_normed[:rows]
    query = dot(normed_a, w_q)
    key_value = dot(all_normed, w_kv)
    key, value = key_value[:, :kv_cols], key_value[:, kv_cols:].astype(jnp.bfloat16)
    mix, log_total, query_rot, key_rot = attend(
        query, key, value, query_table, key_table, query_pos, key_pos
    )
    mlp_pieces = gather_pieces(mlp_local, (query,), mix)
    w_in = jnp.concatenate([piece[:, : 2 * hidden_cols] for piece in mlp_pieces], 0)
    w_dn = jnp.concatenate([piece[:, 2 * hidden_cols :] for piece in mlp_pieces], 0)
    hidden = tokens_f + dot_rows(mix, out_weight)
    scale_m = rms_scale(hidden)
    normed_m = (hidden * scale_m * gain_m).astype(jnp.bfloat16)

    normed_m, cots[2], cots[3] = lax.optimization_barrier((normed_m, cots[2], cots[3]))

    def cot_of(k):
        above = ((place - k) % places) // 2 == 1
        pair = (cots[k], cots[(k + 2) % places])
        return jnp.concatenate([jnp.where(above, one[1], one[0]) for one in pair], 0)

    cots = [cot_of(k) for k in range(places)]
    own_cot = cots[0]
    barrier = lax.optimization_barrier

    group, acts, grads_in, backs = [normed_m], [], [], []
    arriving = shift(normed_m, 1)
    for k, cot in enumerate(cots):
        if k > 0:
            group.append(arriving if k < 3 else after(arriving, grad_nm))
            if k + 1 < places:
                arriving = shift(after(arriving, backs[-1]), 1)
        rows_in = group[k]
        grad_act = dot(cot, w_dn)
        inner = dot(rows_in, w_in)
        gate, up_vals = inner[:, :hidden_cols], inner[:, hidden_cols:]
        sigma = jax.nn.sigmoid(gate)
        acts.append((gate * sigma * up_vals).astype(jnp.bfloat16))
        grad_up = (grad_act * gate * sigma).astype(jnp.bfloat16)
        grad_gate = (grad_act * up_vals * sigma * (1.0 + gate * (1.0 - sigma))).astype(jnp.bfloat16)
        grads_in.append(jnp.concatenate([grad_gate, grad_up], 1))
        backs.append(dot_rows(grads_in[-1], w_in).astype(jnp.bfloat16))
        if k > 0:
            grad_nm = backs[k] if k == 1 else backs[k] + shift(grad_nm, 1)
    bits = bits_of(shards)
    group, grad_in = after(jnp.concatenate(group, 0), grad_nm), jnp.concatenate(grads_in, 0)
    act, cot_group = after(jnp.concatenate(acts, 0), grad_nm), jnp.concatenate(cots, 0)
    mlp_term = jnp.concatenate(
        [dot_cols(group, grad_in).astype(jnp.bfloat16), dot_cols(cot_group, act).astype(jnp.bfloat16)], 1
    )
    mlp_term = scatter_rows(mlp_term, 0, 1)
    half_cols = mlp_term.shape[1] // 2
    first, second = mlp_term[:, :half_cols], mlp_term[:, half_cols:]
    later = context == 1
    mlp_kept, mlp_sent = jnp.where(later, second, first), jnp.where(later, first, second)

    mlp_kept, mlp_sent, last = barrier((mlp_kept, mlp_sent, backs[0]))
    grad_nm = (last + shift(grad_nm, 1)).astype(jnp.float32)
    grad_hidden = own_cot.astype(jnp.float32) + norm_back(grad_nm, hidden, scale_m, gain_m)
    gain_m_term = jnp.sum(grad_nm * (hidden * scale_m), axis=0)
    grad_hidden_low = grad_hidden.astype(jnp.bfloat16)
    grad_mix = dot(grad_hidden_low, out_weight).astype(jnp.bfloat16)
    mlp_half = mlp_kept + swap(mlp_sent, "context", 1)
    out_term = scatter_rows(dot_cols(grad_hidden_low, mix).astype(jnp.bfloat16), 0, bits)
    forward = [dot_rows(act, w_dn).astype(jnp.bfloat16) for act in acts]
    total = shift(after(forward[1], grad_mix), 1)

    grad_query, grad_kv = attend_back(
        query_rot, key_rot, value, mix, grad_mix, log_total, query_table, key_table, query_pos, key_pos
    )
    grad_query, grad_kv, mlp_half, out_term, total = barrier(
        (grad_query, grad_kv, mlp_half, out_term, total)
    )
    out_total = lax.psum(out_term, ("context", "tensor")).astype(jnp.float32).T
    attn_term = jnp.concatenate(
        [
            dot_cols(all_normed, grad_kv).astype(jnp.bfloat16),
            dot_cols(normed_a, grad_query).astype(jnp.bfloat16),
            gain_m_term.astype(jnp.bfloat16)[:, None],
        ],
        1,
    )
    attn_term = scatter_rows(attn_term, 0, bits)
    pair = grad_kv[: 2 * rows] + swap(grad_kv[2 * rows :], "context", 1)
    total = shift(forward[2] + total, 1)
    attn_term, pair, total, mlp_half = barrier((attn_term, pair, total, mlp_half))

    attn_part = group_sum_parts(attn_term)
    own_kv = pair[:rows] + swap(pair[rows:], "tensor", 1)
    grad_na = dot_rows(grad_query, w_q) + dot_rows(own_kv, w_kv)
    grad_tokens = grad_hidden + norm_back(grad_na, tokens_f, scale_a, gain_a)
    grad_tokens = from_relative(grad_tokens.astype(jnp.bfloat16), shards, shard)
    total = shift(forward[3] + total, 1)
    block = hidden + forward[0].astype(jnp.float32) + total.astype(jnp.float32)
    block = from_relative(block.astype(jnp.bfloat16), shards, shard)
    mlp_half = scatter_rows(mlp_half, 1, bits)
    attn_part, grad_tokens, block, mlp_half = barrier((attn_part, grad_tokens, block, mlp_half))

    back_rows = swap(jnp.concatenate([block[length:], grad_tokens[length:]], 0), "tensor", 2)
    block_out = both_sequences(block[:length], back_rows[:length], upper)
    tokens_grad = both_sequences(grad_tokens[:length], back_rows[length:], upper)
    attn_total = group_collect(attn_part, attn_term.shape[0]).astype(jnp.float32)
    attn_total, gain_m_total = attn_total[:, :-1], attn_total[:, -1]
    gain_a_total = jnp.sum(attn_local.astype(jnp.float32) * attn_total, axis=1) / attn_gain

    mlp_other = swap(mlp_half, "context", 1)
    mlp_total = jnp.concatenate(
        [jnp.where(later, mlp_other, mlp_half), jnp.where(later, mlp_half, mlp_other)], 1
    ).astype(jnp.float32)
    gate_total = mlp_total[:, :hidden_cols]
    up_total = mlp_total[:, hidden_cols : 2 * hidden_cols]
    down_total = mlp_total[:, 2 * hidden_cols :].T
    return (
        block_out,
        tokens_grad,
        gain_a_total,
        attn_total[:, 2 * kv_cols :],
        attn_total[:, :kv_cols],
        attn_total[:, kv_cols : 2 * kv_cols],
        out_total,
        gain_m_total,
        gate_total,
        up_total,
        down_total,
    )


def solution(mesh):
    specs = (
        P("shard", ("context", "tensor"), None),
        P("shard"),
        P("shard", None),
        P("shard", None),
        P("shard", None),
        P(None, "shard"),
        P("shard"),
        P("shard", "tensor"),
        P("shard", "tensor"),
        P("tensor", "shard"),
    )
    return jax.shard_map(
        body,
        mesh=mesh,
        in_specs=specs + specs[:1],
        out_specs=specs[:1] + specs,
        check_vma=False,
    )
```

```python
import jax
import jax.numpy as jnp
import numpy as np
from jax import lax
from jax.experimental import pallas as pl
from jax.experimental.pallas import tpu as pltpu
from jax.sharding import PartitionSpec as P

QUERY_HEADS = 15
KEY_VALUE_HEADS = 5
HEAD_SIZE = 64
GROUP = QUERY_HEADS // KEY_VALUE_HEADS
SCALE = HEAD_SIZE ** (-0.5)
EPS = 1e-05
KERNEL_VMEM = 40 * 1024 * 1024


def dot(left, right):
    return jnp.dot(left, right, preferred_element_type=jnp.float32)


def dot_rows(left, right):
    return lax.dot_general(
        left, right, (((1,), (1,)), ((), ())), preferred_element_type=jnp.float32
    )


def dot_cols(left, right):
    return lax.dot_general(
        left, right, (((0,), (0,)), ((), ())), preferred_element_type=jnp.float32
    )


def rms_scale(rows):
    return lax.rsqrt(jnp.mean(rows * rows, axis=-1, keepdims=True) + EPS)


def norm_back(grad_norm, rows, scale_rows, gain):
    normed = rows * scale_rows
    scaled = grad_norm * gain
    return scale_rows * (scaled - normed * jnp.mean(scaled * normed, axis=-1, keepdims=True))


def after(value, *others):
    return lax.optimization_barrier((value, *others))[0]


def bits_of(count):
    return count.bit_length() - 1


def flip_blocks(rows, shards, index):
    width = rows.shape[-1] // shards
    bits = bits_of(shards)
    for place in range(bits):
        step = width << place
        pieces = [rows[..., i * step : (i + 1) * step] for i in range(rows.shape[-1] // step)]
        swapped = jnp.concatenate([pieces[i ^ 1] for i in range(len(pieces))], -1)
        rows = jnp.where((index >> (bits - 1 - place)) & 1 == 1, swapped, rows)
    return rows


def reverse_blocks(rows, shards):
    width = rows.shape[-1] // shards
    bits = bits_of(shards)
    order = [int(format(i, f"0{bits}b")[::-1], 2) for i in range(shards)]
    return jnp.concatenate([rows[..., i * width : (i + 1) * width] for i in order], -1)


def to_relative(rows, shards, index):
    return flip_blocks(reverse_blocks(rows, shards), shards, index)


def from_relative(rows, shards, index):
    return reverse_blocks(flip_blocks(rows, shards, index), shards)


def swap(value, axis, bit):
    size = lax.axis_size(axis)
    return lax.ppermute(value, axis, [(i, i ^ bit) for i in range(size)])


def gather_pieces(rows, gate=None, later=None):
    pieces = [rows]
    for place in reversed(range(bits_of(lax.axis_size("shard")))):
        if len(pieces) > 2:
            pieces = [jnp.concatenate(pieces, 0)]
        sent = pieces
        if gate is not None:
            sent = [after(piece, *gate) for piece in pieces]
            gate = None
        elif later is not None:
            sent = pieces[:1] + [after(piece, later) for piece in pieces[1:]]
        pieces = pieces + [swap(piece, "shard", 1 << place) for piece in sent]
    return pieces


def gather_rows(rows):
    return jnp.concatenate(gather_pieces(rows), 0)


def scatter_rows(rows, first, last):
    for place in range(first, last):
        half = rows.shape[0] // 2
        rows = rows[:half] + swap(rows[half:], "shard", 1 << place)
    return rows


def shift(value, count):
    size = lax.axis_size("tensor")
    return lax.ppermute(value, "tensor", [(i, (i + count) % size) for i in range(size)])


def both_sequences(mine, other, upper):
    return jnp.stack([jnp.where(upper, other, mine), jnp.where(upper, mine, other)])


def group_sum_parts(rows):
    axes = ("context", "tensor")
    group = lax.axis_size(axes)
    count = rows.shape[0]
    chunk = -(-count // group)
    if chunk > 16:
        chunk = -(-chunk // 16) * 16
    padded = jnp.pad(rows, ((0, chunk * group - count), (0, 0)))
    parts = lax.all_to_all(padded, axes, split_axis=0, concat_axis=0, tiled=True)
    parts = parts.reshape(group, chunk, rows.shape[1]).astype(jnp.float32)
    return jnp.sum(parts, axis=0).astype(jnp.bfloat16)


def group_collect(part, count):
    axes = ("context", "tensor")
    group = lax.axis_size(axes)
    spread = jnp.broadcast_to(part[None], (group,) + part.shape)
    spread = spread.reshape(group * part.shape[0], part.shape[1])
    return lax.all_to_all(spread, axes, split_axis=0, concat_axis=0, tiled=True)[:count]


def rope_tables(length):
    half = HEAD_SIZE // 2
    freq = np.float32(10000.0) ** (-np.arange(half).astype(np.float32) * 2.0 / HEAD_SIZE)
    angle = np.arange(length).astype(np.float32)[:, None] * freq.astype(np.float32)[None, :]
    cosine, sine = np.cos(angle), np.sin(angle)
    return np.concatenate([cosine, cosine, -sine, sine], 1).astype(np.float32)


def turn(head, table):
    half = HEAD_SIZE // 2
    swapped = jnp.concatenate([head[:, half:], head[:, :half]], 1)
    return head * table[:, :HEAD_SIZE] + swapped * table[:, HEAD_SIZE:]


def turn_back(head, table):
    half = HEAD_SIZE // 2
    swapped = jnp.concatenate([head[:, half:], head[:, :half]], 1)
    return head * table[:, :HEAD_SIZE] - swapped * table[:, HEAD_SIZE:]


def head_cols(index):
    return slice(index * HEAD_SIZE, (index + 1) * HEAD_SIZE)


def attend_kernel(q_ref, k_ref, v_ref, qt_ref, kt_ref, qp_ref, kp_ref, mix_ref, log_ref, qr_ref, kr_ref):
    hidden = jnp.where(kp_ref[...] <= qp_ref[...], 0.0, -1e30)
    hidden = jnp.concatenate([hidden] * GROUP, 0)
    rows = q_ref.shape[0]
    for g in range(KEY_VALUE_HEADS):
        key = turn(k_ref[:, head_cols(g)], kt_ref[...]).astype(jnp.bfloat16)
        kr_ref[:, head_cols(g)] = key
        value = v_ref[:, head_cols(g)]
        heads = []
        for i in range(GROUP):
            cols = head_cols(g * GROUP + i)
            head = turn(q_ref[:, cols], qt_ref[...]).astype(jnp.bfloat16) * SCALE
            qr_ref[:, cols] = head
            heads.append(head)
        query = jnp.concatenate(heads, 0)
        scores = dot_rows(query, key) + hidden
        peak = jnp.max(scores, axis=-1, keepdims=True)
        expd = jnp.exp(scores - peak)
        total = jnp.sum(expd, axis=-1, keepdims=True)
        mixed = (dot(expd.astype(jnp.bfloat16), value) / total).astype(jnp.bfloat16)
        for i in range(GROUP):
            mix_ref[:, head_cols(g * GROUP + i)] = mixed[i * rows : (i + 1) * rows]
        log_ref[:, g : g + 1] = peak + jnp.log(total)


def attend(query, key, value, query_table, key_table, query_pos, key_pos):
    rows, keys = query.shape[0], key.shape[0]
    return pl.pallas_call(
        attend_kernel,
        out_shape=(
            jax.ShapeDtypeStruct(query.shape, jnp.bfloat16),
            jax.ShapeDtypeStruct((GROUP * rows, 8), jnp.float32),
            jax.ShapeDtypeStruct(query.shape, jnp.bfloat16),
            jax.ShapeDtypeStruct(key.shape, jnp.bfloat16),
        ),
        compiler_params=pltpu.CompilerParams(vmem_limit_bytes=KERNEL_VMEM),
        cost_estimate=pl.CostEstimate(
            flops=4 * rows * keys * QUERY_HEADS * HEAD_SIZE,
            transcendentals=rows * keys * QUERY_HEADS,
            bytes_accessed=4_000_000,
        ),
        name="attend",
    )(query, key, value, query_table, key_table, query_pos, key_pos)


def attend_back_kernel(
    q_ref, k_ref, v_ref, mix_ref, gm_ref, log_ref, qt_ref, kt_ref, qp_ref, kp_ref, grad_ref
):
    hidden = jnp.where(kp_ref[...] <= qp_ref[...], 0.0, -1e30)
    hidden = jnp.concatenate([hidden] * GROUP, 0)
    rows, keys = q_ref.shape[0], k_ref.shape[0]
    kv_cols = 2 * k_ref.shape[1]
    grad_ref[rows:, kv_cols:] = jnp.zeros((keys - rows, grad_ref.shape[1] - kv_cols), jnp.bfloat16)
    used = kv_cols + q_ref.shape[1]
    if used < grad_ref.shape[1]:
        grad_ref[:rows, used:] = jnp.zeros((rows, grad_ref.shape[1] - used), jnp.bfloat16)
    for g in range(KEY_VALUE_HEADS):
        key, value = k_ref[:, head_cols(g)], v_ref[:, head_cols(g)]
        each = [head_cols(g * GROUP + i) for i in range(GROUP)]
        query = jnp.concatenate([q_ref[:, cols] for cols in each], 0)
        mixed = jnp.concatenate([mix_ref[:, cols] for cols in each], 0)
        grad_mix = jnp.concatenate([gm_ref[:, cols] for cols in each], 0)
        scores = dot_rows(query, key) + hidden
        probs = jnp.exp(scores - log_ref[:, g : g + 1])
        grad_probs = dot_rows(grad_mix, value)
        delta = jnp.sum(
            grad_mix.astype(jnp.float32) * mixed.astype(jnp.float32), axis=-1, keepdims=True
        )
        grad_scores = (probs * (grad_probs - delta)).astype(jnp.bfloat16)
        grad_query = dot(grad_scores, key) * SCALE
        grad_key = dot_cols(grad_scores, query)
        grad_value = dot_cols(probs.astype(jnp.bfloat16), grad_mix)
        for i in range(GROUP):
            head = turn_back(grad_query[i * rows : (i + 1) * rows], qt_ref[...])
            grad_ref[:rows, head_cols(2 * KEY_VALUE_HEADS + g * GROUP + i)] = head.astype(jnp.bfloat16)
        grad_ref[:, head_cols(g)] = turn_back(grad_key, kt_ref[...]).astype(jnp.bfloat16)
        grad_ref[:, head_cols(KEY_VALUE_HEADS + g)] = grad_value.astype(jnp.bfloat16)


def attend_back(query, key, value, mix, grad_mix, log_total, query_table, key_table, query_pos, key_pos):
    rows, keys = query.shape[0], key.shape[0]
    used = 2 * key.shape[1] + query.shape[1]
    return pl.pallas_call(
        attend_back_kernel,
        out_shape=jax.ShapeDtypeStruct((keys, used + -used % 128), jnp.bfloat16),
        compiler_params=pltpu.CompilerParams(vmem_limit_bytes=KERNEL_VMEM),
        cost_estimate=pl.CostEstimate(
            flops=10 * rows * keys * QUERY_HEADS * HEAD_SIZE,
            transcendentals=rows * keys * QUERY_HEADS,
            bytes_accessed=6_000_000,
        ),
        name="attend_back",
    )(query, key, value, mix, grad_mix, log_total, query_table, key_table, query_pos, key_pos)


def body(
    tokens,
    attn_gain,
    w_query,
    key_weight,
    value_weight,
    w_output,
    mlp_gain,
    w_gate,
    w_up,
    w_down,
    cotangent,
):
    _, length, width = tokens.shape
    shards, shard = lax.axis_size("shard"), lax.axis_index("shard")
    context, place = lax.axis_index("context"), lax.axis_index("tensor")
    places = lax.axis_size("tensor")
    rows = 2 * length
    upper = place // 2 == 1
    kv_cols, hidden_cols = key_weight.shape[1], w_gate.shape[1]

    starts = [
        (which * places + (place ^ step)) * length
        for which in (context, 1 - context)
        for step in (0, 2, 1, 3)
    ]
    table = jnp.asarray(rope_tables(length * places * lax.axis_size("context")))
    key_table = jnp.concatenate([lax.dynamic_slice_in_dim(table, at, length, 0) for at in starts], 0)
    key_pos = jnp.concatenate([at + jnp.arange(length, dtype=jnp.int32) for at in starts])
    query_table, query_pos = key_table[:rows], key_pos[:rows, None]
    key_pos = key_pos[None, :]

    gains = gather_rows(jnp.concatenate([attn_gain[:, None], mlp_gain[:, None]], 1))
    gain_a, gain_m = gains[:, 0], gains[:, 1]

    mine = jnp.where(upper, tokens[1], tokens[0])
    moved = swap(jnp.where(upper, tokens[0], tokens[1]), "tensor", 2)
    own = jnp.concatenate([to_relative(mine, shards, shard), to_relative(moved, shards, shard)], 0)
    beside = swap(own, "tensor", 1)
    across = swap(own, "context", 1)

    across_beside = swap(after(beside, across), "context", 1)
    all_tokens = jnp.concatenate([own, beside, across, across_beside], 0)

    attn_local = jnp.concatenate([key_weight, value_weight, w_query], 1)
    out_local = w_output.T
    gap = -attn_local.shape[1] % 128
    first_pieces = gather_pieces(
        jnp.concatenate([attn_local, jnp.zeros_like(attn_local[:, :gap]), out_local], 1)
    )
    ends = (2 * kv_cols, attn_local.shape[1], attn_local.shape[1] + gap)
    w_kv = jnp.concatenate([piece[:, : ends[0]] for piece in first_pieces], 0)
    w_q = jnp.concatenate([piece[:, ends[0] : ends[1]] for piece in first_pieces], 0)
    out_weight = jnp.concatenate([piece[:, ends[2] :] for piece in first_pieces], 0)
    mlp_local = jnp.concatenate([w_gate, w_up, w_down.T], 1)

    cots = [after(to_relative(cotangent, shards, shard), beside)]
    cots.append(shift(cots[0], 1))
    cots = [after(cots[0], cots[1]), cots[1], shift(cots[1], 1)]
    cots.append(shift(cots[0], -1))
    all_tokens = after(all_tokens, cots[1])

    all_float = all_tokens.astype(jnp.float32)
    all_scale = rms_scale(all_float)
    all_normed = (all_float * all_scale * gain_a).astype(jnp.bfloat16)
    tokens_f, scale_a, normed_a = all_float[:rows], all_scale[:rows], all_normed[:rows]
    query = dot(normed_a, w_q)
    key_value = dot(all_normed, w_kv)
    key, value = key_value[:, :kv_cols], key_value[:, kv_cols:].astype(jnp.bfloat16)
    mix, log_total, query_rot, key_rot = attend(
        query, key, value, query_table, key_table, query_pos, key_pos
    )
    mlp_pieces = gather_pieces(mlp_local, (query,), mix)
    w_in = jnp.concatenate([piece[:, : 2 * hidden_cols] for piece in mlp_pieces], 0)
    w_dn = jnp.concatenate([piece[:, 2 * hidden_cols :] for piece in mlp_pieces], 0)
    hidden = tokens_f + dot_rows(mix, out_weight)
    scale_m = rms_scale(hidden)
    normed_m = (hidden * scale_m * gain_m).astype(jnp.bfloat16)

    normed_m, cots[2], cots[3] = lax.optimization_barrier((normed_m, cots[2], cots[3]))

    def cot_of(k):
        above = ((place - k) % places) // 2 == 1
        pair = (cots[k], cots[(k + 2) % places])
        return jnp.concatenate([jnp.where(above, one[1], one[0]) for one in pair], 0)

    cots = [cot_of(k) for k in range(places)]
    own_cot = cots[0]
    barrier = lax.optimization_barrier

    group, acts, grads_in, backs = [normed_m], [], [], []
    arriving = shift(normed_m, 1)
    for k, cot in enumerate(cots):
        if k > 0:
            group.append(arriving if k < 3 else after(arriving, grad_nm))
            if k + 1 < places:
                arriving = shift(after(arriving, backs[-1]), 1)
        rows_in = group[k]
        grad_act = dot(cot, w_dn)
        inner = dot(rows_in, w_in)
        gate, up_vals = inner[:, :hidden_cols], inner[:, hidden_cols:]
        sigma = jax.nn.sigmoid(gate)
        acts.append((gate * sigma * up_vals).astype(jnp.bfloat16))
        grad_up = (grad_act * gate * sigma).astype(jnp.bfloat16)
        grad_gate = (grad_act * up_vals * sigma * (1.0 + gate * (1.0 - sigma))).astype(jnp.bfloat16)
        grads_in.append(jnp.concatenate([grad_gate, grad_up], 1))
        backs.append(dot_rows(grads_in[-1], w_in).astype(jnp.bfloat16))
        if k > 0:
            grad_nm = backs[k] if k == 1 else backs[k] + shift(grad_nm, 1)
    bits = bits_of(shards)
    *held, _ = barrier((*grads_in, *acts, grad_nm))
    group, cot_group = jnp.concatenate(group, 0), jnp.concatenate(cots, 0)
    grad_in, act = jnp.concatenate(held[:places], 0), jnp.concatenate(held[places:], 0)
    mlp_term = jnp.concatenate(
        [dot_cols(group, grad_in).astype(jnp.bfloat16), dot_cols(cot_group, act).astype(jnp.bfloat16)], 1
    )
    mlp_term = scatter_rows(mlp_term, 0, 1)
    half_cols = mlp_term.shape[1] // 2
    first, second = mlp_term[:, :half_cols], mlp_term[:, half_cols:]
    later = context == 1
    mlp_kept, mlp_sent = jnp.where(later, second, first), jnp.where(later, first, second)

    grad_nm = (backs[0] + shift(grad_nm, 1)).astype(jnp.float32)
    grad_hidden = own_cot.astype(jnp.float32) + norm_back(grad_nm, hidden, scale_m, gain_m)
    gain_m_term = jnp.sum(grad_nm * (hidden * scale_m), axis=0)
    grad_hidden_low = grad_hidden.astype(jnp.bfloat16)
    grad_mix = dot(grad_hidden_low, out_weight).astype(jnp.bfloat16)
    out_term = scatter_rows(dot_cols(grad_hidden_low, mix).astype(jnp.bfloat16), 0, bits)
    forward = [dot_rows(act, w_dn).astype(jnp.bfloat16) for act in acts]
    total = shift(after(forward[1], grad_mix), 1)

    grads = attend_back(
        query_rot, key_rot, value, mix, grad_mix, log_total, query_table, key_table, query_pos, key_pos
    )
    grads, out_term, total, mlp_kept, mlp_sent = barrier((grads, out_term, total, mlp_kept, mlp_sent))

    attn_cols = attn_local.shape[1]
    spot = (jnp.arange(grads.shape[1]) == attn_cols).astype(jnp.float32)
    attn_term = dot_cols(all_normed, grads) + gain_m_term[:, None] * spot[None, :]
    attn_term = scatter_rows(attn_term.astype(jnp.bfloat16), 0, 1)
    mlp_sent = after(mlp_sent, attn_term)
    attn_term = scatter_rows(attn_term, 1, bits)
    grad_query, grad_kv = grads[:rows, 2 * kv_cols : attn_cols], grads[:, : 2 * kv_cols]
    pair = grad_kv[: 2 * rows] + swap(grad_kv[2 * rows :], "context", 1)
    own_kv = pair[:rows] + swap(pair[rows:], "tensor", 1)
    out_part = group_sum_parts(out_term)
    total = shift(forward[2] + total, 1)
    total = shift(forward[3] + total, 1)
    attn_term, own_kv, out_part, total = barrier((attn_term, own_kv, out_part, total))

    attn_part = group_sum_parts(attn_term)
    mlp_half = mlp_kept + swap(mlp_sent, "context", 1)
    own_kv, grad_query, mlp_half = barrier((own_kv, grad_query, mlp_half))
    mlp_half = scatter_rows(mlp_half, 1, bits)
    block = hidden + forward[0].astype(jnp.float32) + total.astype(jnp.float32)
    block = from_relative(block.astype(jnp.bfloat16), shards, shard)
    grad_na = dot_rows(grad_query, w_q) + dot_rows(own_kv, w_kv)
    grad_tokens = grad_hidden + norm_back(grad_na, tokens_f, scale_a, gain_a)
    grad_tokens = from_relative(grad_tokens.astype(jnp.bfloat16), shards, shard)
    attn_part, mlp_half, block, grad_tokens = barrier((attn_part, mlp_half, block, grad_tokens))

    parts = group_collect(jnp.concatenate([attn_part, out_part], 1), attn_term.shape[0])
    back_rows = swap(jnp.concatenate([block[length:], grad_tokens[length:]], 0), "tensor", 2)
    block_out = both_sequences(block[:length], back_rows[:length], upper)
    tokens_grad = both_sequences(grad_tokens[:length], back_rows[length:], upper)
    mlp_other = swap(mlp_half, "context", 1)
    mlp_total = jnp.concatenate(
        [jnp.where(later, mlp_other, mlp_half), jnp.where(later, mlp_half, mlp_other)], 1
    ).astype(jnp.float32)
    gate_total = mlp_total[:, :hidden_cols]
    up_total = mlp_total[:, hidden_cols : 2 * hidden_cols]
    down_total = mlp_total[:, 2 * hidden_cols :].T
    parts = parts.astype(jnp.float32)
    attn_total, gain_m_total = parts[:, :attn_cols], parts[:, attn_cols]
    out_total = parts[:, attn_part.shape[1] :].T
    gain_a_total = jnp.sum(attn_local.astype(jnp.float32) * attn_total, axis=1) / attn_gain
    return (
        block_out,
        tokens_grad,
        gain_a_total,
        attn_total[:, 2 * kv_cols :],
        attn_total[:, :kv_cols],
        attn_total[:, kv_cols : 2 * kv_cols],
        out_total,
        gain_m_total,
        gate_total,
        up_total,
        down_total,
    )


def solution(mesh):
    specs = (
        P("shard", ("context", "tensor"), None),
        P("shard"),
        P("shard", None),
        P("shard", None),
        P("shard", None),
        P(None, "shard"),
        P("shard"),
        P("shard", "tensor"),
        P("shard", "tensor"),
        P("tensor", "shard"),
    )
    return jax.shard_map(
        body,
        mesh=mesh,
        in_specs=specs + specs[:1],
        out_specs=specs[:1] + specs,
        check_vma=False,
    )
```

```python
import functools

import jax
import jax.numpy as jnp
import numpy as np
from jax import lax
from jax.experimental import pallas as pl
from jax.experimental.pallas import tpu as pltpu
from jax.sharding import PartitionSpec as P

QUERY_HEADS = 15
KEY_VALUE_HEADS = 5
HEAD_SIZE = 64
GROUP = QUERY_HEADS // KEY_VALUE_HEADS
SCALE = HEAD_SIZE ** (-0.5)
EPS = 1e-05
KERNEL_VMEM = 40 * 1024 * 1024


def dot(left, right):
    return jnp.dot(left, right, preferred_element_type=jnp.float32)


def dot_rows(left, right):
    return lax.dot_general(
        left, right, (((1,), (1,)), ((), ())), preferred_element_type=jnp.float32
    )


def dot_cols(left, right):
    return lax.dot_general(
        left, right, (((0,), (0,)), ((), ())), preferred_element_type=jnp.float32
    )


def rms_scale(rows):
    return lax.rsqrt(jnp.mean(rows * rows, axis=-1, keepdims=True) + EPS)


def norm_back(scaled, rows, scale_rows):
    normed = rows * scale_rows
    return scale_rows * (scaled - normed * jnp.mean(scaled * normed, axis=-1, keepdims=True))


def after(value, *others):
    return lax.optimization_barrier((value, *others))[0]


def bits_of(count):
    return count.bit_length() - 1


def flip_blocks(rows, shards, index):
    width = rows.shape[-1] // shards
    bits = bits_of(shards)
    for place in range(bits):
        step = width << place
        pieces = [rows[..., i * step : (i + 1) * step] for i in range(rows.shape[-1] // step)]
        swapped = jnp.concatenate([pieces[i ^ 1] for i in range(len(pieces))], -1)
        rows = jnp.where((index >> (bits - 1 - place)) & 1 == 1, swapped, rows)
    return rows


def reverse_blocks(rows, shards):
    width = rows.shape[-1] // shards
    bits = bits_of(shards)
    order = [int(format(i, f"0{bits}b")[::-1], 2) for i in range(shards)]
    return jnp.concatenate([rows[..., i * width : (i + 1) * width] for i in order], -1)


def to_relative(rows, shards, index):
    return flip_blocks(reverse_blocks(rows, shards), shards, index)


def from_relative(rows, shards, index):
    return reverse_blocks(flip_blocks(rows, shards, index), shards)


def swap(value, axis, bit):
    size = lax.axis_size(axis)
    return lax.ppermute(value, axis, [(i, i ^ bit) for i in range(size)])


def gather_pieces(rows, gate, later=None):
    pieces = [rows]
    for place in reversed(range(bits_of(lax.axis_size("shard")))):
        if len(pieces) > 2:
            pieces = [jnp.concatenate(pieces, 0)]
        sent = pieces
        if gate is not None:
            sent = [after(rows, gate)]
            gate = None
        elif later is not None:
            sent = pieces[:1] + [after(piece, later) for piece in pieces[1:]]
        pieces = pieces + [swap(piece, "shard", 1 << place) for piece in sent]
    return pieces


def scatter_rows(rows, first, last):
    for place in range(first, last):
        half = rows.shape[0] // 2
        rows = rows[:half] + swap(rows[half:], "shard", 1 << place)
    return rows


def shift(value, count):
    size = lax.axis_size("tensor")
    return lax.ppermute(value, "tensor", [(i, (i + count) % size) for i in range(size)])


def both_sequences(mine, other, upper):
    return jnp.stack([jnp.where(upper, other, mine), jnp.where(upper, mine, other)])


def group_sum_parts(rows):
    axes = ("context", "tensor")
    group = lax.axis_size(axes)
    count = rows.shape[0]
    chunk = -(-count // group)
    if chunk > 16:
        chunk = -(-chunk // 16) * 16
    padded = jnp.pad(rows, ((0, chunk * group - count), (0, 0)))
    parts = lax.all_to_all(padded, axes, split_axis=0, concat_axis=0, tiled=True)
    parts = parts.reshape(group, chunk, rows.shape[1]).astype(jnp.float32)
    return jnp.sum(parts, axis=0).astype(jnp.bfloat16)


def group_collect(part):
    axes = ("context", "tensor")
    group = lax.axis_size(axes)
    spread = jnp.broadcast_to(part[None], (group,) + part.shape)
    spread = spread.reshape(group * part.shape[0], part.shape[1])
    return lax.all_to_all(spread, axes, split_axis=0, concat_axis=0, tiled=True)


def unpack_kernel(kv_cols, attn_cols, parts_ref, gain_ref, query_ref, key_ref, value_ref, out_ref):
    rows = query_ref.shape[0]
    gain = gain_ref[...]
    query_ref[...] = parts_ref[:rows, 2 * kv_cols : attn_cols].astype(jnp.float32) * gain
    key_ref[...] = (parts_ref[:rows, :kv_cols].astype(jnp.float32) * gain).T
    value_ref[...] = (parts_ref[:rows, kv_cols : 2 * kv_cols].astype(jnp.float32) * gain).T
    out_ref[...] = parts_ref[:rows, parts_ref.shape[1] - out_ref.shape[0] :].astype(jnp.float32).T


def unpack(parts, gain, kv_cols, attn_cols):
    rows, out_cols = gain.shape[0], parts.shape[1] - attn_cols - -attn_cols % 128
    shapes = ((rows, attn_cols - 2 * kv_cols), (kv_cols, rows), (kv_cols, rows), (out_cols, rows))
    return pl.pallas_call(
        functools.partial(unpack_kernel, kv_cols, attn_cols),
        out_shape=tuple(jax.ShapeDtypeStruct(shape, jnp.float32) for shape in shapes),
        compiler_params=pltpu.CompilerParams(vmem_limit_bytes=KERNEL_VMEM),
        cost_estimate=pl.CostEstimate(flops=0, transcendentals=0, bytes_accessed=4_000_000),
        name="unpack",
    )(parts, gain)


def rope_tables(length):
    half = HEAD_SIZE // 2
    freq = np.float32(10000.0) ** (-np.arange(half).astype(np.float32) * 2.0 / HEAD_SIZE)
    angle = np.arange(length).astype(np.float32)[:, None] * freq.astype(np.float32)[None, :]
    cosine, sine = np.cos(angle), np.sin(angle)
    return np.concatenate([cosine, cosine, -sine, sine], 1).astype(np.float32)


def turn(head, table):
    half = HEAD_SIZE // 2
    swapped = jnp.concatenate([head[:, half:], head[:, :half]], 1)
    return head * table[:, :HEAD_SIZE] + swapped * table[:, HEAD_SIZE:]


def turn_back(head, table):
    half = HEAD_SIZE // 2
    swapped = jnp.concatenate([head[:, half:], head[:, :half]], 1)
    return head * table[:, :HEAD_SIZE] - swapped * table[:, HEAD_SIZE:]


def head_cols(index):
    return slice(index * HEAD_SIZE, (index + 1) * HEAD_SIZE)


def attend_kernel(q_ref, k_ref, v_ref, qt_ref, kt_ref, qp_ref, kp_ref, mix_ref, log_ref, qr_ref, kr_ref):
    hidden = jnp.where(kp_ref[...] <= qp_ref[...], 0.0, -1e30)
    hidden = jnp.concatenate([hidden] * GROUP, 0)
    rows = q_ref.shape[0]
    for g in range(KEY_VALUE_HEADS):
        key = turn(k_ref[:, head_cols(g)], kt_ref[...]).astype(jnp.bfloat16)
        kr_ref[:, head_cols(g)] = key
        value = v_ref[:, head_cols(g)]
        heads = []
        for i in range(GROUP):
            cols = head_cols(g * GROUP + i)
            head = turn(q_ref[:, cols], qt_ref[...]).astype(jnp.bfloat16) * SCALE
            qr_ref[:, cols] = head
            heads.append(head)
        query = jnp.concatenate(heads, 0)
        scores = dot_rows(query, key) + hidden
        peak = jnp.max(scores, axis=-1, keepdims=True)
        expd = jnp.exp(scores - peak)
        total = jnp.sum(expd, axis=-1, keepdims=True)
        mixed = (dot(expd.astype(jnp.bfloat16), value) / total).astype(jnp.bfloat16)
        for i in range(GROUP):
            mix_ref[:, head_cols(g * GROUP + i)] = mixed[i * rows : (i + 1) * rows]
        log_ref[:, g : g + 1] = peak + jnp.log(total)


def attend(query, key, value, query_table, key_table, query_pos, key_pos):
    rows, keys = query.shape[0], key.shape[0]
    return pl.pallas_call(
        attend_kernel,
        out_shape=(
            jax.ShapeDtypeStruct(query.shape, jnp.bfloat16),
            jax.ShapeDtypeStruct((GROUP * rows, 8), jnp.float32),
            jax.ShapeDtypeStruct(query.shape, jnp.bfloat16),
            jax.ShapeDtypeStruct(key.shape, jnp.bfloat16),
        ),
        compiler_params=pltpu.CompilerParams(vmem_limit_bytes=KERNEL_VMEM),
        cost_estimate=pl.CostEstimate(
            flops=4 * rows * keys * QUERY_HEADS * HEAD_SIZE,
            transcendentals=rows * keys * QUERY_HEADS,
            bytes_accessed=4_000_000,
        ),
        name="attend",
    )(query, key, value, query_table, key_table, query_pos, key_pos)


def attend_back_kernel(
    q_ref, k_ref, v_ref, mix_ref, gm_ref, log_ref, qt_ref, kt_ref, qp_ref, kp_ref, grad_ref
):
    hidden = jnp.where(kp_ref[...] <= qp_ref[...], 0.0, -1e30)
    hidden = jnp.concatenate([hidden] * GROUP, 0)
    rows, keys = q_ref.shape[0], k_ref.shape[0]
    kv_cols = 2 * k_ref.shape[1]
    grad_ref[rows:, kv_cols:] = jnp.zeros((keys - rows, grad_ref.shape[1] - kv_cols), jnp.bfloat16)
    used = kv_cols + q_ref.shape[1]
    if used < grad_ref.shape[1]:
        grad_ref[:rows, used:] = jnp.zeros((rows, grad_ref.shape[1] - used), jnp.bfloat16)
    for g in range(KEY_VALUE_HEADS):
        key, value = k_ref[:, head_cols(g)], v_ref[:, head_cols(g)]
        each = [head_cols(g * GROUP + i) for i in range(GROUP)]
        query = jnp.concatenate([q_ref[:, cols] for cols in each], 0)
        mixed = jnp.concatenate([mix_ref[:, cols] for cols in each], 0)
        grad_mix = jnp.concatenate([gm_ref[:, cols] for cols in each], 0)
        scores = dot_rows(query, key) + hidden
        probs = jnp.exp(scores - log_ref[:, g : g + 1])
        grad_probs = dot_rows(grad_mix, value)
        delta = jnp.sum(
            grad_mix.astype(jnp.float32) * mixed.astype(jnp.float32), axis=-1, keepdims=True
        )
        grad_scores = (probs * (grad_probs - delta)).astype(jnp.bfloat16)
        grad_query = dot(grad_scores, key) * SCALE
        grad_key = dot_cols(grad_scores, query)
        grad_value = dot_cols(probs.astype(jnp.bfloat16), grad_mix)
        for i in range(GROUP):
            head = turn_back(grad_query[i * rows : (i + 1) * rows], qt_ref[...])
            grad_ref[:rows, head_cols(2 * KEY_VALUE_HEADS + g * GROUP + i)] = head.astype(jnp.bfloat16)
        grad_ref[:, head_cols(g)] = turn_back(grad_key, kt_ref[...]).astype(jnp.bfloat16)
        grad_ref[:, head_cols(KEY_VALUE_HEADS + g)] = grad_value.astype(jnp.bfloat16)


def attend_back(query, key, value, mix, grad_mix, log_total, query_table, key_table, query_pos, key_pos):
    rows, keys = query.shape[0], key.shape[0]
    used = 2 * key.shape[1] + query.shape[1]
    return pl.pallas_call(
        attend_back_kernel,
        out_shape=jax.ShapeDtypeStruct((keys, used + -used % 128), jnp.bfloat16),
        compiler_params=pltpu.CompilerParams(vmem_limit_bytes=KERNEL_VMEM),
        cost_estimate=pl.CostEstimate(
            flops=10 * rows * keys * QUERY_HEADS * HEAD_SIZE,
            transcendentals=rows * keys * QUERY_HEADS,
            bytes_accessed=6_000_000,
        ),
        name="attend_back",
    )(query, key, value, mix, grad_mix, log_total, query_table, key_table, query_pos, key_pos)


def body(
    tokens,
    attn_gain,
    w_query,
    key_weight,
    value_weight,
    w_output,
    mlp_gain,
    w_gate,
    w_up,
    w_down,
    cotangent,
):
    _, length, width = tokens.shape
    shards, shard = lax.axis_size("shard"), lax.axis_index("shard")
    context, place = lax.axis_index("context"), lax.axis_index("tensor")
    places = lax.axis_size("tensor")
    rows = 2 * length
    upper = place // 2 == 1
    kv_cols, hidden_cols = key_weight.shape[1], w_gate.shape[1]

    starts = [
        (which * places + (place ^ step)) * length
        for which in (context, 1 - context)
        for step in (0, 2, 1, 3)
    ]
    table = jnp.asarray(rope_tables(length * places * lax.axis_size("context")))
    key_table = jnp.concatenate([lax.dynamic_slice_in_dim(table, at, length, 0) for at in starts], 0)
    key_pos = jnp.concatenate([at + jnp.arange(length, dtype=jnp.int32) for at in starts])
    query_table, query_pos = key_table[:rows], key_pos[:rows, None]
    key_pos = key_pos[None, :]

    mine, other = jnp.where(upper, tokens[1], tokens[0]), jnp.where(upper, tokens[0], tokens[1])
    moved = swap(other, "tensor", 2)
    beside = swap(mine, "tensor", 1)
    moved_beside = swap(moved, "tensor", 1)
    pieces = [mine, moved, beside, moved_beside]
    across = {k: swap(pieces[k], "context", 1) for k in (0, 2, 1, 3)}
    pieces = pieces + [across[k] for k in range(4)]
    all_tokens = jnp.concatenate([to_relative(piece, shards, shard) for piece in pieces], 0)

    def gained(weights, gain):
        joined = jnp.concatenate(weights, 1)
        return (joined.astype(jnp.float32) * gain[:, None]).astype(jnp.bfloat16)

    attn_local = jnp.concatenate([key_weight, value_weight, w_query], 1)
    attn_cols = attn_local.shape[1]
    gap = -attn_cols % 128
    gaps = jnp.zeros((attn_local.shape[0], gap), jnp.bfloat16)
    first_local = jnp.concatenate([gained([attn_local], attn_gain), gaps, w_output.T], 1)
    first_pieces = gather_pieces(first_local, beside)
    ends = (2 * kv_cols, attn_cols, attn_cols + gap)
    w_kv = jnp.concatenate([piece[:, : ends[0]] for piece in first_pieces], 0)
    w_q = jnp.concatenate([piece[:, ends[0] : ends[1]] for piece in first_pieces], 0)
    out_weight = jnp.concatenate([piece[:, ends[2] :] for piece in first_pieces], 0)
    mlp_local = jnp.concatenate([gained([w_gate, w_up], mlp_gain), w_down.T], 1)

    cots = [after(to_relative(cotangent, shards, shard), moved_beside)]
    cots.append(shift(cots[0], 1))
    cots = [after(cots[0], cots[1]), cots[1], shift(cots[1], 1)]
    cots.append(shift(cots[0], -1))
    all_tokens = after(all_tokens, cots[1])

    all_float = all_tokens.astype(jnp.float32)
    all_scale = rms_scale(all_float)
    all_normed = (all_float * all_scale).astype(jnp.bfloat16)
    tokens_f, scale_a, normed_a = all_float[:rows], all_scale[:rows], all_normed[:rows]
    query = dot(normed_a, w_q)
    key_value = dot(all_normed, w_kv)
    key, value = key_value[:, :kv_cols], key_value[:, kv_cols:].astype(jnp.bfloat16)
    mix, log_total, query_rot, key_rot = attend(
        query, key, value, query_table, key_table, query_pos, key_pos
    )
    mlp_pieces = gather_pieces(mlp_local, query, mix)
    w_in = jnp.concatenate([piece[:, : 2 * hidden_cols] for piece in mlp_pieces], 0)
    w_dn = jnp.concatenate([piece[:, 2 * hidden_cols :] for piece in mlp_pieces], 0)
    hidden = tokens_f + dot_rows(mix, out_weight)
    scale_m = rms_scale(hidden)
    normed_m = (hidden * scale_m).astype(jnp.bfloat16)

    normed_m, cots[2], cots[3] = lax.optimization_barrier((normed_m, cots[2], cots[3]))

    def cot_of(k):
        above = ((place - k) % places) // 2 == 1
        pair = (cots[k], cots[(k + 2) % places])
        return jnp.concatenate([jnp.where(above, one[1], one[0]) for one in pair], 0)

    cots = [cot_of(k) for k in range(places)]
    own_cot = cots[0]
    barrier = lax.optimization_barrier

    group, acts, grads_in, backs = [normed_m], [], [], []
    arriving = shift(normed_m, 1)
    for k, cot in enumerate(cots):
        if k > 0:
            group.append(arriving if k < 3 else after(arriving, grad_nm))
            if k + 1 < places:
                arriving = shift(arriving if k == 1 else after(arriving, backs[-1]), 1)
        rows_in = group[k]
        grad_act = dot(cot, w_dn)
        inner = dot(rows_in, w_in)
        gate, up_vals = inner[:, :hidden_cols], inner[:, hidden_cols:]
        sigma = jax.nn.sigmoid(gate)
        acts.append((gate * sigma * up_vals).astype(jnp.bfloat16))
        grad_up = (grad_act * gate * sigma).astype(jnp.bfloat16)
        grad_gate = (grad_act * up_vals * sigma * (1.0 + gate * (1.0 - sigma))).astype(jnp.bfloat16)
        grads_in.append(jnp.concatenate([grad_gate, grad_up], 1))
        backs.append(dot_rows(grads_in[-1], w_in).astype(jnp.bfloat16))
        if k > 0:
            grad_nm = backs[k] if k == 1 else backs[k] + shift(grad_nm, 1)
    bits = bits_of(shards)
    *held, _ = barrier((*grads_in, *acts, grad_nm))
    group, cot_group = jnp.concatenate(group, 0), jnp.concatenate(cots, 0)
    grad_in, act = jnp.concatenate(held[:places], 0), jnp.concatenate(held[places:], 0)
    mlp_term = jnp.concatenate(
        [dot_cols(group, grad_in).astype(jnp.bfloat16), dot_cols(cot_group, act).astype(jnp.bfloat16)], 1
    )
    mlp_term = scatter_rows(mlp_term, 0, 1)
    half_cols = mlp_term.shape[1] // 2
    first, second = mlp_term[:, :half_cols], mlp_term[:, half_cols:]
    later = context == 1
    mlp_kept, mlp_sent = jnp.where(later, second, first), jnp.where(later, first, second)

    grad_nm = (backs[0] + shift(grad_nm, 1)).astype(jnp.float32)
    grad_hidden = own_cot.astype(jnp.float32) + norm_back(grad_nm, hidden, scale_m)
    gain_m_term = jnp.sum(grad_nm * (hidden * scale_m), axis=0)
    grad_hidden_low = grad_hidden.astype(jnp.bfloat16)
    grad_mix = dot(grad_hidden_low, out_weight).astype(jnp.bfloat16)
    out_term = scatter_rows(dot_cols(grad_hidden_low, mix).astype(jnp.bfloat16), 0, bits)
    forward = [dot_rows(act, w_dn).astype(jnp.bfloat16) for act in acts]
    total = shift(after(forward[1], grad_mix), 1)

    grads = attend_back(
        query_rot, key_rot, value, mix, grad_mix, log_total, query_table, key_table, query_pos, key_pos
    )
    grads, out_term, total = barrier((grads, out_term, total))

    spot = (jnp.arange(grads.shape[1]) == attn_cols).astype(jnp.float32)
    attn_term = dot_cols(all_normed, grads) + gain_m_term[:, None] * spot[None, :]
    attn_term = scatter_rows(attn_term.astype(jnp.bfloat16), 0, 1)
    mlp_sent = after(mlp_sent, attn_term)
    attn_term = scatter_rows(attn_term, 1, bits)
    grad_query, grad_kv = grads[:rows, 2 * kv_cols : attn_cols], grads[:, : 2 * kv_cols]
    pair = grad_kv[: 2 * rows] + swap(grad_kv[2 * rows :], "context", 1)
    own_kv = pair[:rows] + swap(pair[rows:], "tensor", 1)
    out_part = group_sum_parts(out_term)
    total = shift(forward[2] + total, 1)
    total = shift(forward[3] + total, 1)
    mlp_half = mlp_kept + swap(mlp_sent, "context", 1)
    attn_term, own_kv, out_part, total, mlp_half = barrier((attn_term, own_kv, out_part, total, mlp_half))

    attn_part = group_sum_parts(attn_term)
    mlp_half = scatter_rows(mlp_half, 1, bits)
    own_kv, grad_query, mlp_half = barrier((own_kv, grad_query, mlp_half))
    block = hidden + forward[0].astype(jnp.float32) + total.astype(jnp.float32)
    block = from_relative(block.astype(jnp.bfloat16), shards, shard)
    grad_na = dot_rows(grad_query, w_q) + dot_rows(own_kv, w_kv)
    grad_tokens = grad_hidden + norm_back(grad_na, tokens_f, scale_a)
    grad_tokens = from_relative(grad_tokens.astype(jnp.bfloat16), shards, shard)
    block_back = swap(block[length:], "tensor", 2)
    attn_part, mlp_half, grad_tokens = barrier((attn_part, mlp_half, grad_tokens))

    parts = group_collect(jnp.concatenate([attn_part, out_part], 1))
    mlp_other = swap(mlp_half, "context", 1)
    mlp_total = jnp.concatenate(
        [jnp.where(later, mlp_other, mlp_half), jnp.where(later, mlp_half, mlp_other)], 1
    ).astype(jnp.float32)
    gate_total = mlp_total[:, :hidden_cols] * mlp_gain[:, None]
    up_total = mlp_total[:, hidden_cols : 2 * hidden_cols] * mlp_gain[:, None]
    down_total = mlp_total[:, 2 * hidden_cols :].T
    tokens_back = swap(grad_tokens[length:], "tensor", 2)
    gate_total, block, grad_tokens = barrier((gate_total, block[:length], grad_tokens[:length]))
    block_out = both_sequences(block, block_back, upper)
    tokens_grad = both_sequences(grad_tokens, tokens_back, upper)
    query_total, key_total, value_total, out_total = unpack(parts, attn_gain[:, None], kv_cols, attn_cols)
    heads = parts[: attn_local.shape[0], : attn_cols + 1].astype(jnp.float32)
    gain_m_total = heads[:, attn_cols] / mlp_gain
    gain_a_total = jnp.sum(attn_local.astype(jnp.float32) * heads[:, :attn_cols], axis=1)
    return (
        block_out,
        tokens_grad,
        gain_a_total,
        query_total,
        key_total.T,
        value_total.T,
        out_total,
        gain_m_total,
        gate_total,
        up_total,
        down_total,
    )


def solution(mesh):
    specs = (
        P("shard", ("context", "tensor"), None),
        P("shard"),
        P("shard", None),
        P("shard", None),
        P("shard", None),
        P(None, "shard"),
        P("shard"),
        P("shard", "tensor"),
        P("shard", "tensor"),
        P("tensor", "shard"),
    )
    return jax.shard_map(
        body,
        mesh=mesh,
        in_specs=specs + specs[:1],
        out_specs=specs[:1] + specs,
        check_vma=False,
    )
```

```python
import functools

import jax
import jax.numpy as jnp
import numpy as np
from jax import lax
from jax.experimental import pallas as pl
from jax.experimental.pallas import tpu as pltpu
from jax.sharding import PartitionSpec as P

QUERY_HEADS = 15
KEY_VALUE_HEADS = 5
HEAD_SIZE = 64
GROUP = QUERY_HEADS // KEY_VALUE_HEADS
SCALE = HEAD_SIZE ** (-0.5)
EPS = 1e-05
KERNEL_VMEM = 40 * 1024 * 1024


def dot(left, right):
    return jnp.dot(left, right, preferred_element_type=jnp.float32)


def dot_rows(left, right):
    return lax.dot_general(
        left, right, (((1,), (1,)), ((), ())), preferred_element_type=jnp.float32
    )


def dot_cols(left, right):
    return lax.dot_general(
        left, right, (((0,), (0,)), ((), ())), preferred_element_type=jnp.float32
    )


def rms_scale(rows):
    return lax.rsqrt(jnp.mean(rows * rows, axis=-1, keepdims=True) + EPS)


def norm_back(scaled, rows, scale_rows):
    normed = rows * scale_rows
    return scale_rows * (scaled - normed * jnp.mean(scaled * normed, axis=-1, keepdims=True))


def after(value, *others):
    return lax.optimization_barrier((value, *others))[0]


def bits_of(count):
    return count.bit_length() - 1


def flip_blocks(rows, shards, index):
    width = rows.shape[-1] // shards
    bits = bits_of(shards)
    for place in range(bits):
        step = width << place
        pieces = [rows[..., i * step : (i + 1) * step] for i in range(rows.shape[-1] // step)]
        swapped = jnp.concatenate([pieces[i ^ 1] for i in range(len(pieces))], -1)
        rows = jnp.where((index >> (bits - 1 - place)) & 1 == 1, swapped, rows)
    return rows


def reverse_blocks(rows, shards):
    width = rows.shape[-1] // shards
    bits = bits_of(shards)
    order = [int(format(i, f"0{bits}b")[::-1], 2) for i in range(shards)]
    return jnp.concatenate([rows[..., i * width : (i + 1) * width] for i in order], -1)


def to_relative(rows, shards, index):
    return flip_blocks(reverse_blocks(rows, shards), shards, index)


def from_relative(rows, shards, index):
    return reverse_blocks(flip_blocks(rows, shards, index), shards)


def swap(value, axis, bit):
    size = lax.axis_size(axis)
    return lax.ppermute(value, axis, [(i, i ^ bit) for i in range(size)])


def gather_pieces(rows, gate, later=None):
    pieces = [rows]
    for place in reversed(range(bits_of(lax.axis_size("shard")))):
        if len(pieces) > 2:
            pieces = [jnp.concatenate(pieces, 0)]
        sent = pieces
        if gate is not None:
            sent = [after(rows, gate)]
            gate = None
        elif later is not None:
            sent = pieces[:1] + [after(piece, later) for piece in pieces[1:]]
        pieces = pieces + [swap(piece, "shard", 1 << place) for piece in sent]
    return pieces


def scatter_rows(rows, first, last):
    for place in range(first, last):
        half = rows.shape[0] // 2
        rows = rows[:half] + swap(rows[half:], "shard", 1 << place)
    return rows


def shift(value, count):
    size = lax.axis_size("tensor")
    return lax.ppermute(value, "tensor", [(i, (i + count) % size) for i in range(size)])


def both_sequences(mine, other, upper):
    return jnp.stack([jnp.where(upper, other, mine), jnp.where(upper, mine, other)])


def chunk_rows(count, group):
    chunk = -(-count // group)
    return chunk if chunk <= 16 else -(-chunk // 16) * 16


def group_halves(rows, context):
    chunk = chunk_rows(rows.shape[0], 2 * lax.axis_size("tensor"))
    half = chunk * lax.axis_size("tensor")
    padded = jnp.pad(rows, ((0, 2 * half - rows.shape[0]), (0, 0)))
    kept = lax.dynamic_slice_in_dim(padded, context * half, half, 0)
    sent = lax.dynamic_slice_in_dim(padded, (1 - context) * half, half, 0)
    return kept + swap(sent, "context", 1)


def group_part(half):
    places = lax.axis_size("tensor")
    parts = lax.all_to_all(half, "tensor", split_axis=0, concat_axis=0, tiled=True)
    parts = parts.reshape(places, half.shape[0] // places, half.shape[1]).astype(jnp.float32)
    return jnp.sum(parts, axis=0).astype(jnp.bfloat16)


def group_collect(part):
    places = lax.axis_size("tensor")
    spread = jnp.broadcast_to(part[None], (places,) + part.shape)
    spread = spread.reshape(places * part.shape[0], part.shape[1])
    return lax.all_to_all(spread, "tensor", split_axis=0, concat_axis=0, tiled=True)


def unpack_kernel(kv_cols, attn_cols, parts_ref, gain_ref, query_ref, key_ref, value_ref, out_ref):
    rows = query_ref.shape[0]
    gain = gain_ref[...]
    query_ref[...] = parts_ref[:rows, 2 * kv_cols : attn_cols].astype(jnp.float32) * gain
    key_ref[...] = (parts_ref[:rows, :kv_cols].astype(jnp.float32) * gain).T
    value_ref[...] = (parts_ref[:rows, kv_cols : 2 * kv_cols].astype(jnp.float32) * gain).T
    first = attn_cols + -attn_cols % 128
    out_ref[...] = parts_ref[:rows, first : first + out_ref.shape[0]].astype(jnp.float32).T


def unpack(parts, gain, kv_cols, attn_cols, out_cols):
    rows = gain.shape[0]
    shapes = ((rows, attn_cols - 2 * kv_cols), (kv_cols, rows), (kv_cols, rows), (out_cols, rows))
    return pl.pallas_call(
        functools.partial(unpack_kernel, kv_cols, attn_cols),
        out_shape=tuple(jax.ShapeDtypeStruct(shape, jnp.float32) for shape in shapes),
        compiler_params=pltpu.CompilerParams(vmem_limit_bytes=KERNEL_VMEM),
        cost_estimate=pl.CostEstimate(flops=0, transcendentals=0, bytes_accessed=4_000_000),
        name="unpack",
    )(parts, gain)


def rope_tables(length):
    half = HEAD_SIZE // 2
    freq = np.float32(10000.0) ** (-np.arange(half).astype(np.float32) * 2.0 / HEAD_SIZE)
    angle = np.arange(length).astype(np.float32)[:, None] * freq.astype(np.float32)[None, :]
    cosine, sine = np.cos(angle), np.sin(angle)
    return np.concatenate([cosine, cosine, -sine, sine], 1).astype(np.float32)


def turn(head, table):
    half = HEAD_SIZE // 2
    swapped = jnp.concatenate([head[:, half:], head[:, :half]], 1)
    return head * table[:, :HEAD_SIZE] + swapped * table[:, HEAD_SIZE:]


def turn_back(head, table):
    half = HEAD_SIZE // 2
    swapped = jnp.concatenate([head[:, half:], head[:, :half]], 1)
    return head * table[:, :HEAD_SIZE] - swapped * table[:, HEAD_SIZE:]


def head_cols(index):
    return slice(index * HEAD_SIZE, (index + 1) * HEAD_SIZE)


def attend_kernel(q_ref, k_ref, v_ref, qt_ref, kt_ref, qp_ref, kp_ref, mix_ref, log_ref, qr_ref, kr_ref):
    hidden = jnp.where(kp_ref[...] <= qp_ref[...], 0.0, -1e30)
    hidden = jnp.concatenate([hidden] * GROUP, 0)
    rows = q_ref.shape[0]
    for g in range(KEY_VALUE_HEADS):
        key = turn(k_ref[:, head_cols(g)], kt_ref[...]).astype(jnp.bfloat16)
        kr_ref[:, head_cols(g)] = key
        value = v_ref[:, head_cols(g)]
        heads = []
        for i in range(GROUP):
            cols = head_cols(g * GROUP + i)
            head = turn(q_ref[:, cols], qt_ref[...]).astype(jnp.bfloat16) * SCALE
            qr_ref[:, cols] = head
            heads.append(head)
        query = jnp.concatenate(heads, 0)
        scores = dot_rows(query, key) + hidden
        peak = jnp.max(scores, axis=-1, keepdims=True)
        expd = jnp.exp(scores - peak)
        total = jnp.sum(expd, axis=-1, keepdims=True)
        mixed = (dot(expd.astype(jnp.bfloat16), value) / total).astype(jnp.bfloat16)
        for i in range(GROUP):
            mix_ref[:, head_cols(g * GROUP + i)] = mixed[i * rows : (i + 1) * rows]
        log_ref[:, g : g + 1] = peak + jnp.log(total)


def attend(query, key, value, query_table, key_table, query_pos, key_pos):
    rows, keys = query.shape[0], key.shape[0]
    return pl.pallas_call(
        attend_kernel,
        out_shape=(
            jax.ShapeDtypeStruct(query.shape, jnp.bfloat16),
            jax.ShapeDtypeStruct((GROUP * rows, 8), jnp.float32),
            jax.ShapeDtypeStruct(query.shape, jnp.bfloat16),
            jax.ShapeDtypeStruct(key.shape, jnp.bfloat16),
        ),
        compiler_params=pltpu.CompilerParams(vmem_limit_bytes=KERNEL_VMEM),
        cost_estimate=pl.CostEstimate(
            flops=4 * rows * keys * QUERY_HEADS * HEAD_SIZE,
            transcendentals=rows * keys * QUERY_HEADS,
            bytes_accessed=4_000_000,
        ),
        name="attend",
    )(query, key, value, query_table, key_table, query_pos, key_pos)


def attend_back_kernel(
    q_ref, k_ref, v_ref, mix_ref, gm_ref, log_ref, qt_ref, kt_ref, qp_ref, kp_ref, grad_ref
):
    hidden = jnp.where(kp_ref[...] <= qp_ref[...], 0.0, -1e30)
    hidden = jnp.concatenate([hidden] * GROUP, 0)
    rows, keys = q_ref.shape[0], k_ref.shape[0]
    kv_cols = 2 * k_ref.shape[1]
    grad_ref[rows:, kv_cols:] = jnp.zeros((keys - rows, grad_ref.shape[1] - kv_cols), jnp.bfloat16)
    used = kv_cols + q_ref.shape[1]
    if used < grad_ref.shape[1]:
        grad_ref[:rows, used:] = jnp.zeros((rows, grad_ref.shape[1] - used), jnp.bfloat16)
    for g in range(KEY_VALUE_HEADS):
        key, value = k_ref[:, head_cols(g)], v_ref[:, head_cols(g)]
        each = [head_cols(g * GROUP + i) for i in range(GROUP)]
        query = jnp.concatenate([q_ref[:, cols] for cols in each], 0)
        mixed = jnp.concatenate([mix_ref[:, cols] for cols in each], 0)
        grad_mix = jnp.concatenate([gm_ref[:, cols] for cols in each], 0)
        scores = dot_rows(query, key) + hidden
        probs = jnp.exp(scores - log_ref[:, g : g + 1])
        grad_probs = dot_rows(grad_mix, value)
        delta = jnp.sum(
            grad_mix.astype(jnp.float32) * mixed.astype(jnp.float32), axis=-1, keepdims=True
        )
        grad_scores = (probs * (grad_probs - delta)).astype(jnp.bfloat16)
        grad_query = dot(grad_scores, key) * SCALE
        grad_key = dot_cols(grad_scores, query)
        grad_value = dot_cols(probs.astype(jnp.bfloat16), grad_mix)
        for i in range(GROUP):
            head = turn_back(grad_query[i * rows : (i + 1) * rows], qt_ref[...])
            grad_ref[:rows, head_cols(2 * KEY_VALUE_HEADS + g * GROUP + i)] = head.astype(jnp.bfloat16)
        grad_ref[:, head_cols(g)] = turn_back(grad_key, kt_ref[...]).astype(jnp.bfloat16)
        grad_ref[:, head_cols(KEY_VALUE_HEADS + g)] = grad_value.astype(jnp.bfloat16)


def attend_back(query, key, value, mix, grad_mix, log_total, query_table, key_table, query_pos, key_pos):
    rows, keys = query.shape[0], key.shape[0]
    used = 2 * key.shape[1] + query.shape[1]
    return pl.pallas_call(
        attend_back_kernel,
        out_shape=jax.ShapeDtypeStruct((keys, used + -used % 128), jnp.bfloat16),
        compiler_params=pltpu.CompilerParams(vmem_limit_bytes=KERNEL_VMEM),
        cost_estimate=pl.CostEstimate(
            flops=10 * rows * keys * QUERY_HEADS * HEAD_SIZE,
            transcendentals=rows * keys * QUERY_HEADS,
            bytes_accessed=6_000_000,
        ),
        name="attend_back",
    )(query, key, value, mix, grad_mix, log_total, query_table, key_table, query_pos, key_pos)


def body(
    tokens,
    attn_gain,
    w_query,
    key_weight,
    value_weight,
    w_output,
    mlp_gain,
    w_gate,
    w_up,
    w_down,
    cotangent,
):
    _, length, width = tokens.shape
    shards, shard = lax.axis_size("shard"), lax.axis_index("shard")
    context, place = lax.axis_index("context"), lax.axis_index("tensor")
    places = lax.axis_size("tensor")
    rows = 2 * length
    upper = place // 2 == 1
    kv_cols, hidden_cols = key_weight.shape[1], w_gate.shape[1]

    starts = [
        (which * places + (place ^ step)) * length
        for which in (context, 1 - context)
        for step in (0, 2, 1, 3)
    ]
    table = jnp.asarray(rope_tables(length * places * lax.axis_size("context")))
    key_table = jnp.concatenate([lax.dynamic_slice_in_dim(table, at, length, 0) for at in starts], 0)
    key_pos = jnp.concatenate([at + jnp.arange(length, dtype=jnp.int32) for at in starts])
    query_table, query_pos = key_table[:rows], key_pos[:rows, None]
    key_pos = key_pos[None, :]

    mine, other = jnp.where(upper, tokens[1], tokens[0]), jnp.where(upper, tokens[0], tokens[1])
    moved = swap(other, "tensor", 2)
    own = jnp.concatenate([to_relative(mine, shards, shard), to_relative(moved, shards, shard)], 0)
    beside = swap(own, "tensor", 1)
    across = swap(own, "context", 1)
    across_beside = swap(after(beside, across), "context", 1)
    all_tokens = jnp.concatenate([own, beside, across, across_beside], 0)

    def gained(weights, gain):
        joined = jnp.concatenate(weights, 1)
        return (joined.astype(jnp.float32) * gain[:, None]).astype(jnp.bfloat16)

    attn_local = jnp.concatenate([key_weight, value_weight, w_query], 1)
    attn_cols = attn_local.shape[1]
    gap = -attn_cols % 128
    gaps = jnp.zeros((attn_local.shape[0], gap), jnp.bfloat16)
    first_local = jnp.concatenate([gained([attn_local], attn_gain), gaps, w_output.T], 1)
    first_pieces = gather_pieces(first_local, None)
    ends = (2 * kv_cols, attn_cols, attn_cols + gap)
    w_kv = jnp.concatenate([piece[:, : ends[0]] for piece in first_pieces], 0)
    w_q = jnp.concatenate([piece[:, ends[0] : ends[1]] for piece in first_pieces], 0)
    out_weight = jnp.concatenate([piece[:, ends[2] :] for piece in first_pieces], 0)
    mlp_local = jnp.concatenate([gained([w_gate, w_up], mlp_gain), w_down.T], 1)

    cots = [after(to_relative(cotangent, shards, shard), beside)]
    cots.append(shift(cots[0], 1))
    cots = [after(cots[0], cots[1]), cots[1], shift(cots[1], 1)]
    cots.append(shift(cots[0], -1))
    all_tokens = after(all_tokens, cots[1])

    all_float = all_tokens.astype(jnp.float32)
    all_scale = rms_scale(all_float)
    all_normed = (all_float * all_scale).astype(jnp.bfloat16)
    tokens_f, scale_a, normed_a = all_float[:rows], all_scale[:rows], all_normed[:rows]
    query = dot(normed_a, w_q)
    key_value = dot(all_normed, w_kv)
    key, value = key_value[:, :kv_cols], key_value[:, kv_cols:].astype(jnp.bfloat16)
    mix, log_total, query_rot, key_rot = attend(
        query, key, value, query_table, key_table, query_pos, key_pos
    )
    mlp_pieces = gather_pieces(mlp_local, w_kv, mix)
    w_in = jnp.concatenate([piece[:, : 2 * hidden_cols] for piece in mlp_pieces], 0)
    w_dn = jnp.concatenate([piece[:, 2 * hidden_cols :] for piece in mlp_pieces], 0)
    hidden = tokens_f + dot_rows(mix, out_weight)
    scale_m = rms_scale(hidden)
    normed_m = (hidden * scale_m).astype(jnp.bfloat16)

    normed_m, cots[2], cots[3] = lax.optimization_barrier((normed_m, cots[2], cots[3]))

    def cot_of(k):
        above = ((place - k) % places) // 2 == 1
        pair = (cots[k], cots[(k + 2) % places])
        return jnp.concatenate([jnp.where(above, one[1], one[0]) for one in pair], 0)

    cots = [cot_of(k) for k in range(places)]
    own_cot = cots[0]
    barrier = lax.optimization_barrier

    group, acts, grads_in, backs = [normed_m], [], [], []
    arriving = shift(normed_m, 1)
    for k, cot in enumerate(cots):
        if k > 0:
            group.append(arriving if k < 3 else after(arriving, grad_nm))
            if k + 1 < places:
                arriving = shift(arriving if k == 1 else after(arriving, backs[-1]), 1)
        rows_in = group[k]
        grad_act = dot(cot, w_dn)
        inner = dot(rows_in, w_in)
        gate, up_vals = inner[:, :hidden_cols], inner[:, hidden_cols:]
        sigma = jax.nn.sigmoid(gate)
        acts.append((gate * sigma * up_vals).astype(jnp.bfloat16))
        grad_up = (grad_act * gate * sigma).astype(jnp.bfloat16)
        grad_gate = (grad_act * up_vals * sigma * (1.0 + gate * (1.0 - sigma))).astype(jnp.bfloat16)
        grads_in.append(jnp.concatenate([grad_gate, grad_up], 1))
        backs.append(dot_rows(grads_in[-1], w_in).astype(jnp.bfloat16))
        if k > 0:
            grad_nm = backs[k] if k == 1 else backs[k] + shift(grad_nm, 1)
    bits = bits_of(shards)
    *held, _ = barrier((*grads_in, *acts, grad_nm))
    group, cot_group = jnp.concatenate(group, 0), jnp.concatenate(cots, 0)
    grad_in, act = jnp.concatenate(held[:places], 0), jnp.concatenate(held[places:], 0)
    mlp_term = jnp.concatenate(
        [dot_cols(group, grad_in).astype(jnp.bfloat16), dot_cols(cot_group, act).astype(jnp.bfloat16)], 1
    )
    mlp_term = scatter_rows(mlp_term, 0, 1)
    half_cols = mlp_term.shape[1] // 2
    first, second = mlp_term[:, :half_cols], mlp_term[:, half_cols:]
    later = context == 1
    mlp_kept, mlp_sent = jnp.where(later, second, first), jnp.where(later, first, second)

    grad_nm = (backs[0] + shift(grad_nm, 1)).astype(jnp.float32)
    grad_hidden = own_cot.astype(jnp.float32) + norm_back(grad_nm, hidden, scale_m)
    gain_m_term = jnp.sum(grad_nm * (hidden * scale_m), axis=0)
    grad_hidden_low = grad_hidden.astype(jnp.bfloat16)
    grad_mix = dot(grad_hidden_low, out_weight).astype(jnp.bfloat16)
    out_term = scatter_rows(dot_cols(grad_hidden_low, mix).astype(jnp.bfloat16), 0, bits)
    forward = [dot_rows(act, w_dn).astype(jnp.bfloat16) for act in acts]
    total = shift(after(forward[1], grad_mix), 1)
    grad_mix, mlp_kept, mlp_sent = barrier((grad_mix, mlp_kept, mlp_sent))
    owned = mlp_sent.shape[0] // 2 if bits > 1 else 0
    mlp_early = swap(mlp_sent[owned:], "context", 1)

    grads = attend_back(
        query_rot, key_rot, value, mix, grad_mix, log_total, query_table, key_table, query_pos, key_pos
    )
    grads, out_term, total, mlp_early = barrier((grads, out_term, total, mlp_early))

    spot = (jnp.arange(grads.shape[1]) == attn_cols).astype(jnp.float32)
    attn_term = dot_cols(all_normed, grads) + gain_m_term[:, None] * spot[None, :]
    attn_term = scatter_rows(attn_term.astype(jnp.bfloat16), 0, 1)
    mlp_late = swap(after(mlp_sent[:owned], attn_term), "context", 1)
    attn_term = scatter_rows(attn_term, 1, bits)
    grad_query, grad_kv = grads[:rows, 2 * kv_cols : attn_cols], grads[:, : 2 * kv_cols]
    pair = grad_kv[: 2 * rows] + swap(grad_kv[2 * rows :], "context", 1)
    own_kv = pair[:rows] + swap(pair[rows:], "tensor", 1)
    out_part = group_part(group_halves(out_term, context))
    total = shift(forward[2] + total, 1)
    total = shift(forward[3] + total, 1)
    attn_term, own_kv, out_part, total = barrier((attn_term, own_kv, out_part, total))

    attn_half = group_halves(attn_term, context)
    mlp_half = scatter_rows(mlp_kept + jnp.concatenate([mlp_late, mlp_early], 0), 1, bits)
    attn_part = group_part(attn_half)
    own_kv, grad_query, mlp_half = barrier((own_kv, grad_query, mlp_half))
    block = hidden + forward[0].astype(jnp.float32) + total.astype(jnp.float32)
    block = from_relative(block.astype(jnp.bfloat16), shards, shard)
    grad_na = dot_rows(grad_query, w_q) + dot_rows(own_kv, w_kv)
    grad_tokens = grad_hidden + norm_back(grad_na, tokens_f, scale_a)
    grad_tokens = from_relative(grad_tokens.astype(jnp.bfloat16), shards, shard)
    block_back = swap(block[length:], "tensor", 2)
    attn_part, mlp_half, grad_tokens, block_back = barrier((attn_part, mlp_half, grad_tokens, block_back))

    fill = jnp.zeros((out_part.shape[0], -out_part.shape[1] % 128), jnp.bfloat16)
    parts = group_collect(jnp.concatenate([attn_part, out_part, fill], 1))
    parts_across = swap(parts, "context", 1)
    parts = jnp.concatenate(
        [jnp.where(later, parts_across, parts), jnp.where(later, parts, parts_across)], 0
    )
    mlp_other = swap(mlp_half, "context", 1)
    mlp_total = jnp.concatenate(
        [jnp.where(later, mlp_other, mlp_half), jnp.where(later, mlp_half, mlp_other)], 1
    ).astype(jnp.float32)
    gate_total = mlp_total[:, :hidden_cols] * mlp_gain[:, None]
    up_total = mlp_total[:, hidden_cols : 2 * hidden_cols] * mlp_gain[:, None]
    down_total = mlp_total[:, 2 * hidden_cols :].T
    tokens_back = swap(grad_tokens[length:], "tensor", 2)
    gate_total, block, grad_tokens = barrier((gate_total, block[:length], grad_tokens[:length]))
    block_out = both_sequences(block, block_back, upper)
    tokens_grad = both_sequences(grad_tokens, tokens_back, upper)
    query_total, key_total, value_total, out_total = unpack(
        parts, attn_gain[:, None], kv_cols, attn_cols, out_part.shape[1]
    )
    heads = parts[: attn_local.shape[0], : attn_cols + 1].astype(jnp.float32)
    gain_m_total = heads[:, attn_cols] / mlp_gain
    gain_a_total = jnp.sum(attn_local.astype(jnp.float32) * heads[:, :attn_cols], axis=1)
    return (
        block_out,
        tokens_grad,
        gain_a_total,
        query_total,
        key_total.T,
        value_total.T,
        out_total,
        gain_m_total,
        gate_total,
        up_total,
        down_total,
    )


def solution(mesh):
    specs = (
        P("shard", ("context", "tensor"), None),
        P("shard"),
        P("shard", None),
        P("shard", None),
        P("shard", None),
        P(None, "shard"),
        P("shard"),
        P("shard", "tensor"),
        P("shard", "tensor"),
        P("tensor", "shard"),
    )
    return jax.shard_map(
        body,
        mesh=mesh,
        in_specs=specs + specs[:1],
        out_specs=specs[:1] + specs,
        check_vma=False,
    )
```

```python
import functools

import jax
import jax.numpy as jnp
import numpy as np
from jax import lax
from jax.experimental import pallas as pl
from jax.experimental.pallas import tpu as pltpu
from jax.sharding import PartitionSpec as P

QUERY_HEADS = 15
KEY_VALUE_HEADS = 5
HEAD_SIZE = 64
GROUP = QUERY_HEADS // KEY_VALUE_HEADS
SCALE = HEAD_SIZE ** (-0.5)
EPS = 1e-05
KERNEL_VMEM = 40 * 1024 * 1024


def dot(left, right):
    return jnp.dot(left, right, preferred_element_type=jnp.float32)


def dot_rows(left, right):
    return lax.dot_general(
        left, right, (((1,), (1,)), ((), ())), preferred_element_type=jnp.float32
    )


def dot_cols(left, right):
    return lax.dot_general(
        left, right, (((0,), (0,)), ((), ())), preferred_element_type=jnp.float32
    )


def rms_scale(rows):
    return lax.rsqrt(jnp.mean(rows * rows, axis=-1, keepdims=True) + EPS)


def norm_back(scaled, rows, scale_rows):
    normed = rows * scale_rows
    return scale_rows * (scaled - normed * jnp.mean(scaled * normed, axis=-1, keepdims=True))


def after(value, *others):
    return lax.optimization_barrier((value, *others))[0]


def bits_of(count):
    return count.bit_length() - 1


def flip_blocks(rows, shards, index):
    width = rows.shape[-1] // shards
    bits = bits_of(shards)
    for place in range(bits):
        step = width << place
        pieces = [rows[..., i * step : (i + 1) * step] for i in range(rows.shape[-1] // step)]
        swapped = jnp.concatenate([pieces[i ^ 1] for i in range(len(pieces))], -1)
        rows = jnp.where((index >> (bits - 1 - place)) & 1 == 1, swapped, rows)
    return rows


def reverse_blocks(rows, shards):
    width = rows.shape[-1] // shards
    bits = bits_of(shards)
    order = [int(format(i, f"0{bits}b")[::-1], 2) for i in range(shards)]
    return jnp.concatenate([rows[..., i * width : (i + 1) * width] for i in order], -1)


def to_relative(rows, shards, index):
    return flip_blocks(reverse_blocks(rows, shards), shards, index)


def from_relative(rows, shards, index):
    return reverse_blocks(flip_blocks(rows, shards, index), shards)


def swap(value, axis, bit):
    size = lax.axis_size(axis)
    return lax.ppermute(value, axis, [(i, i ^ bit) for i in range(size)])


def gather_pieces(rows, gate, later=None):
    pieces = [rows]
    for place in reversed(range(bits_of(lax.axis_size("shard")))):
        if len(pieces) > 2:
            pieces = [jnp.concatenate(pieces, 0)]
        sent = pieces
        if gate is not None:
            sent = [after(rows, gate)]
            gate = None
        elif later is not None:
            sent = pieces[:1] + [after(piece, later) for piece in pieces[1:]]
        pieces = pieces + [swap(piece, "shard", 1 << place) for piece in sent]
    return pieces


def scatter_rows(rows, first, last, gate=None):
    for place in range(first, last):
        half = rows.shape[0] // 2
        kept = rows[:half] if gate is None else after(rows[:half], gate)
        rows = kept + swap(rows[half:], "shard", 1 << place)
    return rows


def shift(value, count):
    size = lax.axis_size("tensor")
    return lax.ppermute(value, "tensor", [(i, (i + count) % size) for i in range(size)])


def both_sequences(mine, other, upper):
    return jnp.stack([jnp.where(upper, other, mine), jnp.where(upper, mine, other)])


def chunk_rows(count, group):
    chunk = -(-count // group)
    return chunk if chunk <= 16 else -(-chunk // 16) * 16


def group_halves(rows, context):
    chunk = chunk_rows(rows.shape[0], 2 * lax.axis_size("tensor"))
    half = chunk * lax.axis_size("tensor")
    padded = jnp.pad(rows, ((0, 2 * half - rows.shape[0]), (0, 0)))
    kept = lax.dynamic_slice_in_dim(padded, context * half, half, 0)
    sent = lax.dynamic_slice_in_dim(padded, (1 - context) * half, half, 0)
    return kept + swap(sent, "context", 1)


def group_part(half):
    places = lax.axis_size("tensor")
    parts = lax.all_to_all(half, "tensor", split_axis=0, concat_axis=0, tiled=True)
    parts = parts.reshape(places, half.shape[0] // places, half.shape[1]).astype(jnp.float32)
    return jnp.sum(parts, axis=0).astype(jnp.bfloat16)


def group_collect(part):
    places = lax.axis_size("tensor")
    spread = jnp.broadcast_to(part[None], (places,) + part.shape)
    spread = spread.reshape(places * part.shape[0], part.shape[1])
    return lax.all_to_all(spread, "tensor", split_axis=0, concat_axis=0, tiled=True)


def unpack_kernel(kv_cols, attn_cols, parts_ref, gain_ref, query_ref, key_ref, value_ref, out_ref):
    rows = query_ref.shape[0]
    gain = gain_ref[...]
    query_ref[...] = parts_ref[:rows, 2 * kv_cols : attn_cols].astype(jnp.float32) * gain
    key_ref[...] = (parts_ref[:rows, :kv_cols].astype(jnp.float32) * gain).T
    value_ref[...] = (parts_ref[:rows, kv_cols : 2 * kv_cols].astype(jnp.float32) * gain).T
    first = attn_cols + -attn_cols % 128
    out_ref[...] = parts_ref[:rows, first : first + out_ref.shape[0]].astype(jnp.float32).T


def unpack(parts, gain, kv_cols, attn_cols, out_cols):
    rows = gain.shape[0]
    shapes = ((rows, attn_cols - 2 * kv_cols), (kv_cols, rows), (kv_cols, rows), (out_cols, rows))
    return pl.pallas_call(
        functools.partial(unpack_kernel, kv_cols, attn_cols),
        out_shape=tuple(jax.ShapeDtypeStruct(shape, jnp.float32) for shape in shapes),
        compiler_params=pltpu.CompilerParams(vmem_limit_bytes=KERNEL_VMEM),
        cost_estimate=pl.CostEstimate(flops=0, transcendentals=0, bytes_accessed=4_000_000),
        name="unpack",
    )(parts, gain)


def rope_tables(length):
    half = HEAD_SIZE // 2
    freq = np.float32(10000.0) ** (-np.arange(half).astype(np.float32) * 2.0 / HEAD_SIZE)
    angle = np.arange(length).astype(np.float32)[:, None] * freq.astype(np.float32)[None, :]
    cosine, sine = np.cos(angle), np.sin(angle)
    return np.concatenate([cosine, cosine, -sine, sine], 1).astype(np.float32)


def turn(head, table):
    half = HEAD_SIZE // 2
    swapped = jnp.concatenate([head[:, half:], head[:, :half]], 1)
    return head * table[:, :HEAD_SIZE] + swapped * table[:, HEAD_SIZE:]


def turn_back(head, table):
    half = HEAD_SIZE // 2
    swapped = jnp.concatenate([head[:, half:], head[:, :half]], 1)
    return head * table[:, :HEAD_SIZE] - swapped * table[:, HEAD_SIZE:]


def head_cols(index):
    return slice(index * HEAD_SIZE, (index + 1) * HEAD_SIZE)


def attend_kernel(q_ref, k_ref, v_ref, qt_ref, kt_ref, qp_ref, kp_ref, mix_ref, log_ref, qr_ref, kr_ref):
    hidden = jnp.where(kp_ref[...] <= qp_ref[...], 0.0, -1e30)
    hidden = jnp.concatenate([hidden] * GROUP, 0)
    rows = q_ref.shape[0]
    for g in range(KEY_VALUE_HEADS):
        key = turn(k_ref[:, head_cols(g)], kt_ref[...]).astype(jnp.bfloat16)
        kr_ref[:, head_cols(g)] = key
        value = v_ref[:, head_cols(g)]
        heads = []
        for i in range(GROUP):
            cols = head_cols(g * GROUP + i)
            head = turn(q_ref[:, cols], qt_ref[...]).astype(jnp.bfloat16) * SCALE
            qr_ref[:, cols] = head
            heads.append(head)
        query = jnp.concatenate(heads, 0)
        scores = dot_rows(query, key) + hidden
        peak = jnp.max(scores, axis=-1, keepdims=True)
        expd = jnp.exp(scores - peak)
        total = jnp.sum(expd, axis=-1, keepdims=True)
        mixed = (dot(expd.astype(jnp.bfloat16), value) / total).astype(jnp.bfloat16)
        for i in range(GROUP):
            mix_ref[:, head_cols(g * GROUP + i)] = mixed[i * rows : (i + 1) * rows]
        log_ref[:, g : g + 1] = peak + jnp.log(total)


def attend(query, key, value, query_table, key_table, query_pos, key_pos):
    rows, keys = query.shape[0], key.shape[0]
    return pl.pallas_call(
        attend_kernel,
        out_shape=(
            jax.ShapeDtypeStruct(query.shape, jnp.bfloat16),
            jax.ShapeDtypeStruct((GROUP * rows, 8), jnp.float32),
            jax.ShapeDtypeStruct(query.shape, jnp.bfloat16),
            jax.ShapeDtypeStruct(key.shape, jnp.bfloat16),
        ),
        compiler_params=pltpu.CompilerParams(vmem_limit_bytes=KERNEL_VMEM),
        cost_estimate=pl.CostEstimate(
            flops=4 * rows * keys * QUERY_HEADS * HEAD_SIZE,
            transcendentals=rows * keys * QUERY_HEADS,
            bytes_accessed=4_000_000,
        ),
        name="attend",
    )(query, key, value, query_table, key_table, query_pos, key_pos)


def attend_back_kernel(
    q_ref, k_ref, v_ref, mix_ref, gm_ref, log_ref, qt_ref, kt_ref, qp_ref, kp_ref, grad_ref
):
    hidden = jnp.where(kp_ref[...] <= qp_ref[...], 0.0, -1e30)
    hidden = jnp.concatenate([hidden] * GROUP, 0)
    rows, keys = q_ref.shape[0], k_ref.shape[0]
    kv_cols = 2 * k_ref.shape[1]
    grad_ref[rows:, kv_cols:] = jnp.zeros((keys - rows, grad_ref.shape[1] - kv_cols), jnp.bfloat16)
    used = kv_cols + q_ref.shape[1]
    if used < grad_ref.shape[1]:
        grad_ref[:rows, used:] = jnp.zeros((rows, grad_ref.shape[1] - used), jnp.bfloat16)
    for g in range(KEY_VALUE_HEADS):
        key, value = k_ref[:, head_cols(g)], v_ref[:, head_cols(g)]
        each = [head_cols(g * GROUP + i) for i in range(GROUP)]
        query = jnp.concatenate([q_ref[:, cols] for cols in each], 0)
        mixed = jnp.concatenate([mix_ref[:, cols] for cols in each], 0)
        grad_mix = jnp.concatenate([gm_ref[:, cols] for cols in each], 0)
        scores = dot_rows(query, key) + hidden
        probs = jnp.exp(scores - log_ref[:, g : g + 1])
        grad_probs = dot_rows(grad_mix, value)
        delta = jnp.sum(
            grad_mix.astype(jnp.float32) * mixed.astype(jnp.float32), axis=-1, keepdims=True
        )
        grad_scores = (probs * (grad_probs - delta)).astype(jnp.bfloat16)
        grad_query = dot(grad_scores, key) * SCALE
        grad_key = dot_cols(grad_scores, query)
        grad_value = dot_cols(probs.astype(jnp.bfloat16), grad_mix)
        for i in range(GROUP):
            head = turn_back(grad_query[i * rows : (i + 1) * rows], qt_ref[...])
            grad_ref[:rows, head_cols(2 * KEY_VALUE_HEADS + g * GROUP + i)] = head.astype(jnp.bfloat16)
        grad_ref[:, head_cols(g)] = turn_back(grad_key, kt_ref[...]).astype(jnp.bfloat16)
        grad_ref[:, head_cols(KEY_VALUE_HEADS + g)] = grad_value.astype(jnp.bfloat16)


def attend_back(query, key, value, mix, grad_mix, log_total, query_table, key_table, query_pos, key_pos):
    rows, keys = query.shape[0], key.shape[0]
    used = 2 * key.shape[1] + query.shape[1]
    return pl.pallas_call(
        attend_back_kernel,
        out_shape=jax.ShapeDtypeStruct((keys, used + -used % 128), jnp.bfloat16),
        compiler_params=pltpu.CompilerParams(vmem_limit_bytes=KERNEL_VMEM),
        cost_estimate=pl.CostEstimate(
            flops=10 * rows * keys * QUERY_HEADS * HEAD_SIZE,
            transcendentals=rows * keys * QUERY_HEADS,
            bytes_accessed=6_000_000,
        ),
        name="attend_back",
    )(query, key, value, mix, grad_mix, log_total, query_table, key_table, query_pos, key_pos)


def body(
    tokens,
    attn_gain,
    w_query,
    key_weight,
    value_weight,
    w_output,
    mlp_gain,
    w_gate,
    w_up,
    w_down,
    cotangent,
):
    _, length, width = tokens.shape
    shards, shard = lax.axis_size("shard"), lax.axis_index("shard")
    context, place = lax.axis_index("context"), lax.axis_index("tensor")
    places = lax.axis_size("tensor")
    rows = 2 * length
    upper = place // 2 == 1
    kv_cols, hidden_cols = key_weight.shape[1], w_gate.shape[1]

    starts = [
        (which * places + (place ^ step)) * length
        for which in (context, 1 - context)
        for step in (0, 2, 1, 3)
    ]
    table = jnp.asarray(rope_tables(length * places * lax.axis_size("context")))
    key_table = jnp.concatenate([lax.dynamic_slice_in_dim(table, at, length, 0) for at in starts], 0)
    key_pos = jnp.concatenate([at + jnp.arange(length, dtype=jnp.int32) for at in starts])
    query_table, query_pos = key_table[:rows], key_pos[:rows, None]
    key_pos = key_pos[None, :]

    mine, other = jnp.where(upper, tokens[1], tokens[0]), jnp.where(upper, tokens[0], tokens[1])
    moved = swap(other, "tensor", 2)
    own = jnp.concatenate([to_relative(mine, shards, shard), to_relative(moved, shards, shard)], 0)
    beside = swap(own, "tensor", 1)
    across = swap(own, "context", 1)
    across_beside = swap(after(beside, across), "context", 1)
    all_tokens = jnp.concatenate([own, beside, across, across_beside], 0)

    def gained(weights, gain):
        joined = jnp.concatenate(weights, 1)
        return (joined.astype(jnp.float32) * gain[:, None]).astype(jnp.bfloat16)

    k_early, v_early, q_early, o_early, _ = lax.optimization_barrier(
        (key_weight, value_weight, w_query, w_output, other)
    )
    attn_local = jnp.concatenate([k_early, v_early, q_early], 1)
    attn_cols = attn_local.shape[1]
    gap = -attn_cols % 128
    gaps = jnp.zeros((attn_local.shape[0], gap), jnp.bfloat16)
    first_local = jnp.concatenate([gained([attn_local], attn_gain), gaps, o_early.T], 1)
    first_pieces = gather_pieces(first_local, None)
    ends = (2 * kv_cols, attn_cols, attn_cols + gap)
    w_kv = jnp.concatenate([piece[:, : ends[0]] for piece in first_pieces], 0)
    w_q = jnp.concatenate([piece[:, ends[0] : ends[1]] for piece in first_pieces], 0)
    out_weight = jnp.concatenate([piece[:, ends[2] :] for piece in first_pieces], 0)
    mlp_local = jnp.concatenate([gained([w_gate, w_up], mlp_gain), w_down.T], 1)

    cots = [after(to_relative(cotangent, shards, shard), beside)]
    cots.append(shift(cots[0], 1))
    cots = [after(cots[0], cots[1]), cots[1], shift(cots[1], 1)]
    cots.append(shift(cots[0], -1))
    all_tokens = after(all_tokens, cots[1])

    all_float = all_tokens.astype(jnp.float32)
    all_scale = rms_scale(all_float)
    all_normed = (all_float * all_scale).astype(jnp.bfloat16)
    tokens_f, scale_a, normed_a = all_float[:rows], all_scale[:rows], all_normed[:rows]
    query = dot(normed_a, w_q)
    key_value = dot(all_normed, w_kv)
    key, value = key_value[:, :kv_cols], key_value[:, kv_cols:].astype(jnp.bfloat16)
    mix, log_total, query_rot, key_rot = attend(
        query, key, value, query_table, key_table, query_pos, key_pos
    )
    mlp_pieces = gather_pieces(mlp_local, w_kv, mix)
    w_in = jnp.concatenate([piece[:, : 2 * hidden_cols] for piece in mlp_pieces], 0)
    w_dn = jnp.concatenate([piece[:, 2 * hidden_cols :] for piece in mlp_pieces], 0)
    hidden = tokens_f + dot_rows(mix, out_weight)
    scale_m = rms_scale(hidden)
    normed_m = (hidden * scale_m).astype(jnp.bfloat16)

    normed_m, cots[2], cots[3] = lax.optimization_barrier((normed_m, cots[2], cots[3]))

    def cot_of(k):
        above = ((place - k) % places) // 2 == 1
        pair = (cots[k], cots[(k + 2) % places])
        return jnp.concatenate([jnp.where(above, one[1], one[0]) for one in pair], 0)

    cots = [cot_of(k) for k in range(places)]
    own_cot = cots[0]
    barrier = lax.optimization_barrier

    group, acts, grads_in, backs = [normed_m], [], [], []
    arriving = shift(normed_m, 1)
    for k, cot in enumerate(cots):
        if k > 0:
            group.append(arriving if k < 3 else after(arriving, grad_nm))
            if k + 1 < places:
                arriving = shift(arriving if k == 1 else after(arriving, backs[-1]), 1)
        rows_in = group[k]
        grad_act = dot(cot, w_dn)
        inner = dot(rows_in, w_in)
        gate, up_vals = inner[:, :hidden_cols], inner[:, hidden_cols:]
        sigma = jax.nn.sigmoid(gate)
        acts.append((gate * sigma * up_vals).astype(jnp.bfloat16))
        grad_up = (grad_act * gate * sigma).astype(jnp.bfloat16)
        grad_gate = (grad_act * up_vals * sigma * (1.0 + gate * (1.0 - sigma))).astype(jnp.bfloat16)
        grads_in.append(jnp.concatenate([grad_gate, grad_up], 1))
        backs.append(dot_rows(grads_in[-1], w_in).astype(jnp.bfloat16))
        if k > 0:
            grad_nm = backs[k] if k == 1 else backs[k] + shift(grad_nm, 1)
    bits = bits_of(shards)
    *held, _ = barrier((*grads_in, *acts, grad_nm))
    group, cot_group = jnp.concatenate(group, 0), jnp.concatenate(cots, 0)
    grad_in, act = jnp.concatenate(held[:places], 0), jnp.concatenate(held[places:], 0)
    mlp_term = jnp.concatenate(
        [dot_cols(group, grad_in).astype(jnp.bfloat16), dot_cols(cot_group, act).astype(jnp.bfloat16)], 1
    )
    mlp_beside = swap(mlp_term[mlp_term.shape[0] // 2 :], "shard", 1)
    half_cols = mlp_term.shape[1] // 2
    later = context == 1

    grad_nm = (backs[0] + shift(grad_nm, 1)).astype(jnp.float32)
    grad_hidden = own_cot.astype(jnp.float32) + norm_back(grad_nm, hidden, scale_m)
    gain_m_term = jnp.sum(grad_nm * (hidden * scale_m), axis=0)
    grad_hidden_low = grad_hidden.astype(jnp.bfloat16)
    grad_mix = dot(grad_hidden_low, out_weight).astype(jnp.bfloat16)
    out_term = scatter_rows(dot_cols(grad_hidden_low, mix).astype(jnp.bfloat16), 0, 1)
    forward = [dot_rows(act, w_dn).astype(jnp.bfloat16) for act in acts]
    total = shift(after(forward[1], grad_mix), 1)
    grads = attend_back(
        query_rot, key_rot, value, mix, grad_mix, log_total, query_table, key_table, query_pos, key_pos
    )
    grads, out_term, total, mlp_beside = barrier((grads, out_term, total, mlp_beside))

    spot = (jnp.arange(grads.shape[1]) == attn_cols).astype(jnp.float32)
    attn_term = dot_cols(all_normed, grads) + gain_m_term[:, None] * spot[None, :]
    attn_term = scatter_rows(attn_term.astype(jnp.bfloat16), 0, 1)
    attn_core = attn_term
    out_term = scatter_rows(out_term, 1, bits, attn_core)
    attn_term = scatter_rows(attn_term, 1, bits)
    grad_query, grad_kv = grads[:rows, 2 * kv_cols : attn_cols], grads[:, : 2 * kv_cols]
    pair = after(grad_kv[: 2 * rows], attn_core) + swap(grad_kv[2 * rows :], "context", 1)
    own_kv = pair[:rows] + swap(pair[rows:], "tensor", 1)
    out_part = group_part(group_halves(out_term, context))

    mlp_term = after(mlp_term[: mlp_beside.shape[0]], attn_core) + mlp_beside
    first, second = mlp_term[:, :half_cols], mlp_term[:, half_cols:]
    mlp_kept, mlp_sent = jnp.where(later, second, first), jnp.where(later, first, second)
    owned = mlp_sent.shape[0] // 2
    mlp_moved = swap(mlp_sent[owned:], "context", 1)
    mlp_owned = swap(mlp_sent[:owned], "context", 1)
    total = shift(forward[2] + total, 1)
    total = shift(forward[3] + total, 1)
    attn_term, own_kv, out_part, total, mlp_kept = barrier((attn_term, own_kv, out_part, total, mlp_kept))

    attn_half = group_halves(attn_term, context)
    mlp_half = scatter_rows(mlp_kept + jnp.concatenate([mlp_owned, mlp_moved], 0), 1, bits)
    attn_part = group_part(attn_half)
    own_kv, grad_query, mlp_half = barrier((own_kv, grad_query, mlp_half))
    block = hidden + forward[0].astype(jnp.float32) + total.astype(jnp.float32)
    block = from_relative(block.astype(jnp.bfloat16), shards, shard)
    grad_na = dot_rows(grad_query, w_q) + dot_rows(own_kv, w_kv)
    grad_tokens = grad_hidden + norm_back(grad_na, tokens_f, scale_a)
    grad_tokens = from_relative(grad_tokens.astype(jnp.bfloat16), shards, shard)
    block_back = swap(block[length:], "tensor", 2)
    attn_part, mlp_half, grad_tokens, block_back = barrier((attn_part, mlp_half, grad_tokens, block_back))

    fill = jnp.zeros((out_part.shape[0], -out_part.shape[1] % 128), jnp.bfloat16)
    parts = group_collect(jnp.concatenate([attn_part, out_part, fill], 1))
    parts_across = swap(parts, "context", 1)
    parts = jnp.concatenate(
        [jnp.where(later, parts_across, parts), jnp.where(later, parts, parts_across)], 0
    )
    mlp_other = swap(mlp_half, "context", 1)
    mlp_total = jnp.concatenate(
        [jnp.where(later, mlp_other, mlp_half), jnp.where(later, mlp_half, mlp_other)], 1
    ).astype(jnp.float32)
    gate_total = mlp_total[:, :hidden_cols] * mlp_gain[:, None]
    up_total = mlp_total[:, hidden_cols : 2 * hidden_cols] * mlp_gain[:, None]
    down_total = mlp_total[:, 2 * hidden_cols :].T
    tokens_back = swap(grad_tokens[length:], "tensor", 2)
    gate_total, block, grad_tokens = barrier((gate_total, block[:length], grad_tokens[:length]))
    block_out = both_sequences(block, block_back, upper)
    tokens_grad = both_sequences(grad_tokens, tokens_back, upper)
    query_total, key_total, value_total, out_total = unpack(
        parts, attn_gain[:, None], kv_cols, attn_cols, out_part.shape[1]
    )
    heads = parts[: attn_local.shape[0], : attn_cols + 1].astype(jnp.float32)
    gain_m_total = heads[:, attn_cols] / mlp_gain
    gain_a_total = jnp.sum(attn_local.astype(jnp.float32) * heads[:, :attn_cols], axis=1)
    return (
        block_out,
        tokens_grad,
        gain_a_total,
        query_total,
        key_total.T,
        value_total.T,
        out_total,
        gain_m_total,
        gate_total,
        up_total,
        down_total,
    )


def solution(mesh):
    specs = (
        P("shard", ("context", "tensor"), None),
        P("shard"),
        P("shard", None),
        P("shard", None),
        P("shard", None),
        P(None, "shard"),
        P("shard"),
        P("shard", "tensor"),
        P("shard", "tensor"),
        P("tensor", "shard"),
    )
    return jax.shard_map(
        body,
        mesh=mesh,
        in_specs=specs + specs[:1],
        out_specs=specs[:1] + specs,
        check_vma=False,
    )
```

```python
import functools

import jax
import jax.numpy as jnp
import numpy as np
from jax import lax
from jax.experimental import pallas as pl
from jax.experimental.pallas import tpu as pltpu
from jax.sharding import PartitionSpec as P

QUERY_HEADS = 15
KEY_VALUE_HEADS = 5
HEAD_SIZE = 64
GROUP = QUERY_HEADS // KEY_VALUE_HEADS
SCALE = HEAD_SIZE ** (-0.5)
EPS = 1e-05
KERNEL_VMEM = 40 * 1024 * 1024


def dot(left, right):
    return jnp.dot(left, right, preferred_element_type=jnp.float32)


def dot_rows(left, right):
    return lax.dot_general(
        left, right, (((1,), (1,)), ((), ())), preferred_element_type=jnp.float32
    )


def dot_cols(left, right):
    return lax.dot_general(
        left, right, (((0,), (0,)), ((), ())), preferred_element_type=jnp.float32
    )


def rms_scale(rows):
    return lax.rsqrt(jnp.mean(rows * rows, axis=-1, keepdims=True) + EPS)


def norm_back(scaled, rows, scale_rows):
    normed = rows * scale_rows
    return scale_rows * (scaled - normed * jnp.mean(scaled * normed, axis=-1, keepdims=True))


def after(value, *others):
    return lax.optimization_barrier((value, *others))[0]


def bits_of(count):
    return count.bit_length() - 1


def flip_blocks(rows, shards, index):
    width = rows.shape[-1] // shards
    bits = bits_of(shards)
    for place in range(bits):
        step = width << place
        pieces = [rows[..., i * step : (i + 1) * step] for i in range(rows.shape[-1] // step)]
        swapped = jnp.concatenate([pieces[i ^ 1] for i in range(len(pieces))], -1)
        rows = jnp.where((index >> (bits - 1 - place)) & 1 == 1, swapped, rows)
    return rows


def reverse_blocks(rows, shards):
    width = rows.shape[-1] // shards
    bits = bits_of(shards)
    order = [int(format(i, f"0{bits}b")[::-1], 2) for i in range(shards)]
    return jnp.concatenate([rows[..., i * width : (i + 1) * width] for i in order], -1)


def to_relative(rows, shards, index):
    return flip_blocks(reverse_blocks(rows, shards), shards, index)


def from_relative(rows, shards, index):
    return reverse_blocks(flip_blocks(rows, shards, index), shards)


def swap(value, axis, bit):
    size = lax.axis_size(axis)
    return lax.ppermute(value, axis, [(i, i ^ bit) for i in range(size)])


def gather_pieces(rows, gate, later=None):
    pieces = [rows]
    for place in reversed(range(bits_of(lax.axis_size("shard")))):
        if len(pieces) > 2:
            pieces = [jnp.concatenate(pieces, 0)]
        sent = pieces
        if gate is not None:
            sent = [after(rows, gate)]
            gate = None
        elif later is not None:
            sent = pieces[:1] + [after(piece, later) for piece in pieces[1:]]
        pieces = pieces + [swap(piece, "shard", 1 << place) for piece in sent]
    return pieces


def scatter_rows(rows, first, last, gate=None):
    for place in range(first, last):
        half = rows.shape[0] // 2
        kept = rows[:half] if gate is None else after(rows[:half], gate)
        rows = kept + swap(rows[half:], "shard", 1 << place)
    return rows


def shift(value, count):
    size = lax.axis_size("tensor")
    return lax.ppermute(value, "tensor", [(i, (i + count) % size) for i in range(size)])


def both_sequences(mine, other, upper):
    return jnp.stack([jnp.where(upper, other, mine), jnp.where(upper, mine, other)])


def chunk_rows(count, group):
    chunk = -(-count // group)
    return chunk if chunk <= 16 else -(-chunk // 16) * 16


def group_halves(rows, context):
    chunk = chunk_rows(rows.shape[0], 2 * lax.axis_size("tensor"))
    half = chunk * lax.axis_size("tensor")
    padded = jnp.pad(rows, ((0, 2 * half - rows.shape[0]), (0, 0)))
    kept = lax.dynamic_slice_in_dim(padded, context * half, half, 0)
    sent = lax.dynamic_slice_in_dim(padded, (1 - context) * half, half, 0)
    return kept + swap(sent, "context", 1)


def group_part(half):
    places = lax.axis_size("tensor")
    parts = lax.all_to_all(half, "tensor", split_axis=0, concat_axis=0, tiled=True)
    parts = parts.reshape(places, half.shape[0] // places, half.shape[1]).astype(jnp.float32)
    return jnp.sum(parts, axis=0).astype(jnp.bfloat16)


def group_collect(part):
    places = lax.axis_size("tensor")
    spread = jnp.broadcast_to(part[None], (places,) + part.shape)
    spread = spread.reshape(places * part.shape[0], part.shape[1])
    return lax.all_to_all(spread, "tensor", split_axis=0, concat_axis=0, tiled=True)


def unpack_kernel(kv_cols, attn_cols, parts_ref, gain_ref, query_ref, key_ref, value_ref, out_ref):
    rows = query_ref.shape[0]
    gain = gain_ref[...]
    query_ref[...] = parts_ref[:rows, 2 * kv_cols : attn_cols].astype(jnp.float32) * gain
    key_ref[...] = (parts_ref[:rows, :kv_cols].astype(jnp.float32) * gain).T
    value_ref[...] = (parts_ref[:rows, kv_cols : 2 * kv_cols].astype(jnp.float32) * gain).T
    first = attn_cols + -attn_cols % 128
    out_ref[...] = parts_ref[:rows, first : first + out_ref.shape[0]].astype(jnp.float32).T


def unpack(parts, gain, kv_cols, attn_cols, out_cols):
    rows = gain.shape[0]
    shapes = ((rows, attn_cols - 2 * kv_cols), (kv_cols, rows), (kv_cols, rows), (out_cols, rows))
    return pl.pallas_call(
        functools.partial(unpack_kernel, kv_cols, attn_cols),
        out_shape=tuple(jax.ShapeDtypeStruct(shape, jnp.float32) for shape in shapes),
        compiler_params=pltpu.CompilerParams(vmem_limit_bytes=KERNEL_VMEM),
        cost_estimate=pl.CostEstimate(flops=0, transcendentals=0, bytes_accessed=4_000_000),
        name="unpack",
    )(parts, gain)


def rope_tables(length):
    half = HEAD_SIZE // 2
    freq = np.float32(10000.0) ** (-np.arange(half).astype(np.float32) * 2.0 / HEAD_SIZE)
    angle = np.arange(length).astype(np.float32)[:, None] * freq.astype(np.float32)[None, :]
    cosine, sine = np.cos(angle), np.sin(angle)
    return np.concatenate([cosine, cosine, -sine, sine], 1).astype(np.float32)


def turn(head, table):
    half = HEAD_SIZE // 2
    swapped = jnp.concatenate([head[:, half:], head[:, :half]], 1)
    return head * table[:, :HEAD_SIZE] + swapped * table[:, HEAD_SIZE:]


def turn_back(head, table):
    half = HEAD_SIZE // 2
    swapped = jnp.concatenate([head[:, half:], head[:, :half]], 1)
    return head * table[:, :HEAD_SIZE] - swapped * table[:, HEAD_SIZE:]


def head_cols(index):
    return slice(index * HEAD_SIZE, (index + 1) * HEAD_SIZE)


def attend_kernel(
    x_ref, n_ref, w_ref, kt_ref, qp_ref, kp_ref, mix_ref, log_ref, qr_ref, kr_ref, v_ref, hidden_ref, normed_ref
):
    rows, width = x_ref.shape
    kv_cols, q_cols = kr_ref.shape[1], qr_ref.shape[1]
    used = 2 * kv_cols + q_cols
    first = used + -used % 128
    masked = jnp.where(kp_ref[...] <= qp_ref[...], 0.0, -1e30)
    masked = jnp.concatenate([masked] * GROUP, 0)
    keys_values = dot(n_ref[...], w_ref[:, : 2 * kv_cols])
    queries = dot(n_ref[:rows, :], w_ref[:, 2 * kv_cols : used])
    v_ref[...] = keys_values[:, kv_cols:].astype(jnp.bfloat16)
    for g in range(KEY_VALUE_HEADS):
        key = turn(keys_values[:, head_cols(g)], kt_ref[...]).astype(jnp.bfloat16)
        kr_ref[:, head_cols(g)] = key
        value = v_ref[:, head_cols(g)]
        heads = []
        for i in range(GROUP):
            cols = head_cols(g * GROUP + i)
            head = turn(queries[:, cols], kt_ref[:rows, :]).astype(jnp.bfloat16) * SCALE
            qr_ref[:, cols] = head
            heads.append(head)
        query = jnp.concatenate(heads, 0)
        scores = dot_rows(query, key) + masked
        peak = jnp.max(scores, axis=-1, keepdims=True)
        expd = jnp.exp(scores - peak)
        total = jnp.sum(expd, axis=-1, keepdims=True)
        mixed = (dot(expd.astype(jnp.bfloat16), value) / total).astype(jnp.bfloat16)
        for i in range(GROUP):
            mix_ref[:, head_cols(g * GROUP + i)] = mixed[i * rows : (i + 1) * rows]
        log_ref[:, g : g + 1] = peak + jnp.log(total)
    hidden = x_ref[...].astype(jnp.float32) + dot_rows(mix_ref[...], w_ref[:, first : first + q_cols])
    hidden_ref[...] = hidden
    normed_ref[...] = (hidden * rms_scale(hidden)).astype(jnp.bfloat16)


def attend(tokens, normed, weights, key_table, query_pos, key_pos, kv_cols, q_cols):
    (rows, width), keys = tokens.shape, normed.shape[0]
    bf16, f32 = jnp.bfloat16, jnp.float32
    return pl.pallas_call(
        attend_kernel,
        out_shape=(
            jax.ShapeDtypeStruct((rows, q_cols), bf16),
            jax.ShapeDtypeStruct((GROUP * rows, 8), f32),
            jax.ShapeDtypeStruct((rows, q_cols), bf16),
            jax.ShapeDtypeStruct((keys, kv_cols), bf16),
            jax.ShapeDtypeStruct((keys, kv_cols), bf16),
            jax.ShapeDtypeStruct((rows, width), f32),
            jax.ShapeDtypeStruct((rows, width), bf16),
        ),
        compiler_params=pltpu.CompilerParams(vmem_limit_bytes=KERNEL_VMEM),
        cost_estimate=pl.CostEstimate(
            flops=4 * rows * keys * QUERY_HEADS * HEAD_SIZE + 4 * keys * width * kv_cols,
            transcendentals=rows * keys * QUERY_HEADS,
            bytes_accessed=10_000_000,
        ),
        name="attend",
    )(tokens, normed, weights, key_table, query_pos, key_pos)


def attend_back_kernel(
    q_ref, k_ref, v_ref, mix_ref, gm_ref, log_ref, qt_ref, kt_ref, qp_ref, kp_ref, grad_ref
):
    hidden = jnp.where(kp_ref[...] <= qp_ref[...], 0.0, -1e30)
    hidden = jnp.concatenate([hidden] * GROUP, 0)
    rows, keys = q_ref.shape[0], k_ref.shape[0]
    kv_cols = 2 * k_ref.shape[1]
    grad_ref[rows:, kv_cols:] = jnp.zeros((keys - rows, grad_ref.shape[1] - kv_cols), jnp.bfloat16)
    used = kv_cols + q_ref.shape[1]
    if used < grad_ref.shape[1]:
        grad_ref[:rows, used:] = jnp.zeros((rows, grad_ref.shape[1] - used), jnp.bfloat16)
    for g in range(KEY_VALUE_HEADS):
        key, value = k_ref[:, head_cols(g)], v_ref[:, head_cols(g)]
        each = [head_cols(g * GROUP + i) for i in range(GROUP)]
        query = jnp.concatenate([q_ref[:, cols] for cols in each], 0)
        mixed = jnp.concatenate([mix_ref[:, cols] for cols in each], 0)
        grad_mix = jnp.concatenate([gm_ref[:, cols] for cols in each], 0)
        scores = dot_rows(query, key) + hidden
        probs = jnp.exp(scores - log_ref[:, g : g + 1])
        grad_probs = dot_rows(grad_mix, value)
        delta = jnp.sum(
            grad_mix.astype(jnp.float32) * mixed.astype(jnp.float32), axis=-1, keepdims=True
        )
        grad_scores = (probs * (grad_probs - delta)).astype(jnp.bfloat16)
        grad_query = dot(grad_scores, key) * SCALE
        grad_key = dot_cols(grad_scores, query)
        grad_value = dot_cols(probs.astype(jnp.bfloat16), grad_mix)
        for i in range(GROUP):
            head = turn_back(grad_query[i * rows : (i + 1) * rows], qt_ref[...])
            grad_ref[:rows, head_cols(2 * KEY_VALUE_HEADS + g * GROUP + i)] = head.astype(jnp.bfloat16)
        grad_ref[:, head_cols(g)] = turn_back(grad_key, kt_ref[...]).astype(jnp.bfloat16)
        grad_ref[:, head_cols(KEY_VALUE_HEADS + g)] = grad_value.astype(jnp.bfloat16)


def attend_back(query, key, value, mix, grad_mix, log_total, query_table, key_table, query_pos, key_pos):
    rows, keys = query.shape[0], key.shape[0]
    used = 2 * key.shape[1] + query.shape[1]
    return pl.pallas_call(
        attend_back_kernel,
        out_shape=jax.ShapeDtypeStruct((keys, used + -used % 128), jnp.bfloat16),
        compiler_params=pltpu.CompilerParams(vmem_limit_bytes=KERNEL_VMEM),
        cost_estimate=pl.CostEstimate(
            flops=10 * rows * keys * QUERY_HEADS * HEAD_SIZE,
            transcendentals=rows * keys * QUERY_HEADS,
            bytes_accessed=6_000_000,
        ),
        name="attend_back",
    )(query, key, value, mix, grad_mix, log_total, query_table, key_table, query_pos, key_pos)


def body(
    tokens,
    attn_gain,
    w_query,
    key_weight,
    value_weight,
    w_output,
    mlp_gain,
    w_gate,
    w_up,
    w_down,
    cotangent,
):
    _, length, width = tokens.shape
    shards, shard = lax.axis_size("shard"), lax.axis_index("shard")
    context, place = lax.axis_index("context"), lax.axis_index("tensor")
    places = lax.axis_size("tensor")
    rows = 2 * length
    upper = place // 2 == 1
    kv_cols, hidden_cols = key_weight.shape[1], w_gate.shape[1]

    starts = [
        (which * places + (place ^ step)) * length
        for which in (context, 1 - context)
        for step in (0, 2, 1, 3)
    ]
    table = jnp.asarray(rope_tables(length * places * lax.axis_size("context")))
    key_table = jnp.concatenate([lax.dynamic_slice_in_dim(table, at, length, 0) for at in starts], 0)
    key_pos = jnp.concatenate([at + jnp.arange(length, dtype=jnp.int32) for at in starts])
    query_table, query_pos = key_table[:rows], key_pos[:rows, None]
    key_pos = key_pos[None, :]

    mine, other = jnp.where(upper, tokens[1], tokens[0]), jnp.where(upper, tokens[0], tokens[1])
    moved = swap(other, "tensor", 2)
    own = jnp.concatenate([to_relative(mine, shards, shard), to_relative(moved, shards, shard)], 0)
    beside = swap(own, "tensor", 1)
    across = swap(own, "context", 1)
    across_beside = swap(after(beside, across), "context", 1)
    all_tokens = jnp.concatenate([own, beside, across, across_beside], 0)

    def gained(weights, gain):
        joined = jnp.concatenate(weights, 1)
        return (joined.astype(jnp.float32) * gain[:, None]).astype(jnp.bfloat16)

    k_early, v_early, q_early, o_early, _ = lax.optimization_barrier(
        (key_weight, value_weight, w_query, w_output, other)
    )
    attn_local = jnp.concatenate([k_early, v_early, q_early], 1)
    attn_cols = attn_local.shape[1]
    gap = -attn_cols % 128
    gaps = jnp.zeros((attn_local.shape[0], gap), jnp.bfloat16)
    first_local = jnp.concatenate([gained([attn_local], attn_gain), gaps, o_early.T], 1)
    first_pieces = gather_pieces(first_local, None)
    ends = (2 * kv_cols, attn_cols, attn_cols + gap)
    first_weight = lax.optimization_barrier(jnp.concatenate(first_pieces, 0))
    mlp_local = jnp.concatenate([gained([w_gate, w_up], mlp_gain), w_down.T], 1)

    cots = [after(to_relative(cotangent, shards, shard), beside)]
    cots.append(shift(cots[0], 1))
    cots = [after(cots[0], cots[1]), cots[1], shift(cots[1], 1)]
    cots.append(shift(cots[0], -1))
    all_tokens = after(all_tokens, cots[1])

    all_float = all_tokens.astype(jnp.float32)
    all_scale = rms_scale(all_float)
    all_normed = (all_float * all_scale).astype(jnp.bfloat16)
    tokens_f, scale_a = all_float[:rows], all_scale[:rows]
    mix, log_total, query_rot, key_rot, value, hidden, normed_m = attend(
        own, all_normed, first_weight, key_table, query_pos, key_pos, kv_cols, w_query.shape[1]
    )
    w_kv, w_q, out_weight = first_weight[:, : ends[0]], first_weight[:, ends[0] : ends[1]], first_weight[:, ends[2] :]
    mlp_pieces = gather_pieces(mlp_local, first_weight, mix)
    w_in = jnp.concatenate([piece[:, : 2 * hidden_cols] for piece in mlp_pieces], 0)
    w_dn = jnp.concatenate([piece[:, 2 * hidden_cols :] for piece in mlp_pieces], 0)
    scale_m = rms_scale(hidden)
    normed_m, cots[2], cots[3] = lax.optimization_barrier((normed_m, cots[2], cots[3]))

    def cot_of(k):
        above = ((place - k) % places) // 2 == 1
        pair = (cots[k], cots[(k + 2) % places])
        return jnp.concatenate([jnp.where(above, one[1], one[0]) for one in pair], 0)

    cots = [cot_of(k) for k in range(places)]
    own_cot = cots[0]
    barrier = lax.optimization_barrier

    group, acts, grads_in, backs = [normed_m], [], [], []
    arriving = shift(normed_m, 1)
    for k, cot in enumerate(cots):
        if k > 0:
            group.append(arriving if k < 3 else after(arriving, grad_nm))
            if k + 1 < places:
                arriving = shift(arriving if k == 1 else after(arriving, backs[-1]), 1)
        rows_in = group[k]
        grad_act = dot(cot, w_dn)
        inner = dot(rows_in, w_in)
        gate, up_vals = inner[:, :hidden_cols], inner[:, hidden_cols:]
        sigma = jax.nn.sigmoid(gate)
        acts.append((gate * sigma * up_vals).astype(jnp.bfloat16))
        grad_up = (grad_act * gate * sigma).astype(jnp.bfloat16)
        grad_gate = (grad_act * up_vals * sigma * (1.0 + gate * (1.0 - sigma))).astype(jnp.bfloat16)
        grads_in.append(jnp.concatenate([grad_gate, grad_up], 1))
        backs.append(dot_rows(grads_in[-1], w_in).astype(jnp.bfloat16))
        if k > 0:
            grad_nm = backs[k] if k == 1 else backs[k] + shift(grad_nm, 1)
    bits = bits_of(shards)
    *held, _ = barrier((*grads_in, *acts, grad_nm))
    group, cot_group = jnp.concatenate(group, 0), jnp.concatenate(cots, 0)
    grad_in, act = jnp.concatenate(held[:places], 0), jnp.concatenate(held[places:], 0)
    mlp_term = jnp.concatenate(
        [dot_cols(group, grad_in).astype(jnp.bfloat16), dot_cols(cot_group, act).astype(jnp.bfloat16)], 1
    )
    mlp_beside = swap(mlp_term[mlp_term.shape[0] // 2 :], "shard", 1)
    half_cols = mlp_term.shape[1] // 2
    later = context == 1

    grad_nm = (backs[0] + shift(grad_nm, 1)).astype(jnp.float32)
    grad_hidden = own_cot.astype(jnp.float32) + norm_back(grad_nm, hidden, scale_m)
    gain_m_term = jnp.sum(grad_nm * (hidden * scale_m), axis=0)
    grad_hidden_low = grad_hidden.astype(jnp.bfloat16)
    grad_mix = dot(grad_hidden_low, out_weight).astype(jnp.bfloat16)
    out_term = scatter_rows(dot_cols(grad_hidden_low, mix).astype(jnp.bfloat16), 0, 1)
    forward = [dot_rows(act, w_dn).astype(jnp.bfloat16) for act in acts]
    total = shift(after(forward[1], grad_mix), 1)
    grads = attend_back(
        query_rot, key_rot, value, mix, grad_mix, log_total, query_table, key_table, query_pos, key_pos
    )
    grads, out_term, total, mlp_beside = barrier((grads, out_term, total, mlp_beside))

    spot = (jnp.arange(grads.shape[1]) == attn_cols).astype(jnp.float32)
    attn_term = dot_cols(all_normed, grads) + gain_m_term[:, None] * spot[None, :]
    attn_term = scatter_rows(attn_term.astype(jnp.bfloat16), 0, 1)
    attn_core = attn_term
    out_term = scatter_rows(out_term, 1, bits, attn_core)
    attn_term = scatter_rows(attn_term, 1, bits)
    grad_query, grad_kv = grads[:rows, 2 * kv_cols : attn_cols], grads[:, : 2 * kv_cols]
    pair = after(grad_kv[: 2 * rows], attn_core) + swap(grad_kv[2 * rows :], "context", 1)
    own_kv = pair[:rows] + swap(pair[rows:], "tensor", 1)
    out_part = group_part(group_halves(out_term, context))

    mlp_term = after(mlp_term[: mlp_beside.shape[0]], attn_core) + mlp_beside
    first, second = mlp_term[:, :half_cols], mlp_term[:, half_cols:]
    mlp_kept, mlp_sent = jnp.where(later, second, first), jnp.where(later, first, second)
    owned = mlp_sent.shape[0] // 2
    mlp_moved = swap(mlp_sent[owned:], "context", 1)
    total = shift(forward[2] + total, 1)
    total = shift(after(forward[3], attn_core) + total, 1)
    attn_term, own_kv, out_part, total, mlp_kept = barrier((attn_term, own_kv, out_part, total, mlp_kept))

    attn_half = group_halves(attn_term, context)
    mlp_owned = swap(after(mlp_sent[:owned], attn_half), "context", 1)
    mlp_half = swap(mlp_kept[owned:] + mlp_moved, "shard", 2) + mlp_kept[:owned] + mlp_owned
    mlp_half = scatter_rows(mlp_half, 2, bits)
    attn_part = group_part(attn_half)
    own_kv, grad_query, mlp_half = barrier((own_kv, grad_query, mlp_half))
    block = hidden + forward[0].astype(jnp.float32) + total.astype(jnp.float32)
    block = from_relative(block.astype(jnp.bfloat16), shards, shard)
    grad_na = dot_rows(grad_query, w_q) + dot_rows(own_kv, w_kv)
    grad_tokens = grad_hidden + norm_back(grad_na, tokens_f, scale_a)
    grad_tokens = from_relative(grad_tokens.astype(jnp.bfloat16), shards, shard)
    attn_part, mlp_half, grad_tokens = barrier((attn_part, mlp_half, grad_tokens))

    fill = jnp.zeros((out_part.shape[0], -out_part.shape[1] % 128), jnp.bfloat16)
    parts = group_collect(jnp.concatenate([attn_part, out_part, fill], 1))
    parts_across = swap(parts, "context", 1)
    parts = jnp.concatenate(
        [jnp.where(later, parts_across, parts), jnp.where(later, parts, parts_across)], 0
    )
    mlp_other = swap(mlp_half, "context", 1)
    mlp_total = jnp.concatenate(
        [jnp.where(later, mlp_other, mlp_half), jnp.where(later, mlp_half, mlp_other)], 1
    ).astype(jnp.float32)
    gate_total = mlp_total[:, :hidden_cols] * mlp_gain[:, None]
    up_total = mlp_total[:, hidden_cols : 2 * hidden_cols] * mlp_gain[:, None]
    down_total = mlp_total[:, 2 * hidden_cols :].T
    tokens_back = swap(grad_tokens[length:], "tensor", 2)
    block_back = swap(block[length:], "tensor", 2)
    gate_total, block, grad_tokens = barrier((gate_total, block[:length], grad_tokens[:length]))
    block_out = both_sequences(block, block_back, upper)
    tokens_grad = both_sequences(grad_tokens, tokens_back, upper)
    query_total, key_total, value_total, out_total = unpack(
        parts, attn_gain[:, None], kv_cols, attn_cols, out_part.shape[1]
    )
    heads = parts[: attn_local.shape[0], : attn_cols + 1].astype(jnp.float32)
    gain_m_total = heads[:, attn_cols] / mlp_gain
    gain_a_total = jnp.sum(attn_local.astype(jnp.float32) * heads[:, :attn_cols], axis=1)
    return (
        block_out,
        tokens_grad,
        gain_a_total,
        query_total,
        key_total.T,
        value_total.T,
        out_total,
        gain_m_total,
        gate_total,
        up_total,
        down_total,
    )


def solution(mesh):
    specs = (
        P("shard", ("context", "tensor"), None),
        P("shard"),
        P("shard", None),
        P("shard", None),
        P("shard", None),
        P(None, "shard"),
        P("shard"),
        P("shard", "tensor"),
        P("shard", "tensor"),
        P("tensor", "shard"),
    )
    return jax.shard_map(
        body,
        mesh=mesh,
        in_specs=specs + specs[:1],
        out_specs=specs[:1] + specs,
        check_vma=False,
    )
```

```python
import functools

import jax
import jax.numpy as jnp
import numpy as np
from jax import lax
from jax.experimental import pallas as pl
from jax.experimental.pallas import tpu as pltpu
from jax.sharding import PartitionSpec as P

QUERY_HEADS = 15
KEY_VALUE_HEADS = 5
HEAD_SIZE = 64
GROUP = QUERY_HEADS // KEY_VALUE_HEADS
SCALE = HEAD_SIZE ** (-0.5)
EPS = 1e-05
KERNEL_VMEM = 40 * 1024 * 1024


def dot(left, right):
    return jnp.dot(left, right, preferred_element_type=jnp.float32)


def dot_rows(left, right):
    return lax.dot_general(
        left, right, (((1,), (1,)), ((), ())), preferred_element_type=jnp.float32
    )


def dot_cols(left, right):
    return lax.dot_general(
        left, right, (((0,), (0,)), ((), ())), preferred_element_type=jnp.float32
    )


def rms_scale(rows):
    return lax.rsqrt(jnp.mean(rows * rows, axis=-1, keepdims=True) + EPS)


def norm_back(scaled, rows, scale_rows):
    normed = rows * scale_rows
    return scale_rows * (scaled - normed * jnp.mean(scaled * normed, axis=-1, keepdims=True))


def after(value, *others):
    return lax.optimization_barrier((value, *others))[0]


def bits_of(count):
    return count.bit_length() - 1


def flip_blocks(rows, shards, index):
    width = rows.shape[-1] // shards
    bits = bits_of(shards)
    for place in range(bits):
        step = width << place
        pieces = [rows[..., i * step : (i + 1) * step] for i in range(rows.shape[-1] // step)]
        swapped = jnp.concatenate([pieces[i ^ 1] for i in range(len(pieces))], -1)
        rows = jnp.where((index >> (bits - 1 - place)) & 1 == 1, swapped, rows)
    return rows


def reverse_blocks(rows, shards):
    width = rows.shape[-1] // shards
    bits = bits_of(shards)
    order = [int(format(i, f"0{bits}b")[::-1], 2) for i in range(shards)]
    return jnp.concatenate([rows[..., i * width : (i + 1) * width] for i in order], -1)


def to_relative(rows, shards, index):
    return flip_blocks(reverse_blocks(rows, shards), shards, index)


def from_relative(rows, shards, index):
    return reverse_blocks(flip_blocks(rows, shards, index), shards)


def swap(value, axis, bit):
    size = lax.axis_size(axis)
    return lax.ppermute(value, axis, [(i, i ^ bit) for i in range(size)])


def gather_pieces(rows, gate, later=None):
    pieces = [rows]
    for place in reversed(range(bits_of(lax.axis_size("shard")))):
        if len(pieces) > 2:
            pieces = [jnp.concatenate(pieces, 0)]
        sent = pieces
        if gate is not None:
            sent = [after(rows, gate)]
            gate = None
        elif later is not None:
            sent = pieces[:1] + [after(piece, later) for piece in pieces[1:]]
        pieces = pieces + [swap(piece, "shard", 1 << place) for piece in sent]
    return pieces


def scatter_rows(rows, first, last, gate=None):
    for place in range(first, last):
        half = rows.shape[0] // 2
        kept = rows[:half] if gate is None else after(rows[:half], gate)
        rows = kept + swap(rows[half:], "shard", 1 << place)
    return rows


def shift(value, count):
    size = lax.axis_size("tensor")
    return lax.ppermute(value, "tensor", [(i, (i + count) % size) for i in range(size)])


def both_sequences(mine, other, upper):
    return jnp.stack([jnp.where(upper, other, mine), jnp.where(upper, mine, other)])


def chunk_rows(count, group):
    chunk = -(-count // group)
    return chunk if chunk <= 16 else -(-chunk // 16) * 16


def group_halves(rows, context):
    chunk = chunk_rows(rows.shape[0], 2 * lax.axis_size("tensor"))
    half = chunk * lax.axis_size("tensor")
    padded = jnp.pad(rows, ((0, 2 * half - rows.shape[0]), (0, 0)))
    kept = lax.dynamic_slice_in_dim(padded, context * half, half, 0)
    sent = lax.dynamic_slice_in_dim(padded, (1 - context) * half, half, 0)
    return kept + swap(sent, "context", 1)


def group_part(half):
    places = lax.axis_size("tensor")
    parts = lax.all_to_all(half, "tensor", split_axis=0, concat_axis=0, tiled=True)
    parts = parts.reshape(places, half.shape[0] // places, half.shape[1]).astype(jnp.float32)
    return jnp.sum(parts, axis=0).astype(jnp.bfloat16)


def group_collect(part):
    places = lax.axis_size("tensor")
    spread = jnp.broadcast_to(part[None], (places,) + part.shape)
    spread = spread.reshape(places * part.shape[0], part.shape[1])
    return lax.all_to_all(spread, "tensor", split_axis=0, concat_axis=0, tiled=True)


def unpack_kernel(kv_cols, attn_cols, parts_ref, gain_ref, query_ref, key_ref, value_ref, out_ref):
    rows = query_ref.shape[0]
    gain = gain_ref[...]
    query_ref[...] = parts_ref[:rows, 2 * kv_cols : attn_cols].astype(jnp.float32) * gain
    key_ref[...] = (parts_ref[:rows, :kv_cols].astype(jnp.float32) * gain).T
    value_ref[...] = (parts_ref[:rows, kv_cols : 2 * kv_cols].astype(jnp.float32) * gain).T
    first = attn_cols + -attn_cols % 128
    out_ref[...] = parts_ref[:rows, first : first + out_ref.shape[0]].astype(jnp.float32).T


def unpack(parts, gain, kv_cols, attn_cols, out_cols):
    rows = gain.shape[0]
    shapes = ((rows, attn_cols - 2 * kv_cols), (kv_cols, rows), (kv_cols, rows), (out_cols, rows))
    return pl.pallas_call(
        functools.partial(unpack_kernel, kv_cols, attn_cols),
        out_shape=tuple(jax.ShapeDtypeStruct(shape, jnp.float32) for shape in shapes),
        compiler_params=pltpu.CompilerParams(vmem_limit_bytes=KERNEL_VMEM),
        cost_estimate=pl.CostEstimate(flops=0, transcendentals=0, bytes_accessed=4_000_000),
        name="unpack",
    )(parts, gain)


def rope_tables(length):
    half = HEAD_SIZE // 2
    freq = np.float32(10000.0) ** (-np.arange(half).astype(np.float32) * 2.0 / HEAD_SIZE)
    angle = np.arange(length).astype(np.float32)[:, None] * freq.astype(np.float32)[None, :]
    cosine, sine = np.cos(angle), np.sin(angle)
    return np.concatenate([cosine, cosine, -sine, sine], 1).astype(np.float32)


def turn(head, table):
    half = HEAD_SIZE // 2
    swapped = jnp.concatenate([head[:, half:], head[:, :half]], 1)
    return head * table[:, :HEAD_SIZE] + swapped * table[:, HEAD_SIZE:]


def turn_back(head, table):
    half = HEAD_SIZE // 2
    swapped = jnp.concatenate([head[:, half:], head[:, :half]], 1)
    return head * table[:, :HEAD_SIZE] - swapped * table[:, HEAD_SIZE:]


def head_cols(index):
    return slice(index * HEAD_SIZE, (index + 1) * HEAD_SIZE)


def attend_kernel(
    x_ref, n_ref, w_ref, kt_ref, qp_ref, kp_ref, mix_ref, log_ref, qr_ref, kr_ref, v_ref, hidden_ref, normed_ref
):
    rows, width = x_ref.shape
    kv_cols, q_cols = kr_ref.shape[1], qr_ref.shape[1]
    used = 2 * kv_cols + q_cols
    first = used + -used % 128
    masked = jnp.where(kp_ref[...] <= qp_ref[...], 0.0, -1e30)
    masked = jnp.concatenate([masked] * GROUP, 0)
    keys_values = dot(n_ref[...], w_ref[:, : 2 * kv_cols])
    queries = dot(n_ref[:rows, :], w_ref[:, 2 * kv_cols : used])
    v_ref[...] = keys_values[:, kv_cols:].astype(jnp.bfloat16)
    for g in range(KEY_VALUE_HEADS):
        key = turn(keys_values[:, head_cols(g)], kt_ref[...]).astype(jnp.bfloat16)
        kr_ref[:, head_cols(g)] = key
        value = v_ref[:, head_cols(g)]
        heads = []
        for i in range(GROUP):
            cols = head_cols(g * GROUP + i)
            head = turn(queries[:, cols], kt_ref[:rows, :]).astype(jnp.bfloat16) * SCALE
            qr_ref[:, cols] = head
            heads.append(head)
        query = jnp.concatenate(heads, 0)
        scores = dot_rows(query, key) + masked
        peak = jnp.max(scores, axis=-1, keepdims=True)
        expd = jnp.exp(scores - peak)
        total = jnp.sum(expd, axis=-1, keepdims=True)
        mixed = (dot(expd.astype(jnp.bfloat16), value) / total).astype(jnp.bfloat16)
        for i in range(GROUP):
            mix_ref[:, head_cols(g * GROUP + i)] = mixed[i * rows : (i + 1) * rows]
        log_ref[:, g : g + 1] = peak + jnp.log(total)
    hidden = x_ref[...].astype(jnp.float32) + dot_rows(mix_ref[...], w_ref[:, first : first + q_cols])
    hidden_ref[...] = hidden
    normed_ref[...] = (hidden * rms_scale(hidden)).astype(jnp.bfloat16)


def attend(tokens, normed, weights, key_table, query_pos, key_pos, kv_cols, q_cols):
    (rows, width), keys = tokens.shape, normed.shape[0]
    bf16, f32 = jnp.bfloat16, jnp.float32
    return pl.pallas_call(
        attend_kernel,
        out_shape=(
            jax.ShapeDtypeStruct((rows, q_cols), bf16),
            jax.ShapeDtypeStruct((GROUP * rows, 8), f32),
            jax.ShapeDtypeStruct((rows, q_cols), bf16),
            jax.ShapeDtypeStruct((keys, kv_cols), bf16),
            jax.ShapeDtypeStruct((keys, kv_cols), bf16),
            jax.ShapeDtypeStruct((rows, width), f32),
            jax.ShapeDtypeStruct((rows, width), bf16),
        ),
        compiler_params=pltpu.CompilerParams(vmem_limit_bytes=KERNEL_VMEM),
        cost_estimate=pl.CostEstimate(
            flops=4 * rows * keys * QUERY_HEADS * HEAD_SIZE + 4 * keys * width * kv_cols,
            transcendentals=rows * keys * QUERY_HEADS,
            bytes_accessed=10_000_000,
        ),
        name="attend",
    )(tokens, normed, weights, key_table, query_pos, key_pos)


def attend_back_kernel(
    q_ref, k_ref, v_ref, mix_ref, gm_ref, log_ref, qt_ref, kt_ref, qp_ref, kp_ref, grad_ref
):
    hidden = jnp.where(kp_ref[...] <= qp_ref[...], 0.0, -1e30)
    hidden = jnp.concatenate([hidden] * GROUP, 0)
    rows, keys = q_ref.shape[0], k_ref.shape[0]
    kv_cols = 2 * k_ref.shape[1]
    grad_ref[rows:, kv_cols:] = jnp.zeros((keys - rows, grad_ref.shape[1] - kv_cols), jnp.bfloat16)
    used = kv_cols + q_ref.shape[1]
    if used < grad_ref.shape[1]:
        grad_ref[:rows, used:] = jnp.zeros((rows, grad_ref.shape[1] - used), jnp.bfloat16)
    for g in range(KEY_VALUE_HEADS):
        key, value = k_ref[:, head_cols(g)], v_ref[:, head_cols(g)]
        each = [head_cols(g * GROUP + i) for i in range(GROUP)]
        query = jnp.concatenate([q_ref[:, cols] for cols in each], 0)
        mixed = jnp.concatenate([mix_ref[:, cols] for cols in each], 0)
        grad_mix = jnp.concatenate([gm_ref[:, cols] for cols in each], 0)
        scores = dot_rows(query, key) + hidden
        probs = jnp.exp(scores - log_ref[:, g : g + 1])
        grad_probs = dot_rows(grad_mix, value)
        delta = jnp.sum(
            grad_mix.astype(jnp.float32) * mixed.astype(jnp.float32), axis=-1, keepdims=True
        )
        grad_scores = (probs * (grad_probs - delta)).astype(jnp.bfloat16)
        grad_query = dot(grad_scores, key) * SCALE
        grad_key = dot_cols(grad_scores, query)
        grad_value = dot_cols(probs.astype(jnp.bfloat16), grad_mix)
        for i in range(GROUP):
            head = turn_back(grad_query[i * rows : (i + 1) * rows], qt_ref[...])
            grad_ref[:rows, head_cols(2 * KEY_VALUE_HEADS + g * GROUP + i)] = head.astype(jnp.bfloat16)
        grad_ref[:, head_cols(g)] = turn_back(grad_key, kt_ref[...]).astype(jnp.bfloat16)
        grad_ref[:, head_cols(KEY_VALUE_HEADS + g)] = grad_value.astype(jnp.bfloat16)


def attend_back(query, key, value, mix, grad_mix, log_total, query_table, key_table, query_pos, key_pos):
    rows, keys = query.shape[0], key.shape[0]
    used = 2 * key.shape[1] + query.shape[1]
    return pl.pallas_call(
        attend_back_kernel,
        out_shape=jax.ShapeDtypeStruct((keys, used + -used % 128), jnp.bfloat16),
        compiler_params=pltpu.CompilerParams(vmem_limit_bytes=KERNEL_VMEM),
        cost_estimate=pl.CostEstimate(
            flops=10 * rows * keys * QUERY_HEADS * HEAD_SIZE,
            transcendentals=rows * keys * QUERY_HEADS,
            bytes_accessed=6_000_000,
        ),
        name="attend_back",
    )(query, key, value, mix, grad_mix, log_total, query_table, key_table, query_pos, key_pos)


def body(
    tokens,
    attn_gain,
    w_query,
    key_weight,
    value_weight,
    w_output,
    mlp_gain,
    w_gate,
    w_up,
    w_down,
    cotangent,
):
    _, length, width = tokens.shape
    shards, shard = lax.axis_size("shard"), lax.axis_index("shard")
    context, place = lax.axis_index("context"), lax.axis_index("tensor")
    places = lax.axis_size("tensor")
    rows = 2 * length
    upper = place // 2 == 1
    kv_cols, hidden_cols = key_weight.shape[1], w_gate.shape[1]

    starts = [
        (which * places + (place ^ step)) * length
        for which in (context, 1 - context)
        for step in (0, 2, 1, 3)
    ]
    table = jnp.asarray(rope_tables(length * places * lax.axis_size("context")))
    key_table = jnp.concatenate([lax.dynamic_slice_in_dim(table, at, length, 0) for at in starts], 0)
    key_pos = jnp.concatenate([at + jnp.arange(length, dtype=jnp.int32) for at in starts])
    query_table, query_pos = key_table[:rows], key_pos[:rows, None]
    key_pos = key_pos[None, :]

    mine, other = jnp.where(upper, tokens[1], tokens[0]), jnp.where(upper, tokens[0], tokens[1])
    moved = swap(other, "tensor", 2)
    own = jnp.concatenate([to_relative(mine, shards, shard), to_relative(moved, shards, shard)], 0)
    beside = swap(own, "tensor", 1)
    across = swap(own, "context", 1)
    across_beside = swap(after(beside, across), "context", 1)
    all_tokens = jnp.concatenate([own, beside, across, across_beside], 0)

    def gained(weights, gain):
        joined = jnp.concatenate(weights, 1)
        return (joined.astype(jnp.float32) * gain[:, None]).astype(jnp.bfloat16)

    k_early, v_early, q_early, o_early, _ = lax.optimization_barrier(
        (key_weight, value_weight, w_query, w_output, other)
    )
    attn_local = jnp.concatenate([k_early, v_early, q_early], 1)
    attn_cols = attn_local.shape[1]
    gap = -attn_cols % 128
    gaps = jnp.zeros((attn_local.shape[0], gap), jnp.bfloat16)
    first_local = jnp.concatenate([gained([attn_local], attn_gain), gaps, o_early.T], 1)
    first_pieces = gather_pieces(first_local, None)
    ends = (2 * kv_cols, attn_cols, attn_cols + gap)
    first_weight = lax.optimization_barrier(jnp.concatenate(first_pieces, 0))
    mlp_local = jnp.concatenate([gained([w_gate, w_up], mlp_gain), w_down.T], 1)

    cots = [after(to_relative(cotangent, shards, shard), beside)]
    cots.append(shift(cots[0], 1))
    cots = [after(cots[0], cots[1]), cots[1], shift(cots[1], 1)]
    cots.append(shift(cots[0], -1))
    all_tokens = after(all_tokens, cots[1])

    all_float = all_tokens.astype(jnp.float32)
    all_scale = rms_scale(all_float)
    all_normed = (all_float * all_scale).astype(jnp.bfloat16)
    tokens_f, scale_a = all_float[:rows], all_scale[:rows]
    mix, log_total, query_rot, key_rot, value, hidden, normed_m = attend(
        own, all_normed, first_weight, key_table, query_pos, key_pos, kv_cols, w_query.shape[1]
    )
    w_kv, w_q, out_weight = first_weight[:, : ends[0]], first_weight[:, ends[0] : ends[1]], first_weight[:, ends[2] :]
    mlp_pieces = gather_pieces(mlp_local, first_weight, mix)
    w_in = jnp.concatenate([piece[:, : 2 * hidden_cols] for piece in mlp_pieces], 0)
    w_dn = jnp.concatenate([piece[:, 2 * hidden_cols :] for piece in mlp_pieces], 0)
    scale_m = rms_scale(hidden)
    normed_m, cots[2], cots[3] = lax.optimization_barrier((normed_m, cots[2], cots[3]))

    def cot_of(k):
        above = ((place - k) % places) // 2 == 1
        pair = (cots[k], cots[(k + 2) % places])
        return jnp.concatenate([jnp.where(above, one[1], one[0]) for one in pair], 0)

    cots = [cot_of(k) for k in range(places)]
    own_cot = cots[0]
    barrier = lax.optimization_barrier

    group, acts, grads_in, backs = [normed_m], [], [], []
    arriving = shift(normed_m, 1)
    for k, cot in enumerate(cots):
        if k > 0:
            group.append(arriving if k < 3 else after(arriving, grad_nm))
            if k + 1 < places:
                arriving = shift(arriving if k == 1 else after(arriving, backs[-1]), 1)
        rows_in = group[k]
        grad_act = dot(cot, w_dn)
        inner = dot(rows_in, w_in)
        gate, up_vals = inner[:, :hidden_cols], inner[:, hidden_cols:]
        sigma = jax.nn.sigmoid(gate)
        acts.append((gate * sigma * up_vals).astype(jnp.bfloat16))
        grad_up = (grad_act * gate * sigma).astype(jnp.bfloat16)
        grad_gate = (grad_act * up_vals * sigma * (1.0 + gate * (1.0 - sigma))).astype(jnp.bfloat16)
        grads_in.append(jnp.concatenate([grad_gate, grad_up], 1))
        backs.append(dot_rows(grads_in[-1], w_in).astype(jnp.bfloat16))
        if k > 0:
            grad_nm = backs[k] if k == 1 else backs[k] + shift(grad_nm, 1)
    bits = bits_of(shards)
    *held, _ = barrier((*grads_in, *acts, grad_nm))
    group, cot_group = jnp.concatenate(group, 0), jnp.concatenate(cots, 0)
    grad_in, act = jnp.concatenate(held[:places], 0), jnp.concatenate(held[places:], 0)
    mlp_term = jnp.concatenate(
        [dot_cols(group, grad_in).astype(jnp.bfloat16), dot_cols(cot_group, act).astype(jnp.bfloat16)], 1
    )
    mlp_beside = swap(mlp_term[mlp_term.shape[0] // 2 :], "shard", 1)
    half_cols = mlp_term.shape[1] // 2
    later = context == 1

    grad_nm = (backs[0] + shift(grad_nm, 1)).astype(jnp.float32)
    grad_hidden = own_cot.astype(jnp.float32) + norm_back(grad_nm, hidden, scale_m)
    gain_m_term = jnp.sum(grad_nm * (hidden * scale_m), axis=0)
    grad_hidden_low = grad_hidden.astype(jnp.bfloat16)
    grad_mix = dot(grad_hidden_low, out_weight).astype(jnp.bfloat16)
    out_term = scatter_rows(dot_cols(grad_hidden_low, mix).astype(jnp.bfloat16), 0, bits)
    forward = [dot_rows(act, w_dn).astype(jnp.bfloat16) for act in acts]
    total = shift(after(forward[1], grad_mix), 1)
    grads = attend_back(
        query_rot, key_rot, value, mix, grad_mix, log_total, query_table, key_table, query_pos, key_pos
    )
    grads, out_term, total, mlp_beside = barrier((grads, out_term, total, mlp_beside))

    spot = (jnp.arange(grads.shape[1]) == attn_cols).astype(jnp.float32)
    attn_term = dot_cols(all_normed, grads) + gain_m_term[:, None] * spot[None, :]
    attn_term = scatter_rows(attn_term.astype(jnp.bfloat16), 0, 1)
    attn_core = attn_term
    attn_term = scatter_rows(attn_term, 1, bits)
    grad_query, grad_kv = grads[:rows, 2 * kv_cols : attn_cols], grads[:, : 2 * kv_cols]
    pair = after(grad_kv[: 2 * rows], attn_core) + swap(grad_kv[2 * rows :], "context", 1)
    own_kv = pair[:rows] + swap(pair[rows:], "tensor", 1)
    out_part = group_part(group_halves(after(out_term, attn_core), context))

    mlp_term = after(mlp_term[: mlp_beside.shape[0]], attn_core) + mlp_beside
    first, second = mlp_term[:, :half_cols], mlp_term[:, half_cols:]
    mlp_kept, mlp_sent = jnp.where(later, second, first), jnp.where(later, first, second)
    owned = mlp_sent.shape[0] // 2
    mlp_moved = swap(mlp_sent[owned:], "context", 1)
    total = shift(forward[2] + total, 1)
    total = shift(after(forward[3], attn_core) + total, 1)
    attn_term, own_kv, out_part, total, mlp_kept = barrier((attn_term, own_kv, out_part, total, mlp_kept))

    attn_half = group_halves(attn_term, context)
    mlp_owned = swap(after(mlp_sent[:owned], attn_half), "context", 1)
    mlp_half = swap(mlp_kept[owned:] + mlp_moved, "shard", 2) + mlp_kept[:owned] + mlp_owned
    mlp_half = scatter_rows(mlp_half, 2, bits)
    attn_part = group_part(attn_half)
    own_kv, grad_query, mlp_half = barrier((own_kv, grad_query, mlp_half))
    block = hidden + forward[0].astype(jnp.float32) + total.astype(jnp.float32)
    block = from_relative(block.astype(jnp.bfloat16), shards, shard)
    grad_na = dot_rows(grad_query, w_q) + dot_rows(own_kv, w_kv)
    grad_tokens = grad_hidden + norm_back(grad_na, tokens_f, scale_a)
    grad_tokens = from_relative(grad_tokens.astype(jnp.bfloat16), shards, shard)
    attn_part, mlp_half, grad_tokens = barrier((attn_part, mlp_half, grad_tokens))

    fill = jnp.zeros((out_part.shape[0], -out_part.shape[1] % 128), jnp.bfloat16)
    parts = group_collect(jnp.concatenate([attn_part, out_part, fill], 1))
    parts_across = swap(parts, "context", 1)
    parts = jnp.concatenate(
        [jnp.where(later, parts_across, parts), jnp.where(later, parts, parts_across)], 0
    )
    mlp_other = swap(mlp_half, "context", 1)
    mlp_total = jnp.concatenate(
        [jnp.where(later, mlp_other, mlp_half), jnp.where(later, mlp_half, mlp_other)], 1
    ).astype(jnp.float32)
    gate_total = mlp_total[:, :hidden_cols] * mlp_gain[:, None]
    up_total = mlp_total[:, hidden_cols : 2 * hidden_cols] * mlp_gain[:, None]
    down_total = mlp_total[:, 2 * hidden_cols :].T
    tokens_back = swap(grad_tokens[length:], "tensor", 2)
    block_back = swap(block[length:], "tensor", 2)
    gate_total, block, grad_tokens = barrier((gate_total, block[:length], grad_tokens[:length]))
    block_out = both_sequences(block, block_back, upper)
    tokens_grad = both_sequences(grad_tokens, tokens_back, upper)
    query_total, key_total, value_total, out_total = unpack(
        parts, attn_gain[:, None], kv_cols, attn_cols, out_part.shape[1]
    )
    heads = parts[: attn_local.shape[0], : attn_cols + 1].astype(jnp.float32)
    gain_m_total = heads[:, attn_cols] / mlp_gain
    gain_a_total = jnp.sum(attn_local.astype(jnp.float32) * heads[:, :attn_cols], axis=1)
    return (
        block_out,
        tokens_grad,
        gain_a_total,
        query_total,
        key_total.T,
        value_total.T,
        out_total,
        gain_m_total,
        gate_total,
        up_total,
        down_total,
    )


def solution(mesh):
    specs = (
        P("shard", ("context", "tensor"), None),
        P("shard"),
        P("shard", None),
        P("shard", None),
        P("shard", None),
        P(None, "shard"),
        P("shard"),
        P("shard", "tensor"),
        P("shard", "tensor"),
        P("tensor", "shard"),
    )
    return jax.shard_map(
        body,
        mesh=mesh,
        in_specs=specs + specs[:1],
        out_specs=specs[:1] + specs,
        check_vma=False,
    )
```

```python
import functools

import jax
import jax.numpy as jnp
import numpy as np
from jax import lax
from jax.experimental import pallas as pl
from jax.experimental.pallas import tpu as pltpu
from jax.sharding import PartitionSpec as P

QUERY_HEADS = 15
KEY_VALUE_HEADS = 5
HEAD_SIZE = 64
GROUP = QUERY_HEADS // KEY_VALUE_HEADS
SCALE = HEAD_SIZE ** (-0.5)
EPS = 1e-05
KERNEL_VMEM = 40 * 1024 * 1024


def dot(left, right):
    return jnp.dot(left, right, preferred_element_type=jnp.float32)


def dot_rows(left, right):
    return lax.dot_general(
        left, right, (((1,), (1,)), ((), ())), preferred_element_type=jnp.float32
    )


def dot_cols(left, right):
    return lax.dot_general(
        left, right, (((0,), (0,)), ((), ())), preferred_element_type=jnp.float32
    )


def rms_scale(rows):
    return lax.rsqrt(jnp.mean(rows * rows, axis=-1, keepdims=True) + EPS)


def norm_back(scaled, rows, scale_rows):
    normed = rows * scale_rows
    return scale_rows * (scaled - normed * jnp.mean(scaled * normed, axis=-1, keepdims=True))


def after(value, *others):
    return lax.optimization_barrier((value, *others))[0]


def bits_of(count):
    return count.bit_length() - 1


def flip_blocks(rows, shards, index):
    width = rows.shape[-1] // shards
    bits = bits_of(shards)
    for place in range(bits):
        step = width << place
        pieces = [rows[..., i * step : (i + 1) * step] for i in range(rows.shape[-1] // step)]
        swapped = jnp.concatenate([pieces[i ^ 1] for i in range(len(pieces))], -1)
        rows = jnp.where((index >> (bits - 1 - place)) & 1 == 1, swapped, rows)
    return rows


def reverse_blocks(rows, shards):
    width = rows.shape[-1] // shards
    bits = bits_of(shards)
    order = [int(format(i, f"0{bits}b")[::-1], 2) for i in range(shards)]
    return jnp.concatenate([rows[..., i * width : (i + 1) * width] for i in order], -1)


def to_relative(rows, shards, index):
    return flip_blocks(reverse_blocks(rows, shards), shards, index)


def from_relative(rows, shards, index):
    return reverse_blocks(flip_blocks(rows, shards, index), shards)


def swap(value, axis, bit):
    size = lax.axis_size(axis)
    return lax.ppermute(value, axis, [(i, i ^ bit) for i in range(size)])


def gather_pieces(rows, gate, later=None):
    pieces = [rows]
    for place in reversed(range(bits_of(lax.axis_size("shard")))):
        if len(pieces) > 2:
            pieces = [jnp.concatenate(pieces, 0)]
        sent = pieces
        if gate is not None:
            sent = [after(rows, gate)]
            gate = None
        elif later is not None:
            sent = pieces[:1] + [after(piece, later) for piece in pieces[1:]]
        pieces = pieces + [swap(piece, "shard", 1 << place) for piece in sent]
    return pieces


def scatter_rows(rows, first, last, gate=None):
    for place in range(first, last):
        half = rows.shape[0] // 2
        kept = rows[:half] if gate is None else after(rows[:half], gate)
        rows = kept + swap(rows[half:], "shard", 1 << place)
    return rows


def shift(value, count):
    size = lax.axis_size("tensor")
    return lax.ppermute(value, "tensor", [(i, (i + count) % size) for i in range(size)])


def both_sequences(mine, other, upper):
    return jnp.stack([jnp.where(upper, other, mine), jnp.where(upper, mine, other)])


def chunk_rows(count, group):
    chunk = -(-count // group)
    return chunk if chunk <= 16 else -(-chunk // 16) * 16


def group_halves(rows, context):
    chunk = chunk_rows(rows.shape[0], 2 * lax.axis_size("tensor"))
    half = chunk * lax.axis_size("tensor")
    padded = jnp.pad(rows, ((0, 2 * half - rows.shape[0]), (0, 0)))
    kept = lax.dynamic_slice_in_dim(padded, context * half, half, 0)
    sent = lax.dynamic_slice_in_dim(padded, (1 - context) * half, half, 0)
    return kept + swap(sent, "context", 1)


def group_part(half):
    places = lax.axis_size("tensor")
    parts = lax.all_to_all(half, "tensor", split_axis=0, concat_axis=0, tiled=True)
    parts = parts.reshape(places, half.shape[0] // places, half.shape[1]).astype(jnp.float32)
    return jnp.sum(parts, axis=0).astype(jnp.bfloat16)


def group_collect(part):
    places = lax.axis_size("tensor")
    spread = jnp.broadcast_to(part[None], (places,) + part.shape)
    spread = spread.reshape(places * part.shape[0], part.shape[1])
    return lax.all_to_all(spread, "tensor", split_axis=0, concat_axis=0, tiled=True)


def unpack_kernel(kv_cols, attn_cols, parts_ref, gain_ref, query_ref, key_ref, value_ref, out_ref):
    rows = query_ref.shape[0]
    gain = gain_ref[...]
    query_ref[...] = parts_ref[:rows, 2 * kv_cols : attn_cols].astype(jnp.float32) * gain
    key_ref[...] = (parts_ref[:rows, :kv_cols].astype(jnp.float32) * gain).T
    value_ref[...] = (parts_ref[:rows, kv_cols : 2 * kv_cols].astype(jnp.float32) * gain).T
    first = attn_cols + -attn_cols % 128
    out_ref[...] = parts_ref[:rows, first : first + out_ref.shape[0]].astype(jnp.float32).T


def unpack(parts, gain, kv_cols, attn_cols, out_cols):
    rows = gain.shape[0]
    shapes = ((rows, attn_cols - 2 * kv_cols), (kv_cols, rows), (kv_cols, rows), (out_cols, rows))
    return pl.pallas_call(
        functools.partial(unpack_kernel, kv_cols, attn_cols),
        out_shape=tuple(jax.ShapeDtypeStruct(shape, jnp.float32) for shape in shapes),
        compiler_params=pltpu.CompilerParams(vmem_limit_bytes=KERNEL_VMEM),
        cost_estimate=pl.CostEstimate(flops=0, transcendentals=0, bytes_accessed=4_000_000),
        name="unpack",
    )(parts, gain)


def rope_tables(length):
    half = HEAD_SIZE // 2
    freq = np.float32(10000.0) ** (-np.arange(half).astype(np.float32) * 2.0 / HEAD_SIZE)
    angle = np.arange(length).astype(np.float32)[:, None] * freq.astype(np.float32)[None, :]
    cosine, sine = np.cos(angle), np.sin(angle)
    return np.concatenate([cosine, cosine, -sine, sine], 1).astype(np.float32)


def turn(head, table):
    half = HEAD_SIZE // 2
    swapped = jnp.concatenate([head[:, half:], head[:, :half]], 1)
    return head * table[:, :HEAD_SIZE] + swapped * table[:, HEAD_SIZE:]


def turn_back(head, table):
    half = HEAD_SIZE // 2
    swapped = jnp.concatenate([head[:, half:], head[:, :half]], 1)
    return head * table[:, :HEAD_SIZE] - swapped * table[:, HEAD_SIZE:]


def head_cols(index):
    return slice(index * HEAD_SIZE, (index + 1) * HEAD_SIZE)


def attend_kernel(
    x_ref, n_ref, w_ref, kt_ref, qp_ref, kp_ref, mix_ref, log_ref, qr_ref, kr_ref, v_ref, hidden_ref, normed_ref
):
    rows, width = x_ref.shape
    kv_cols, q_cols = kr_ref.shape[1], qr_ref.shape[1]
    used = 2 * kv_cols + q_cols
    first = used + -used % 128
    masked = jnp.where(kp_ref[...] <= qp_ref[...], 0.0, -1e30)
    masked = jnp.concatenate([masked] * GROUP, 0)
    keys_values = dot(n_ref[...], w_ref[:, : 2 * kv_cols])
    queries = dot(n_ref[:rows, :], w_ref[:, 2 * kv_cols : used])
    v_ref[...] = keys_values[:, kv_cols:].astype(jnp.bfloat16)
    for g in range(KEY_VALUE_HEADS):
        key = turn(keys_values[:, head_cols(g)], kt_ref[...]).astype(jnp.bfloat16)
        kr_ref[:, head_cols(g)] = key
        value = v_ref[:, head_cols(g)]
        heads = []
        for i in range(GROUP):
            cols = head_cols(g * GROUP + i)
            head = turn(queries[:, cols], kt_ref[:rows, :]).astype(jnp.bfloat16) * SCALE
            qr_ref[:, cols] = head
            heads.append(head)
        query = jnp.concatenate(heads, 0)
        scores = dot_rows(query, key) + masked
        peak = jnp.max(scores, axis=-1, keepdims=True)
        expd = jnp.exp(scores - peak)
        total = jnp.sum(expd, axis=-1, keepdims=True)
        mixed = (dot(expd.astype(jnp.bfloat16), value) / total).astype(jnp.bfloat16)
        for i in range(GROUP):
            mix_ref[:, head_cols(g * GROUP + i)] = mixed[i * rows : (i + 1) * rows]
        log_ref[:, g : g + 1] = peak + jnp.log(total)
    hidden = x_ref[...].astype(jnp.float32) + dot_rows(mix_ref[...], w_ref[:, first : first + q_cols])
    hidden_ref[...] = hidden
    normed_ref[...] = (hidden * rms_scale(hidden)).astype(jnp.bfloat16)


def attend(tokens, normed, weights, key_table, query_pos, key_pos, kv_cols, q_cols):
    (rows, width), keys = tokens.shape, normed.shape[0]
    bf16, f32 = jnp.bfloat16, jnp.float32
    return pl.pallas_call(
        attend_kernel,
        out_shape=(
            jax.ShapeDtypeStruct((rows, q_cols), bf16),
            jax.ShapeDtypeStruct((GROUP * rows, 8), f32),
            jax.ShapeDtypeStruct((rows, q_cols), bf16),
            jax.ShapeDtypeStruct((keys, kv_cols), bf16),
            jax.ShapeDtypeStruct((keys, kv_cols), bf16),
            jax.ShapeDtypeStruct((rows, width), f32),
            jax.ShapeDtypeStruct((rows, width), bf16),
        ),
        compiler_params=pltpu.CompilerParams(vmem_limit_bytes=KERNEL_VMEM),
        cost_estimate=pl.CostEstimate(
            flops=4 * rows * keys * QUERY_HEADS * HEAD_SIZE + 4 * keys * width * kv_cols,
            transcendentals=rows * keys * QUERY_HEADS,
            bytes_accessed=10_000_000,
        ),
        name="attend",
    )(tokens, normed, weights, key_table, query_pos, key_pos)


def attend_back_kernel(
    q_ref, k_ref, v_ref, mix_ref, gm_ref, log_ref, qt_ref, kt_ref, qp_ref, kp_ref, grad_ref
):
    hidden = jnp.where(kp_ref[...] <= qp_ref[...], 0.0, -1e30)
    hidden = jnp.concatenate([hidden] * GROUP, 0)
    rows, keys = q_ref.shape[0], k_ref.shape[0]
    kv_cols = 2 * k_ref.shape[1]
    grad_ref[rows:, kv_cols:] = jnp.zeros((keys - rows, grad_ref.shape[1] - kv_cols), jnp.bfloat16)
    used = kv_cols + q_ref.shape[1]
    if used < grad_ref.shape[1]:
        grad_ref[:rows, used:] = jnp.zeros((rows, grad_ref.shape[1] - used), jnp.bfloat16)
    for g in range(KEY_VALUE_HEADS):
        key, value = k_ref[:, head_cols(g)], v_ref[:, head_cols(g)]
        each = [head_cols(g * GROUP + i) for i in range(GROUP)]
        query = jnp.concatenate([q_ref[:, cols] for cols in each], 0)
        mixed = jnp.concatenate([mix_ref[:, cols] for cols in each], 0)
        grad_mix = jnp.concatenate([gm_ref[:, cols] for cols in each], 0)
        scores = dot_rows(query, key) + hidden
        probs = jnp.exp(scores - log_ref[:, g : g + 1])
        grad_probs = dot_rows(grad_mix, value)
        delta = jnp.sum(
            grad_mix.astype(jnp.float32) * mixed.astype(jnp.float32), axis=-1, keepdims=True
        )
        grad_scores = (probs * (grad_probs - delta)).astype(jnp.bfloat16)
        grad_query = dot(grad_scores, key) * SCALE
        grad_key = dot_cols(grad_scores, query)
        grad_value = dot_cols(probs.astype(jnp.bfloat16), grad_mix)
        for i in range(GROUP):
            head = turn_back(grad_query[i * rows : (i + 1) * rows], qt_ref[...])
            grad_ref[:rows, head_cols(2 * KEY_VALUE_HEADS + g * GROUP + i)] = head.astype(jnp.bfloat16)
        grad_ref[:, head_cols(g)] = turn_back(grad_key, kt_ref[...]).astype(jnp.bfloat16)
        grad_ref[:, head_cols(KEY_VALUE_HEADS + g)] = grad_value.astype(jnp.bfloat16)


def attend_back(query, key, value, mix, grad_mix, log_total, query_table, key_table, query_pos, key_pos):
    rows, keys = query.shape[0], key.shape[0]
    used = 2 * key.shape[1] + query.shape[1]
    return pl.pallas_call(
        attend_back_kernel,
        out_shape=jax.ShapeDtypeStruct((keys, used + -used % 128), jnp.bfloat16),
        compiler_params=pltpu.CompilerParams(vmem_limit_bytes=KERNEL_VMEM),
        cost_estimate=pl.CostEstimate(
            flops=10 * rows * keys * QUERY_HEADS * HEAD_SIZE,
            transcendentals=rows * keys * QUERY_HEADS,
            bytes_accessed=6_000_000,
        ),
        name="attend_back",
    )(query, key, value, mix, grad_mix, log_total, query_table, key_table, query_pos, key_pos)


def body(
    tokens,
    attn_gain,
    w_query,
    key_weight,
    value_weight,
    w_output,
    mlp_gain,
    w_gate,
    w_up,
    w_down,
    cotangent,
):
    _, length, width = tokens.shape
    shards, shard = lax.axis_size("shard"), lax.axis_index("shard")
    context, place = lax.axis_index("context"), lax.axis_index("tensor")
    places = lax.axis_size("tensor")
    rows = 2 * length
    upper = place // 2 == 1
    kv_cols, hidden_cols = key_weight.shape[1], w_gate.shape[1]

    starts = [
        (which * places + (place ^ step)) * length
        for which in (context, 1 - context)
        for step in (0, 2, 1, 3)
    ]
    table = jnp.asarray(rope_tables(length * places * lax.axis_size("context")))
    key_table = jnp.concatenate([lax.dynamic_slice_in_dim(table, at, length, 0) for at in starts], 0)
    key_pos = jnp.concatenate([at + jnp.arange(length, dtype=jnp.int32) for at in starts])
    query_table, query_pos = key_table[:rows], key_pos[:rows, None]
    key_pos = key_pos[None, :]

    mine, other = jnp.where(upper, tokens[1], tokens[0]), jnp.where(upper, tokens[0], tokens[1])
    moved = swap(other, "tensor", 2)
    own = jnp.concatenate([to_relative(mine, shards, shard), to_relative(moved, shards, shard)], 0)
    beside = swap(own, "tensor", 1)
    across = swap(own, "context", 1)
    across_beside = swap(after(beside, across), "context", 1)
    all_tokens = jnp.concatenate([own, beside, across, across_beside], 0)

    def gained(weights, gain):
        joined = jnp.concatenate(weights, 1)
        return (joined.astype(jnp.float32) * gain[:, None]).astype(jnp.bfloat16)

    k_early, v_early, q_early, o_early, _ = lax.optimization_barrier(
        (key_weight, value_weight, w_query, w_output, other)
    )
    attn_local = jnp.concatenate([k_early, v_early, q_early], 1)
    attn_cols = attn_local.shape[1]
    gap = -attn_cols % 128
    gaps = jnp.zeros((attn_local.shape[0], gap), jnp.bfloat16)
    first_local = jnp.concatenate([gained([attn_local], attn_gain), gaps, o_early.T], 1)
    first_pieces = gather_pieces(first_local, None)
    ends = (2 * kv_cols, attn_cols, attn_cols + gap)
    first_weight = lax.optimization_barrier(jnp.concatenate(first_pieces, 0))
    mlp_local = jnp.concatenate([gained([w_gate, w_up], mlp_gain), w_down.T], 1)

    cots = [after(to_relative(cotangent, shards, shard), beside)]
    cots.append(shift(cots[0], 1))
    cots = [after(cots[0], cots[1]), cots[1], shift(cots[1], 1)]
    cots.append(shift(cots[0], -1))

    all_float = all_tokens.astype(jnp.float32)
    all_scale = rms_scale(all_float)
    all_normed = after((all_float * all_scale).astype(jnp.bfloat16), cots[1])
    tokens_f = own.astype(jnp.float32)
    scale_a = rms_scale(tokens_f)
    mix, log_total, query_rot, key_rot, value, hidden, normed_m = attend(
        own, all_normed, first_weight, key_table, query_pos, key_pos, kv_cols, w_query.shape[1]
    )
    w_kv, w_q, out_weight = first_weight[:, : ends[0]], first_weight[:, ends[0] : ends[1]], first_weight[:, ends[2] :]
    mlp_pieces = gather_pieces(mlp_local, first_weight, mix)
    w_in = jnp.concatenate([piece[:, : 2 * hidden_cols] for piece in mlp_pieces], 0)
    w_dn = jnp.concatenate([piece[:, 2 * hidden_cols :] for piece in mlp_pieces], 0)
    scale_m = rms_scale(hidden)
    normed_m, cots[2], cots[3] = lax.optimization_barrier((normed_m, cots[2], cots[3]))

    def cot_of(k):
        above = ((place - k) % places) // 2 == 1
        pair = (cots[k], cots[(k + 2) % places])
        return jnp.concatenate([jnp.where(above, one[1], one[0]) for one in pair], 0)

    cots = [cot_of(k) for k in range(places)]
    own_cot = cots[0]
    barrier = lax.optimization_barrier

    group, acts, grads_in, backs = [normed_m], [], [], []
    arriving = shift(normed_m, 1)
    for k, cot in enumerate(cots):
        if k > 0:
            group.append(arriving if k < 3 else after(arriving, grad_nm))
            if k + 1 < places:
                arriving = shift(arriving if k == 1 else after(arriving, backs[-1]), 1)
        rows_in = group[k]
        grad_act = dot(cot, w_dn)
        inner = dot(rows_in, w_in)
        gate, up_vals = inner[:, :hidden_cols], inner[:, hidden_cols:]
        sigma = jax.nn.sigmoid(gate)
        acts.append((gate * sigma * up_vals).astype(jnp.bfloat16))
        grad_up = (grad_act * gate * sigma).astype(jnp.bfloat16)
        grad_gate = (grad_act * up_vals * sigma * (1.0 + gate * (1.0 - sigma))).astype(jnp.bfloat16)
        grads_in.append(jnp.concatenate([grad_gate, grad_up], 1))
        backs.append(dot_rows(grads_in[-1], w_in).astype(jnp.bfloat16))
        if k > 0:
            grad_nm = backs[k] if k == 1 else backs[k] + shift(grad_nm, 1)
    bits = bits_of(shards)
    *held, _ = barrier((*grads_in, *acts, grad_nm))
    group, cot_group = jnp.concatenate(group, 0), jnp.concatenate(cots, 0)
    grad_in, act = jnp.concatenate(held[:places], 0), jnp.concatenate(held[places:], 0)
    mlp_term = jnp.concatenate(
        [dot_cols(group, grad_in).astype(jnp.bfloat16), dot_cols(cot_group, act).astype(jnp.bfloat16)], 1
    )
    mlp_beside = swap(mlp_term[mlp_term.shape[0] // 2 :], "shard", 1)
    half_cols = mlp_term.shape[1] // 2
    later = context == 1

    grad_nm = (backs[0] + shift(grad_nm, 1)).astype(jnp.float32)
    grad_hidden = own_cot.astype(jnp.float32) + norm_back(grad_nm, hidden, scale_m)
    gain_m_term = jnp.sum(grad_nm * (hidden * scale_m), axis=0)
    grad_hidden_low = grad_hidden.astype(jnp.bfloat16)
    grad_mix = dot(grad_hidden_low, out_weight).astype(jnp.bfloat16)
    out_term = scatter_rows(dot_cols(grad_hidden_low, mix).astype(jnp.bfloat16), 0, 1)
    forward = [dot_rows(act, w_dn).astype(jnp.bfloat16) for act in acts]
    total = shift(after(forward[1], grad_mix), 1)
    grads = attend_back(
        query_rot, key_rot, value, mix, grad_mix, log_total, query_table, key_table, query_pos, key_pos
    )
    grads, out_term, total, mlp_beside = barrier((grads, out_term, total, mlp_beside))

    spot = (jnp.arange(grads.shape[1]) == attn_cols).astype(jnp.float32)
    attn_term = dot_cols(all_normed, grads) + gain_m_term[:, None] * spot[None, :]
    attn_term = scatter_rows(attn_term.astype(jnp.bfloat16), 0, 1)
    attn_core = attn_term
    out_term = scatter_rows(out_term, 1, bits, attn_core)
    attn_term = scatter_rows(attn_term, 1, bits)
    grad_query, grad_kv = grads[:rows, 2 * kv_cols : attn_cols], grads[:, : 2 * kv_cols]
    pair = after(grad_kv[: 2 * rows], attn_core) + swap(grad_kv[2 * rows :], "context", 1)
    own_kv = pair[:rows] + swap(pair[rows:], "tensor", 1)
    out_part = group_part(group_halves(out_term, context))

    mlp_term = after(mlp_term[: mlp_beside.shape[0]], attn_core) + mlp_beside
    first, second = mlp_term[:, :half_cols], mlp_term[:, half_cols:]
    mlp_kept, mlp_sent = jnp.where(later, second, first), jnp.where(later, first, second)
    owned = mlp_sent.shape[0] // 2
    mlp_moved = swap(mlp_sent[owned:], "context", 1)
    total = shift(forward[2] + total, 1)
    total = shift(after(forward[3], attn_core) + total, 1)
    attn_term, own_kv, out_part, total, mlp_kept = barrier((attn_term, own_kv, out_part, total, mlp_kept))

    attn_half = group_halves(attn_term, context)
    mlp_owned = swap(after(mlp_sent[:owned], attn_half), "context", 1)
    mlp_half = swap(mlp_kept[owned:] + mlp_moved, "shard", 2) + mlp_kept[:owned] + mlp_owned
    mlp_half = scatter_rows(mlp_half, 2, bits)
    attn_part = group_part(attn_half)
    own_kv, grad_query, mlp_half = barrier((own_kv, grad_query, mlp_half))
    block = hidden + forward[0].astype(jnp.float32) + total.astype(jnp.float32)
    block = from_relative(block.astype(jnp.bfloat16), shards, shard)
    grad_na = dot_rows(grad_query, w_q) + dot_rows(own_kv, w_kv)
    grad_tokens = grad_hidden + norm_back(grad_na, tokens_f, scale_a)
    grad_tokens = from_relative(grad_tokens.astype(jnp.bfloat16), shards, shard)
    attn_part, mlp_half, grad_tokens = barrier((attn_part, mlp_half, grad_tokens))

    fill = jnp.zeros((out_part.shape[0], -out_part.shape[1] % 128), jnp.bfloat16)
    parts = group_collect(jnp.concatenate([attn_part, out_part, fill], 1))
    parts_across = swap(parts, "context", 1)
    parts = jnp.concatenate(
        [jnp.where(later, parts_across, parts), jnp.where(later, parts, parts_across)], 0
    )
    mlp_other = swap(mlp_half, "context", 1)
    mlp_total = jnp.concatenate(
        [jnp.where(later, mlp_other, mlp_half), jnp.where(later, mlp_half, mlp_other)], 1
    ).astype(jnp.float32)
    gate_total = mlp_total[:, :hidden_cols] * mlp_gain[:, None]
    up_total = mlp_total[:, hidden_cols : 2 * hidden_cols] * mlp_gain[:, None]
    down_total = mlp_total[:, 2 * hidden_cols :].T
    tokens_back = swap(grad_tokens[length:], "tensor", 2)
    block_back = swap(block[length:], "tensor", 2)
    gate_total, block, grad_tokens = barrier((gate_total, block[:length], grad_tokens[:length]))
    block_out = both_sequences(block, block_back, upper)
    tokens_grad = both_sequences(grad_tokens, tokens_back, upper)
    query_total, key_total, value_total, out_total = unpack(
        parts, attn_gain[:, None], kv_cols, attn_cols, out_part.shape[1]
    )
    heads = parts[: attn_local.shape[0], : attn_cols + 1].astype(jnp.float32)
    gain_m_total = heads[:, attn_cols] / mlp_gain
    gain_a_total = jnp.sum(attn_local.astype(jnp.float32) * heads[:, :attn_cols], axis=1)
    return (
        block_out,
        tokens_grad,
        gain_a_total,
        query_total,
        key_total.T,
        value_total.T,
        out_total,
        gain_m_total,
        gate_total,
        up_total,
        down_total,
    )


def solution(mesh):
    specs = (
        P("shard", ("context", "tensor"), None),
        P("shard"),
        P("shard", None),
        P("shard", None),
        P("shard", None),
        P(None, "shard"),
        P("shard"),
        P("shard", "tensor"),
        P("shard", "tensor"),
        P("tensor", "shard"),
    )
    return jax.shard_map(
        body,
        mesh=mesh,
        in_specs=specs + specs[:1],
        out_specs=specs[:1] + specs,
        check_vma=False,
    )
```

```python
import functools

import jax
import jax.numpy as jnp
import numpy as np
from jax import lax
from jax.experimental import pallas as pl
from jax.experimental.pallas import tpu as pltpu
from jax.sharding import PartitionSpec as P

QUERY_HEADS = 15
KEY_VALUE_HEADS = 5
HEAD_SIZE = 64
GROUP = QUERY_HEADS // KEY_VALUE_HEADS
SCALE = HEAD_SIZE ** (-0.5)
EPS = 1e-05
KERNEL_VMEM = 40 * 1024 * 1024


def dot(left, right):
    return jnp.dot(left, right, preferred_element_type=jnp.float32)


def dot_rows(left, right):
    return lax.dot_general(
        left, right, (((1,), (1,)), ((), ())), preferred_element_type=jnp.float32
    )


def dot_cols(left, right):
    return lax.dot_general(
        left, right, (((0,), (0,)), ((), ())), preferred_element_type=jnp.float32
    )


def rms_scale(rows):
    return lax.rsqrt(jnp.mean(rows * rows, axis=-1, keepdims=True) + EPS)


def norm_back(scaled, rows, scale_rows):
    normed = rows * scale_rows
    return scale_rows * (scaled - normed * jnp.mean(scaled * normed, axis=-1, keepdims=True))


def after(value, *others):
    return lax.optimization_barrier((value, *others))[0]


def bits_of(count):
    return count.bit_length() - 1


def flip_blocks(rows, shards, index):
    width = rows.shape[-1] // shards
    bits = bits_of(shards)
    for place in range(bits):
        step = width << place
        pieces = [rows[..., i * step : (i + 1) * step] for i in range(rows.shape[-1] // step)]
        swapped = jnp.concatenate([pieces[i ^ 1] for i in range(len(pieces))], -1)
        rows = jnp.where((index >> (bits - 1 - place)) & 1 == 1, swapped, rows)
    return rows


def reverse_blocks(rows, shards):
    width = rows.shape[-1] // shards
    bits = bits_of(shards)
    order = [int(format(i, f"0{bits}b")[::-1], 2) for i in range(shards)]
    return jnp.concatenate([rows[..., i * width : (i + 1) * width] for i in order], -1)


def to_relative(rows, shards, index):
    return flip_blocks(reverse_blocks(rows, shards), shards, index)


def from_relative(rows, shards, index):
    return reverse_blocks(flip_blocks(rows, shards, index), shards)


def swap(value, axis, bit):
    size = lax.axis_size(axis)
    return lax.ppermute(value, axis, [(i, i ^ bit) for i in range(size)])


def gather_pieces(rows, gate, later=None):
    pieces = [rows]
    for place in reversed(range(bits_of(lax.axis_size("shard")))):
        if len(pieces) > 2:
            pieces = [jnp.concatenate(pieces, 0)]
        sent = pieces
        if gate is not None:
            sent = [after(rows, gate)]
            gate = None
        elif later is not None:
            sent = pieces[:1] + [after(piece, later) for piece in pieces[1:]]
        pieces = pieces + [swap(piece, "shard", 1 << place) for piece in sent]
    return pieces


def scatter_rows(rows, first, last, gate=None):
    for place in range(first, last):
        half = rows.shape[0] // 2
        kept = rows[:half] if gate is None else after(rows[:half], gate)
        rows = kept + swap(rows[half:], "shard", 1 << place)
    return rows


def shift(value, count):
    size = lax.axis_size("tensor")
    return lax.ppermute(value, "tensor", [(i, (i + count) % size) for i in range(size)])


def both_sequences(mine, other, upper):
    return jnp.stack([jnp.where(upper, other, mine), jnp.where(upper, mine, other)])


def chunk_rows(count, group):
    chunk = -(-count // group)
    return chunk if chunk <= 16 else -(-chunk // 16) * 16


def group_halves(rows, context):
    chunk = chunk_rows(rows.shape[0], 2 * lax.axis_size("tensor"))
    half = chunk * lax.axis_size("tensor")
    padded = jnp.pad(rows, ((0, 2 * half - rows.shape[0]), (0, 0)))
    kept = lax.dynamic_slice_in_dim(padded, context * half, half, 0)
    sent = lax.dynamic_slice_in_dim(padded, (1 - context) * half, half, 0)
    return kept + swap(sent, "context", 1)


def group_part(half):
    places = lax.axis_size("tensor")
    parts = lax.all_to_all(half, "tensor", split_axis=0, concat_axis=0, tiled=True)
    parts = parts.reshape(places, half.shape[0] // places, half.shape[1]).astype(jnp.float32)
    return jnp.sum(parts, axis=0).astype(jnp.bfloat16)


def group_collect(part):
    places = lax.axis_size("tensor")
    spread = jnp.broadcast_to(part[None], (places,) + part.shape)
    spread = spread.reshape(places * part.shape[0], part.shape[1])
    return lax.all_to_all(spread, "tensor", split_axis=0, concat_axis=0, tiled=True)


def unpack_kernel(kv_cols, attn_cols, parts_ref, gain_ref, query_ref, key_ref, value_ref, out_ref):
    rows = query_ref.shape[0]
    gain = gain_ref[...]
    query_ref[...] = parts_ref[:rows, 2 * kv_cols : attn_cols].astype(jnp.float32) * gain
    key_ref[...] = (parts_ref[:rows, :kv_cols].astype(jnp.float32) * gain).T
    value_ref[...] = (parts_ref[:rows, kv_cols : 2 * kv_cols].astype(jnp.float32) * gain).T
    first = attn_cols + -attn_cols % 128
    out_ref[...] = parts_ref[:rows, first : first + out_ref.shape[0]].astype(jnp.float32).T


def unpack(parts, gain, kv_cols, attn_cols, out_cols):
    rows = gain.shape[0]
    shapes = ((rows, attn_cols - 2 * kv_cols), (kv_cols, rows), (kv_cols, rows), (out_cols, rows))
    return pl.pallas_call(
        functools.partial(unpack_kernel, kv_cols, attn_cols),
        out_shape=tuple(jax.ShapeDtypeStruct(shape, jnp.float32) for shape in shapes),
        compiler_params=pltpu.CompilerParams(vmem_limit_bytes=KERNEL_VMEM),
        cost_estimate=pl.CostEstimate(flops=0, transcendentals=0, bytes_accessed=4_000_000),
        name="unpack",
    )(parts, gain)


def rope_tables(length):
    half = HEAD_SIZE // 2
    freq = np.float32(10000.0) ** (-np.arange(half).astype(np.float32) * 2.0 / HEAD_SIZE)
    angle = np.arange(length).astype(np.float32)[:, None] * freq.astype(np.float32)[None, :]
    cosine, sine = np.cos(angle), np.sin(angle)
    return np.concatenate([cosine, cosine, -sine, sine], 1).astype(np.float32)


def turn(head, table):
    half = HEAD_SIZE // 2
    swapped = jnp.concatenate([head[:, half:], head[:, :half]], 1)
    return head * table[:, :HEAD_SIZE] + swapped * table[:, HEAD_SIZE:]


def turn_back(head, table):
    half = HEAD_SIZE // 2
    swapped = jnp.concatenate([head[:, half:], head[:, :half]], 1)
    return head * table[:, :HEAD_SIZE] - swapped * table[:, HEAD_SIZE:]


def head_cols(index):
    return slice(index * HEAD_SIZE, (index + 1) * HEAD_SIZE)


def attend_kernel(
    x_ref, n_ref, w_ref, kt_ref, qp_ref, kp_ref, mix_ref, log_ref, qr_ref, kr_ref, v_ref, hidden_ref, normed_ref
):
    rows, width = x_ref.shape
    kv_cols, q_cols = kr_ref.shape[1], qr_ref.shape[1]
    used = 2 * kv_cols + q_cols
    first = used + -used % 128
    masked = jnp.where(kp_ref[...] <= qp_ref[...], 0.0, -1e30)
    masked = jnp.concatenate([masked] * GROUP, 0)
    keys_values = dot(n_ref[...], w_ref[:, : 2 * kv_cols])
    queries = dot(n_ref[:rows, :], w_ref[:, 2 * kv_cols : used])
    v_ref[...] = keys_values[:, kv_cols:].astype(jnp.bfloat16)
    for g in range(KEY_VALUE_HEADS):
        key = turn(keys_values[:, head_cols(g)], kt_ref[...]).astype(jnp.bfloat16)
        kr_ref[:, head_cols(g)] = key
        value = v_ref[:, head_cols(g)]
        heads = []
        for i in range(GROUP):
            cols = head_cols(g * GROUP + i)
            head = turn(queries[:, cols], kt_ref[:rows, :]).astype(jnp.bfloat16) * SCALE
            qr_ref[:, cols] = head
            heads.append(head)
        query = jnp.concatenate(heads, 0)
        scores = dot_rows(query, key) + masked
        peak = jnp.max(scores, axis=-1, keepdims=True)
        expd = jnp.exp(scores - peak)
        total = jnp.sum(expd, axis=-1, keepdims=True)
        mixed = (dot(expd.astype(jnp.bfloat16), value) / total).astype(jnp.bfloat16)
        for i in range(GROUP):
            mix_ref[:, head_cols(g * GROUP + i)] = mixed[i * rows : (i + 1) * rows]
        log_ref[:, g : g + 1] = peak + jnp.log(total)
    hidden = x_ref[...].astype(jnp.float32) + dot_rows(mix_ref[...], w_ref[:, first : first + q_cols])
    hidden_ref[...] = hidden
    normed_ref[...] = (hidden * rms_scale(hidden)).astype(jnp.bfloat16)


def attend(tokens, normed, weights, key_table, query_pos, key_pos, kv_cols, q_cols):
    (rows, width), keys = tokens.shape, normed.shape[0]
    bf16, f32 = jnp.bfloat16, jnp.float32
    return pl.pallas_call(
        attend_kernel,
        out_shape=(
            jax.ShapeDtypeStruct((rows, q_cols), bf16),
            jax.ShapeDtypeStruct((GROUP * rows, 8), f32),
            jax.ShapeDtypeStruct((rows, q_cols), bf16),
            jax.ShapeDtypeStruct((keys, kv_cols), bf16),
            jax.ShapeDtypeStruct((keys, kv_cols), bf16),
            jax.ShapeDtypeStruct((rows, width), f32),
            jax.ShapeDtypeStruct((rows, width), bf16),
        ),
        compiler_params=pltpu.CompilerParams(vmem_limit_bytes=KERNEL_VMEM),
        cost_estimate=pl.CostEstimate(
            flops=4 * rows * keys * QUERY_HEADS * HEAD_SIZE + 4 * keys * width * kv_cols,
            transcendentals=rows * keys * QUERY_HEADS,
            bytes_accessed=10_000_000,
        ),
        name="attend",
    )(tokens, normed, weights, key_table, query_pos, key_pos)


def attend_back_kernel(
    q_ref, k_ref, v_ref, mix_ref, gm_ref, log_ref, qt_ref, kt_ref, qp_ref, kp_ref, grad_ref
):
    hidden = jnp.where(kp_ref[...] <= qp_ref[...], 0.0, -1e30)
    hidden = jnp.concatenate([hidden] * GROUP, 0)
    rows, keys = q_ref.shape[0], k_ref.shape[0]
    kv_cols = 2 * k_ref.shape[1]
    grad_ref[rows:, kv_cols:] = jnp.zeros((keys - rows, grad_ref.shape[1] - kv_cols), jnp.bfloat16)
    used = kv_cols + q_ref.shape[1]
    if used < grad_ref.shape[1]:
        grad_ref[:rows, used:] = jnp.zeros((rows, grad_ref.shape[1] - used), jnp.bfloat16)
    for g in range(KEY_VALUE_HEADS):
        key, value = k_ref[:, head_cols(g)], v_ref[:, head_cols(g)]
        each = [head_cols(g * GROUP + i) for i in range(GROUP)]
        query = jnp.concatenate([q_ref[:, cols] for cols in each], 0)
        mixed = jnp.concatenate([mix_ref[:, cols] for cols in each], 0)
        grad_mix = jnp.concatenate([gm_ref[:, cols] for cols in each], 0)
        scores = dot_rows(query, key) + hidden
        probs = jnp.exp(scores - log_ref[:, g : g + 1])
        grad_probs = dot_rows(grad_mix, value)
        delta = jnp.sum(
            grad_mix.astype(jnp.float32) * mixed.astype(jnp.float32), axis=-1, keepdims=True
        )
        grad_scores = (probs * (grad_probs - delta)).astype(jnp.bfloat16)
        grad_query = dot(grad_scores, key) * SCALE
        grad_key = dot_cols(grad_scores, query)
        grad_value = dot_cols(probs.astype(jnp.bfloat16), grad_mix)
        for i in range(GROUP):
            head = turn_back(grad_query[i * rows : (i + 1) * rows], qt_ref[...])
            grad_ref[:rows, head_cols(2 * KEY_VALUE_HEADS + g * GROUP + i)] = head.astype(jnp.bfloat16)
        grad_ref[:, head_cols(g)] = turn_back(grad_key, kt_ref[...]).astype(jnp.bfloat16)
        grad_ref[:, head_cols(KEY_VALUE_HEADS + g)] = grad_value.astype(jnp.bfloat16)


def attend_back(query, key, value, mix, grad_mix, log_total, query_table, key_table, query_pos, key_pos):
    rows, keys = query.shape[0], key.shape[0]
    used = 2 * key.shape[1] + query.shape[1]
    return pl.pallas_call(
        attend_back_kernel,
        out_shape=jax.ShapeDtypeStruct((keys, used + -used % 128), jnp.bfloat16),
        compiler_params=pltpu.CompilerParams(vmem_limit_bytes=KERNEL_VMEM),
        cost_estimate=pl.CostEstimate(
            flops=10 * rows * keys * QUERY_HEADS * HEAD_SIZE,
            transcendentals=rows * keys * QUERY_HEADS,
            bytes_accessed=6_000_000,
        ),
        name="attend_back",
    )(query, key, value, mix, grad_mix, log_total, query_table, key_table, query_pos, key_pos)


def body(
    tokens,
    attn_gain,
    w_query,
    key_weight,
    value_weight,
    w_output,
    mlp_gain,
    w_gate,
    w_up,
    w_down,
    cotangent,
):
    _, length, width = tokens.shape
    shards, shard = lax.axis_size("shard"), lax.axis_index("shard")
    context, place = lax.axis_index("context"), lax.axis_index("tensor")
    places = lax.axis_size("tensor")
    rows = 2 * length
    upper = place // 2 == 1
    kv_cols, hidden_cols = key_weight.shape[1], w_gate.shape[1]

    starts = [
        (which * places + (place ^ step)) * length
        for which in (context, 1 - context)
        for step in (0, 2, 1, 3)
    ]
    table = jnp.asarray(rope_tables(length * places * lax.axis_size("context")))
    key_table = jnp.concatenate([lax.dynamic_slice_in_dim(table, at, length, 0) for at in starts], 0)
    key_pos = jnp.concatenate([at + jnp.arange(length, dtype=jnp.int32) for at in starts])
    query_table, query_pos = key_table[:rows], key_pos[:rows, None]
    key_pos = key_pos[None, :]

    mine, other = jnp.where(upper, tokens[1], tokens[0]), jnp.where(upper, tokens[0], tokens[1])
    moved = swap(other, "tensor", 2)
    own = jnp.concatenate([to_relative(mine, shards, shard), to_relative(moved, shards, shard)], 0)
    beside = swap(own, "tensor", 1)
    across = swap(own, "context", 1)
    across_beside = swap(after(beside, across), "context", 1)
    all_tokens = jnp.concatenate([own, beside, across, across_beside], 0)

    def gained(weights, gain):
        joined = jnp.concatenate(weights, 1)
        return (joined.astype(jnp.float32) * gain[:, None]).astype(jnp.bfloat16)

    k_early, v_early, q_early, o_early, _ = lax.optimization_barrier(
        (key_weight, value_weight, w_query, w_output, other)
    )
    attn_local = jnp.concatenate([k_early, v_early, q_early], 1)
    attn_cols = attn_local.shape[1]
    gap = -attn_cols % 128
    gaps = jnp.zeros((attn_local.shape[0], gap), jnp.bfloat16)
    first_local = jnp.concatenate([gained([attn_local], attn_gain), gaps, o_early.T], 1)
    first_pieces = gather_pieces(first_local, None)
    ends = (2 * kv_cols, attn_cols, attn_cols + gap)
    first_weight = lax.optimization_barrier(jnp.concatenate(first_pieces, 0))
    mlp_local = jnp.concatenate([gained([w_gate, w_up], mlp_gain), w_down.T], 1)

    cots = [after(to_relative(cotangent, shards, shard), beside)]
    cots.append(shift(cots[0], 1))
    cots = [after(cots[0], cots[1]), cots[1], shift(cots[1], 1)]
    cots.append(shift(cots[0], -1))

    all_float = all_tokens.astype(jnp.float32)
    all_scale = rms_scale(all_float)
    all_normed = after((all_float * all_scale).astype(jnp.bfloat16), cots[1])
    tokens_f = own.astype(jnp.float32)
    scale_a = rms_scale(tokens_f)
    mix, log_total, query_rot, key_rot, value, hidden, normed_m = attend(
        own, all_normed, first_weight, key_table, query_pos, key_pos, kv_cols, w_query.shape[1]
    )
    w_kv, w_q, out_weight = first_weight[:, : ends[0]], first_weight[:, ends[0] : ends[1]], first_weight[:, ends[2] :]
    mlp_pieces = gather_pieces(mlp_local, first_weight, mix)
    w_in = jnp.concatenate([piece[:, : 2 * hidden_cols] for piece in mlp_pieces], 0)
    w_dn = jnp.concatenate([piece[:, 2 * hidden_cols :] for piece in mlp_pieces], 0)
    scale_m = rms_scale(hidden)
    normed_m, cots[2], cots[3] = lax.optimization_barrier((normed_m, cots[2], cots[3]))

    def cot_of(k):
        above = ((place - k) % places) // 2 == 1
        pair = (cots[k], cots[(k + 2) % places])
        return jnp.concatenate([jnp.where(above, one[1], one[0]) for one in pair], 0)

    cots = [cot_of(k) for k in range(places)]
    own_cot = cots[0]
    barrier = lax.optimization_barrier

    group, acts, grads_in, backs = [normed_m], [], [], []
    arriving = shift(normed_m, 1)
    for k, cot in enumerate(cots):
        if k > 0:
            group.append(arriving if k < 3 else after(arriving, grad_nm))
            if k + 1 < places:
                arriving = shift(arriving if k == 1 else after(arriving, backs[-1]), 1)
        rows_in = group[k]
        grad_act = dot(cot, w_dn)
        inner = dot(rows_in, w_in)
        gate, up_vals = inner[:, :hidden_cols], inner[:, hidden_cols:]
        sigma = jax.nn.sigmoid(gate)
        acts.append((gate * sigma * up_vals).astype(jnp.bfloat16))
        grad_up = (grad_act * gate * sigma).astype(jnp.bfloat16)
        grad_gate = (grad_act * up_vals * sigma * (1.0 + gate * (1.0 - sigma))).astype(jnp.bfloat16)
        grads_in.append(jnp.concatenate([grad_gate, grad_up], 1))
        backs.append(dot_rows(grads_in[-1], w_in).astype(jnp.bfloat16))
        if k > 0:
            grad_nm = backs[k] if k == 1 else backs[k] + shift(grad_nm, 1)
    bits = bits_of(shards)
    *held, _ = barrier((*grads_in, *acts, grad_nm))
    group, cot_group = jnp.concatenate(group, 0), jnp.concatenate(cots, 0)
    grad_in, act = jnp.concatenate(held[:places], 0), jnp.concatenate(held[places:], 0)
    mlp_term = jnp.concatenate(
        [dot_cols(group, grad_in).astype(jnp.bfloat16), dot_cols(cot_group, act).astype(jnp.bfloat16)], 1
    )
    mlp_beside = swap(mlp_term[mlp_term.shape[0] // 2 :], "shard", 1)
    half_cols = mlp_term.shape[1] // 2
    later = context == 1

    grad_nm = (backs[0] + shift(grad_nm, 1)).astype(jnp.float32)
    grad_hidden = own_cot.astype(jnp.float32) + norm_back(grad_nm, hidden, scale_m)
    gain_m_term = jnp.sum(grad_nm * (hidden * scale_m), axis=0)
    grad_hidden_low = grad_hidden.astype(jnp.bfloat16)
    grad_mix = dot(grad_hidden_low, out_weight).astype(jnp.bfloat16)
    out_term = scatter_rows(dot_cols(grad_hidden_low, mix).astype(jnp.bfloat16), 0, 1)
    forward = [dot_rows(act, w_dn).astype(jnp.bfloat16) for act in acts]
    total = shift(after(forward[1], grad_mix), 1)
    grads = attend_back(
        query_rot, key_rot, value, mix, grad_mix, log_total, query_table, key_table, query_pos, key_pos
    )
    grads, out_term, total, mlp_beside = barrier((grads, out_term, total, mlp_beside))

    spot = (jnp.arange(grads.shape[1]) == attn_cols).astype(jnp.float32)
    half = all_normed.shape[1] // 2
    sent, kept = [
        (dot_cols(all_normed[:, part], grads) + gain_m_term[part, None] * spot[None, :]).astype(jnp.bfloat16)
        for part in (slice(half, None), slice(half))
    ]
    arrived = swap(sent, "shard", 1)
    attn_core = kept[half // 2 :] + arrived[half // 2 :]
    out_term = scatter_rows(out_term, 1, bits, attn_core)
    attn_term = kept[: half // 2] + arrived[: half // 2] + swap(attn_core, "shard", 2)
    attn_term = scatter_rows(attn_term, 2, bits)
    grad_query, grad_kv = grads[:rows, 2 * kv_cols : attn_cols], grads[:, : 2 * kv_cols]
    pair = after(grad_kv[: 2 * rows], attn_core) + swap(grad_kv[2 * rows :], "context", 1)
    own_kv = pair[:rows] + swap(pair[rows:], "tensor", 1)
    out_part = group_part(group_halves(out_term, context))

    mlp_term = after(mlp_term[: mlp_beside.shape[0]], attn_core) + mlp_beside
    first, second = mlp_term[:, :half_cols], mlp_term[:, half_cols:]
    mlp_kept, mlp_sent = jnp.where(later, second, first), jnp.where(later, first, second)
    owned = mlp_sent.shape[0] // 2
    mlp_moved = swap(mlp_sent[owned:], "context", 1)
    total = shift(forward[2] + total, 1)
    total = shift(after(forward[3], attn_core) + total, 1)
    attn_term, own_kv, out_part, total, mlp_kept = barrier((attn_term, own_kv, out_part, total, mlp_kept))

    attn_half = group_halves(attn_term, context)
    mlp_owned = swap(after(mlp_sent[:owned], attn_half), "context", 1)
    mlp_half = swap(mlp_kept[owned:] + mlp_moved, "shard", 2) + mlp_kept[:owned] + mlp_owned
    mlp_half = scatter_rows(mlp_half, 2, bits)
    attn_part = group_part(attn_half)
    own_kv, grad_query, mlp_half = barrier((own_kv, grad_query, mlp_half))
    block = hidden + forward[0].astype(jnp.float32) + total.astype(jnp.float32)
    block = from_relative(block.astype(jnp.bfloat16), shards, shard)
    grad_na = dot_rows(grad_query, w_q) + dot_rows(own_kv, w_kv)
    grad_tokens = grad_hidden + norm_back(grad_na, tokens_f, scale_a)
    grad_tokens = from_relative(grad_tokens.astype(jnp.bfloat16), shards, shard)
    attn_part, mlp_half, grad_tokens = barrier((attn_part, mlp_half, grad_tokens))

    fill = jnp.zeros((out_part.shape[0], -out_part.shape[1] % 128), jnp.bfloat16)
    parts = group_collect(jnp.concatenate([attn_part, out_part, fill], 1))
    parts_across = swap(parts, "context", 1)
    parts = jnp.concatenate(
        [jnp.where(later, parts_across, parts), jnp.where(later, parts, parts_across)], 0
    )
    mlp_other = swap(mlp_half, "context", 1)
    mlp_total = jnp.concatenate(
        [jnp.where(later, mlp_other, mlp_half), jnp.where(later, mlp_half, mlp_other)], 1
    ).astype(jnp.float32)
    gate_total = mlp_total[:, :hidden_cols] * mlp_gain[:, None]
    up_total = mlp_total[:, hidden_cols : 2 * hidden_cols] * mlp_gain[:, None]
    down_total = mlp_total[:, 2 * hidden_cols :].T
    tokens_back = swap(grad_tokens[length:], "tensor", 2)
    block_back = swap(block[length:], "tensor", 2)
    gate_total, block, grad_tokens = barrier((gate_total, block[:length], grad_tokens[:length]))
    block_out = both_sequences(block, block_back, upper)
    tokens_grad = both_sequences(grad_tokens, tokens_back, upper)
    query_total, key_total, value_total, out_total = unpack(
        parts, attn_gain[:, None], kv_cols, attn_cols, out_part.shape[1]
    )
    heads = parts[: attn_local.shape[0], : attn_cols + 1].astype(jnp.float32)
    gain_m_total = heads[:, attn_cols] / mlp_gain
    gain_a_total = jnp.sum(attn_local.astype(jnp.float32) * heads[:, :attn_cols], axis=1)
    return (
        block_out,
        tokens_grad,
        gain_a_total,
        query_total,
        key_total.T,
        value_total.T,
        out_total,
        gain_m_total,
        gate_total,
        up_total,
        down_total,
    )


def solution(mesh):
    specs = (
        P("shard", ("context", "tensor"), None),
        P("shard"),
        P("shard", None),
        P("shard", None),
        P("shard", None),
        P(None, "shard"),
        P("shard"),
        P("shard", "tensor"),
        P("shard", "tensor"),
        P("tensor", "shard"),
    )
    return jax.shard_map(
        body,
        mesh=mesh,
        in_specs=specs + specs[:1],
        out_specs=specs[:1] + specs,
        check_vma=False,
    )
```
